32 devices in a mesh: groups: 2 (over y), seq: 2 (over core), mp: 8 (over z, x).
Axes of the slice: x: 2, y: 2, z: 4, core: 2. Of those that a mesh axis runs over, the one named last changes fastest.
Arguments:
- residual: bfloat16 [1024, 5376], P(('groups', 'seq', 'mp')), parts along dimension 0, may hold values from -6 to 6
- positions: int32 [1024], P(('groups', 'seq')), parts along dimension 0, may hold values from 0 to 383, as said below
- window_start: int32 [1024], P(('groups', 'seq')), parts along dimension 0, may hold values from 0 to 448, as said below
- input_gain: float32 [5376], replicated, may hold values from 0.1 to 1.9
- attention_gain: float32 [5376], replicated, may hold values from 0.1 to 1.9
- feedforward_gain: float32 [5376], replicated, may hold values from 0.1 to 1.9
- output_gain: float32 [5376], replicated, may hold values from 0.1 to 1.9
- query_weight: bfloat16 [5376, 4096], P(None, 'mp'), may hold values from -0.078125 to 0.078125
- key_weight: bfloat16 [5376, 2048], P(None, 'mp'), may hold values from -0.078125 to 0.078125
- value_weight: bfloat16 [5376, 2048], P(None, 'mp'), may hold values from -0.078125 to 0.078125
- output_weight: bfloat16 [4096, 5376], P('mp'), may hold values from -0.09375 to 0.09375
- gate_weight: bfloat16 [5376, 21504], P(None, 'mp'), may hold values from -0.078125 to 0.078125
- up_weight: bfloat16 [5376, 21504], P(None, 'mp'), may hold values from -0.078125 to 0.078125
- down_weight: bfloat16 [21504, 5376], P('mp'), may hold values from -0.0390625 to 0.0390625
Outputs:
- layer_out: bfloat16 [1024, 5376], P(('groups', 'seq', 'mp')), parts along dimension 0
The draws below stay inside these ranges and needn't reach their ends.
There are 2 independent parts, one for each index of `groups`. The reference program is written for one: setup_inputs(seed, part) draws one part's arguments, and reference() takes and returns one part's arrays. A program takes and returns all parts, laid end to end along the dimension named above; an argument that names none is the same for every part. Nothing has to cross between parts.
Inputs may be any that keep to these rules, and one draw needn't show every extreme that they name: positions[i] is i minus the first row of the document that holds row i; documents are consecutive runs of rows; one document of exactly 384 rows starts before row 32, the rows before it and the rows after it up to row 448 form shorter documents, and the last document starts at row 448. window_start[i] = max(first row of the document that holds row i, i - 191).
All inputs are finite; a program needn't handle non-finite values.
Results may differ from the reference program's by a relative error of at most 0.02.
Values may be sent and summed in bfloat16 or wider, within the bound.
A program may use at most 192 MiB of HBM per device.

```python
import jax
import jax.numpy as jnp
from jax import lax

D = 5376
FF = 21504
QH = 32
KVH = 16
HD = 128
WAL = 64
TOK_DEV = 256
WINDOW = 192
SEQ = 512


def document_starts(base_key):
    folded = jax.random.fold_in(base_key, 7)
    cut_key, flag_key = jax.random.split(folded)
    first_cut = jax.random.randint(cut_key, (), 1, TOK_DEV // 8)
    second_cut = first_cut + (SEQ - TOK_DEV // 2)
    third_cut = SEQ - TOK_DEV // 4
    row_index = jnp.arange(SEQ, dtype=jnp.int32)
    random_flags = jax.random.randint(flag_key, (SEQ,), 0, 2) == 1
    in_front = row_index < first_cut
    in_middle = (row_index > second_cut) & (row_index < third_cut)
    fixed_start = (row_index == 0) | (row_index == first_cut) | (row_index == second_cut) | (row_index == third_cut)
    is_start = fixed_start | (in_front | in_middle) & random_flags
    marked = jnp.where(is_start, row_index, 0).astype(jnp.int32)
    starts = lax.cummax(marked, axis=0)
    return (row_index, starts.astype(jnp.int32))


def draw_positions(key, part):
    row_index, starts = document_starts(key)
    return (row_index - starts).astype(jnp.int32)


def draw_window_start(key, part):
    row_index, starts = document_starts(key)
    return jnp.maximum(starts, row_index - WINDOW + 1).astype(jnp.int32)


def level_of(rng, shape, cuts, least, top_value):
    def one(axis_at, parts):
        draws = jax.random.uniform(jax.random.fold_in(jax.random.fold_in(rng, 6), axis_at), (parts,), jnp.float32, least / len(cuts), top_value / len(cuts))
        return jnp.repeat(jnp.exp(draws), shape[axis_at] // parts).reshape((-1,) + (1,) * (len(shape) - axis_at - 1))

    loudness = one(*cuts[0])
    for cut in cuts[1:]:
        loudness = loudness * one(*cut)
    return loudness


def centred(own_key, shape, width, limit, pieces=(), kind=jnp.bfloat16):
    values = width * jax.random.normal(own_key, shape, jnp.float32)
    if pieces:
        values = values * level_of(own_key, shape, pieces, -0.22, 0.18)
    return jnp.clip(values, -limit, limit).astype(kind)


def setup_inputs(seed: int = 0, part: int = 0) -> dict:
    keys = jax.random.split(jax.random.key(seed), 15)
    part_splits = jax.random.split(jax.random.fold_in(keys[14], part), 15)
    residual = centred(part_splits[0], (SEQ, D), 1.0, 6.0, ((0, 16),))
    positions = draw_positions(jax.random.fold_in(jax.random.fold_in(keys[14], part), 71), part)
    window_start = draw_window_start(jax.random.fold_in(jax.random.fold_in(keys[14], part), 71), part)
    input_gain = jnp.clip(1.0 + 0.18 * jax.random.normal(keys[3], (D,), jnp.float32), 0.1, 1.9)
    attention_gain = jnp.clip(1.0 + 0.18 * jax.random.normal(keys[4], (D,), jnp.float32), 0.1, 1.9)
    feedforward_gain = jnp.clip(1.0 + 0.18 * jax.random.normal(keys[5], (D,), jnp.float32), 0.1, 1.9)
    output_gain = jnp.clip(1.0 + 0.18 * jax.random.normal(keys[6], (D,), jnp.float32), 0.1, 1.9)
    query_weight = centred(keys[7], (D, QH * HD), D ** -0.5, 0.078125, ((1, 8),))
    key_weight = centred(keys[8], (D, KVH * HD), D ** -0.5, 0.078125, ((1, 8),))
    value_weight = centred(keys[9], (D, KVH * HD), D ** -0.5, 0.078125, ((1, 8),))
    output_weight = centred(keys[10], (QH * HD, D), (QH * HD) ** -0.5, 0.09375, ((0, 8),))
    gate_weight = centred(keys[11], (D, FF), D ** -0.5, 0.078125, ((1, 8),))
    up_weight = centred(keys[12], (D, FF), D ** -0.5, 0.078125, ((1, 8),))
    down_weight = centred(keys[13], (FF, D), FF ** -0.5, 0.0390625, ((0, 8),))
    return dict(residual=residual, positions=positions, window_start=window_start, input_gain=input_gain, attention_gain=attention_gain, feedforward_gain=feedforward_gain, output_gain=output_gain, query_weight=query_weight, key_weight=key_weight, value_weight=value_weight, output_weight=output_weight, gate_weight=gate_weight, up_weight=up_weight, down_weight=down_weight)


epsilon = 1e-06

def normalize(values_in, gain_row):
    widened = values_in.astype(jnp.float32)
    mean_square = lax.optimization_barrier(jnp.mean(widened * widened, axis=-1, keepdims=True))
    return widened * lax.rsqrt(mean_square + epsilon) * gain_row

def walsh_table(length):
    row_index = lax.broadcasted_iota(jnp.int32, (length, length), 0)
    column_index = lax.broadcasted_iota(jnp.int32, (length, length), 1)
    common = jnp.bitwise_and(row_index, column_index)
    parity = jnp.zeros((length, length), jnp.int32)
    for offset in range(max(length.bit_length() - 1, 0)):
        parity = parity + jnp.bitwise_and(jnp.right_shift(common, offset), 1)
    return (1 - 2 * jnp.bitwise_and(parity, 1)).astype(jnp.float32)

def angle_tables(positions, head_size):
    half_size = head_size // 2
    inverse = jnp.power(10000.0, -jnp.arange(half_size, dtype=jnp.float32) / half_size)
    angles = positions.astype(jnp.float32)[:, None] * inverse[None, :]
    return (jnp.cos(angles), jnp.sin(angles))

def rotary(linear, cosine_table, sine_table):
    row_count = linear.shape[0]
    half_size = cosine_table.shape[1]
    split_heads = linear.astype(jnp.float32).reshape(row_count, -1, 2 * half_size)
    front_half = split_heads[:, :, :half_size]
    back_half = split_heads[:, :, half_size:]
    cos_rows = cosine_table[:, None, :]
    sin_rows = sine_table[:, None, :]
    turned = jnp.concatenate([front_half * cos_rows - back_half * sin_rows, back_half * cos_rows + front_half * sin_rows], axis=-1)
    return turned.reshape(row_count, -1)

def reference(residual, positions, window_start, input_gain, attention_gain, feedforward_gain, output_gain, query_weight, key_weight, value_weight, output_weight, gate_weight, up_weight, down_weight):
    highest = lax.Precision.HIGHEST
    normed = normalize(residual, input_gain).astype(jnp.bfloat16)
    query_linear = jnp.dot(normed, query_weight, preferred_element_type=jnp.float32).astype(jnp.bfloat16)
    key_linear = jnp.dot(normed, key_weight, preferred_element_type=jnp.float32).astype(jnp.bfloat16)
    value_rows = jnp.dot(normed, value_weight, preferred_element_type=jnp.float32).astype(jnp.bfloat16)
    cosine_table, sine_table = angle_tables(positions, HD)
    queries = (rotary(query_linear, cosine_table, sine_table) * float(D // QH) ** (-0.5)).astype(jnp.bfloat16)
    key_rows = rotary(key_linear, cosine_table, sine_table).astype(jnp.bfloat16)
    row_index = jnp.arange(SEQ, dtype=jnp.int32)
    allowed = (row_index[None, :] <= row_index[:, None]) & (row_index[None, :] >= window_start[:, None])
    grouped_queries = queries.reshape(SEQ, KVH, 2, HD).transpose(1, 0, 2, 3)
    grouped_keys = key_rows.reshape(SEQ, KVH, HD).transpose(1, 0, 2)
    grouped_values = value_rows.reshape(SEQ, KVH, HD).transpose(1, 0, 2)

    def one_group(operands):
        group_queries, group_keys, group_values = operands
        scores = jnp.einsum('qtd,kd->tqk', group_queries.astype(jnp.float32), group_keys.astype(jnp.float32), precision=highest)
        scores = jnp.where(allowed[None], scores, -1e+30)
        largest = lax.optimization_barrier(jnp.max(scores, axis=-1, keepdims=True))
        exponent = jnp.exp(scores - largest)
        probabilities = (exponent / lax.optimization_barrier(jnp.sum(exponent, axis=-1, keepdims=True))).astype(jnp.bfloat16)
        combined = jnp.einsum('tqk,kd->qtd', probabilities.astype(jnp.float32), group_values.astype(jnp.float32), precision=highest)
        return combined.astype(jnp.bfloat16)
    attended = lax.map(one_group, (grouped_queries, grouped_keys, grouped_values))
    attended = attended.transpose(1, 0, 2, 3).reshape(SEQ, QH, HD)
    rotated = jnp.einsum('shd,de->she', attended.astype(jnp.float32), walsh_table(HD), precision=highest) * float(HD) ** (-0.5)
    rotated = rotated.astype(jnp.bfloat16).reshape(SEQ, QH * HD)
    attention_out = jnp.dot(rotated, output_weight, preferred_element_type=jnp.float32)
    first_sum = (residual.astype(jnp.float32) + normalize(attention_out, attention_gain)).astype(jnp.bfloat16)
    feed_input = normalize(first_sum, feedforward_gain).astype(jnp.bfloat16)
    gate_out = jnp.dot(feed_input, gate_weight, preferred_element_type=jnp.float32)
    up_out = jnp.dot(feed_input, up_weight, preferred_element_type=jnp.float32)
    activated = (jax.nn.gelu(gate_out, approximate=True) * up_out).astype(jnp.bfloat16)
    spread = jnp.einsum('sab,ac->scb', activated.reshape(SEQ, WAL, FF // WAL).astype(jnp.float32), walsh_table(WAL), precision=highest) * float(WAL) ** (-0.5)
    spread = spread.astype(jnp.bfloat16).reshape(SEQ, FF)
    down_out = jnp.dot(spread, down_weight, preferred_element_type=jnp.float32)
    return (first_sum.astype(jnp.float32) + normalize(down_out, output_gain)).astype(jnp.bfloat16)
```

```python
import functools

import jax
import jax.numpy as jnp
from jax import lax
from jax.experimental import pallas as pl
from jax.experimental.pallas import tpu as pltpu
from jax.sharding import PartitionSpec as P

D = 5376
FF = 21504
QH = 32
HD = 128
WAL = 64


epsilon = 1e-06


MESH = pl.DeviceIdType.MESH


def block_of(ref, index, rows):
    return ref.at[pl.ds(pl.multiple_of(index * rows, rows), rows)]


def send(source, target, send_sem, recv_sem, device):
    return pltpu.make_async_remote_copy(
        src_ref=source,
        dst_ref=target,
        send_sem=send_sem,
        recv_sem=recv_sem,
        device_id={"mp": device},
        device_id_type=MESH,
    )


def place(count):
    me = lax.axis_index("mp")
    column = lax.rem(me, 2)
    line = lax.div(me, 2)
    return me, column, line, count // 2, me + 1 - 2 * column


def greet(me, line, lines, peer):
    barrier = pltpu.get_barrier_semaphore()
    pl.semaphore_signal(barrier, inc=1, device_id={"mp": peer}, device_id_type=MESH)

    @pl.when(line > 0)
    def _():
        pl.semaphore_signal(barrier, inc=1, device_id={"mp": me - 2}, device_id_type=MESH)

    @pl.when(line < lines - 1)
    def _():
        pl.semaphore_signal(barrier, inc=1, device_id={"mp": me + 2}, device_id_type=MESH)

    beside = jnp.minimum(line, 1) + jnp.minimum(lines - 1 - line, 1)
    pl.semaphore_wait(barrier, 1 + beside)


def gather_kernel(count, own_ref, all_ref, xs, xr, us, ur, ds, dr):
    rows = own_ref.shape[0]
    me, column, line, lines, peer = place(count)
    greet(me, line, lines, peer)

    def across(origin, source):
        there = block_of(all_ref, origin * 2 + column, rows)
        return send(source, there, xs.at[origin], xr.at[origin], peer)

    def upward(origin, source):
        there = block_of(all_ref, origin * 2 + column, rows)
        return send(source, there, us.at[origin], ur.at[origin], me + 2)

    def downward(origin, source):
        there = block_of(all_ref, origin * 2 + column, rows)
        return send(source, there, ds.at[origin], dr.at[origin], me - 2)

    @pl.when(line < lines - 1)
    def _():
        upward(line, own_ref).start()

    @pl.when(line > 0)
    def _():
        downward(line, own_ref).start()

    across(line, own_ref).start()
    all_ref[pl.ds(pl.multiple_of(me * rows, rows), rows), :] = own_ref[...]
    for step in range(1, lines):

        @pl.when(line - step >= 0)
        def _():
            origin = line - step
            held = block_of(all_ref, origin * 2 + column, rows)
            upward(origin, held).wait_recv()

            @pl.when(line < lines - 1)
            def _():
                upward(origin, held).start()

            across(origin, held).start()

        @pl.when(line + step < lines)
        def _():
            origin = line + step
            held = block_of(all_ref, origin * 2 + column, rows)
            downward(origin, held).wait_recv()

            @pl.when(line > 0)
            def _():
                downward(origin, held).start()

            across(origin, held).start()

    for origin in range(lines):
        across(origin, own_ref).wait_send()
        there = block_of(all_ref, origin * 2 + 1 - column, rows)
        send(own_ref, there, xs.at[origin], xr.at[origin], peer).wait_recv()

        @pl.when((origin <= line) & (line < lines - 1))
        def _():
            upward(origin, own_ref).wait_send()

        @pl.when((origin >= line) & (line > 0))
        def _():
            downward(origin, own_ref).wait_send()


def gather_rows(own):
    count = lax.axis_size("mp")
    rows, width = own.shape
    if rows % 16 or count % 2 or count < 4:
        return lax.all_gather(own, "mp", axis=0, tiled=True)
    lines = count // 2
    return pl.pallas_call(
        functools.partial(gather_kernel, count),
        out_shape=jax.ShapeDtypeStruct((count * rows, width), own.dtype),
        in_specs=[pl.BlockSpec(memory_space=pltpu.VMEM)],
        out_specs=pl.BlockSpec(memory_space=pltpu.VMEM),
        scratch_shapes=[pltpu.SemaphoreType.DMA((lines,))] * 6,
        compiler_params=pltpu.CompilerParams(
            collective_id=0, has_side_effects=True, vmem_limit_bytes=16 * 1024 * 1024
        ),
    )(own)


def scatter_kernel(count, term_ref, sum_ref, xb, ub, db, sb, xs, xr, us, ur, ds, dr):
    rows, width = sum_ref.shape
    me, column, line, lines, peer = place(count)
    step_width = 768 if width % 768 == 0 else 128
    greet(me, line, lines, peer)

    def across(dest):
        mine = block_of(term_ref, dest * 2 + 1 - column, rows)
        return send(mine, xb.at[dest], xs.at[dest], xr.at[dest], peer)

    def upward(dest):
        return send(sb.at[dest], ub.at[dest], us.at[dest], ur.at[dest], me + 2)

    def downward(dest):
        return send(sb.at[dest], db.at[dest], ds.at[dest], dr.at[dest], me - 2)

    for away in range(lines - 1, -1, -1):

        @pl.when(line - away >= 0)
        def _():
            across(line - away).start()

        if away:

            @pl.when(line + away < lines)
            def _():
                across(line + away).start()

    def add(dest, arrived, target, index):
        first = pl.multiple_of((dest * 2 + column) * rows, rows)

        def some(i, carry):
            cols = pl.ds(pl.multiple_of(i * step_width, step_width), step_width)
            total = term_ref[pl.ds(first, rows), cols].astype(jnp.float32)
            total = total + xb[dest, :, cols].astype(jnp.float32)
            for ref in arrived:
                total = total + ref[dest, :, cols].astype(jnp.float32)
            if index:
                target[dest, :, cols] = total.astype(target.dtype)
            else:
                target[:, cols] = total
            return carry

        lax.fori_loop(0, width // step_width, some, 0)

    def go_up(dest):
        @pl.when(dest > line)
        def _():
            across(dest).wait_recv()

            @pl.when(line > 0)
            def _():
                upward(dest).wait_recv()
                add(dest, (ub,), sb, True)

            @pl.when(line == 0)
            def _():
                add(dest, (), sb, True)

            upward(dest).start()

    def go_down(dest):
        @pl.when(dest < line)
        def _():
            across(dest).wait_recv()

            @pl.when(line < lines - 1)
            def _():
                downward(dest).wait_recv()
                add(dest, (db,), sb, True)

            @pl.when(line == lines - 1)
            def _():
                add(dest, (), sb, True)

            downward(dest).start()

    for j in range(lines - 1):

        @pl.when(2 * line < lines)
        def _():
            go_up(lines - 1 - j)
            go_down(j)

        @pl.when(2 * line >= lines)
        def _():
            go_down(j)
            go_up(lines - 1 - j)

    across(line).wait_recv()

    @pl.when(line > 0)
    def _():
        upward(line).wait_recv()

    @pl.when(line < lines - 1)
    def _():
        downward(line).wait_recv()

    @pl.when((line > 0) & (line < lines - 1))
    def _():
        add(line, (ub, db), sum_ref, False)

    @pl.when(line == 0)
    def _():
        add(line, (db,), sum_ref, False)

    @pl.when(line == lines - 1)
    def _():
        add(line, (ub,), sum_ref, False)

    for dest in range(lines):
        across(dest).wait_send()

        @pl.when(dest > line)
        def _():
            upward(dest).wait_send()

        @pl.when(dest < line)
        def _():
            downward(dest).wait_send()


def scatter_rows(term):
    count = lax.axis_size("mp")
    rows, width = term.shape[0] // count, term.shape[1]
    if rows % 16 or count % 2 or count < 4:
        return lax.psum_scatter(term, "mp", scatter_dimension=0, tiled=True)
    lines = count // 2
    blocks = pltpu.VMEM((lines, rows, width), jnp.bfloat16)
    return pl.pallas_call(
        functools.partial(scatter_kernel, count),
        out_shape=jax.ShapeDtypeStruct((rows, width), jnp.float32),
        in_specs=[pl.BlockSpec(memory_space=pltpu.VMEM)],
        out_specs=pl.BlockSpec(memory_space=pltpu.VMEM),
        scratch_shapes=[blocks] * 4 + [pltpu.SemaphoreType.DMA((lines,))] * 6,
        compiler_params=pltpu.CompilerParams(
            collective_id=1, has_side_effects=True, vmem_limit_bytes=24 * 1024 * 1024
        ),
    )(term.astype(jnp.bfloat16))


def hidden_kernel(count, tiles, feed_ref, gate_ref, up_ref, out_ref, act, got, ss, rs):
    rows = feed_ref.shape[0] // count
    width = gate_ref.shape[1]
    tile = pl.program_id(0)
    me = lax.axis_index("mp")

    @pl.when(tile == 0)
    def _():
        barrier = pltpu.get_barrier_semaphore()
        for k in range(1, count):
            other = lax.rem(me + k, count)
            pl.semaphore_signal(barrier, inc=1, device_id={"mp": other}, device_id_type=MESH)
        pl.semaphore_wait(barrier, count - 1)

    feed = feed_ref[...]
    gate_out = jnp.dot(feed, gate_ref[...], preferred_element_type=jnp.float32)
    up_out = jnp.dot(feed, up_ref[...], preferred_element_type=jnp.float32)
    act[tile] = (jax.nn.gelu(gate_out, approximate=True) * up_out).astype(jnp.bfloat16)

    def to(k, t):
        other = lax.rem(me + k, count)
        source = act.at[t, pl.ds(pl.multiple_of(other * rows, rows), rows), :]
        target = got.at[t, pl.ds(pl.multiple_of(me * rows, rows), rows), :]
        return send(source, target, ss.at[k, t], rs.at[k, t], other)

    for k in range(1, count):
        to(k, tile).start()
    own = pl.ds(pl.multiple_of(me * rows, rows), rows)
    got[tile, own, :] = act[tile, own, :]

    @pl.when(tile == tiles - 1)
    def _():
        for t in range(tiles):
            for k in range(1, count):
                to(k, t).wait_recv()
            out_ref[:, t * width : (t + 1) * width] = got[t]
        for t in range(tiles):
            for k in range(1, count):
                to(k, t).wait_send()


def hidden_rows(feed, gate_weight, up_weight):
    count = lax.axis_size("mp")
    length, depth = feed.shape
    hidden = gate_weight.shape[1]
    rows, tile = length // count, 384
    tiles = hidden // tile
    weights = pl.BlockSpec((depth, tile), lambda t: (0, t))
    return pl.pallas_call(
        functools.partial(hidden_kernel, count, tiles),
        grid=(tiles,),
        out_shape=jax.ShapeDtypeStruct((length, hidden), jnp.bfloat16),
        in_specs=[pl.BlockSpec((length, depth), lambda t: (0, 0)), weights, weights],
        out_specs=pl.BlockSpec((length, hidden), lambda t: (0, 0)),
        scratch_shapes=[
            pltpu.VMEM((tiles, length, tile), jnp.bfloat16),
            pltpu.VMEM((tiles, length, tile), jnp.bfloat16),
            pltpu.SemaphoreType.DMA((count, tiles)),
            pltpu.SemaphoreType.DMA((count, tiles)),
        ],
        compiler_params=pltpu.CompilerParams(
            collective_id=2,
            has_side_effects=True,
            dimension_semantics=("arbitrary",),
            vmem_limit_bytes=48 * 1024 * 1024,
        ),
    )(feed, gate_weight, up_weight)


def chunk_width(width):
    return 768 if width % 768 == 0 else 128


def signal_to(device):
    barrier = pltpu.get_barrier_semaphore()
    pl.semaphore_signal(barrier, inc=1, device_id={"mp": device}, device_id_type=MESH)


def row_scale(read, parts, width):
    def some(c, total):
        values = read(c)
        return total + jnp.sum(values * values, axis=-1, keepdims=True)

    first = read(0)
    total = lax.fori_loop(1, parts, some, jnp.sum(first * first, axis=-1, keepdims=True))
    return lax.rsqrt(total / width + epsilon)


def columns_of(c, width):
    return pl.ds(pl.multiple_of(c * width, width), width)


class Gather:
    def __init__(self, count, rows, buf, sems):
        self.buf, self.rows, self.sems = buf, rows, sems
        self.parts = buf.shape[0]
        self.me, self.column, self.line, self.lines, self.peer = place(count)

    def block(self, c, origin, column):
        first = pl.multiple_of((origin * 2 + column) * self.rows, self.rows)
        return self.buf.at[c, pl.ds(first, self.rows), :]

    def move(self, c, origin, column, which, device):
        there = self.block(c, origin, column)
        return send(
            there, there, self.sems[which].at[c, origin], self.sems[which + 1].at[c, origin], device
        )

    def across(self, c, origin):
        return self.move(c, origin, self.column, 0, self.peer)

    def upward(self, c, origin):
        return self.move(c, origin, self.column, 2, self.me + 2)

    def downward(self, c, origin):
        return self.move(c, origin, self.column, 4, self.me - 2)

    def step(self, t):
        line, lines = self.line, self.lines

        @pl.when(t < self.parts)
        def _():
            @pl.when(line < lines - 1)
            def _():
                self.upward(t, line).start()

            @pl.when(line > 0)
            def _():
                self.downward(t, line).start()

            self.across(t, line).start()

        for away in range(1, lines):
            c = t - away

            @pl.when((c >= 0) & (c < self.parts) & (line - away >= 0))
            def _():
                self.upward(c, line - away).wait_recv()

                @pl.when(line < lines - 1)
                def _():
                    self.upward(c, line - away).start()

                self.across(c, line - away).start()

            @pl.when((c >= 0) & (c < self.parts) & (line + away < lines))
            def _():
                self.downward(c, line + away).wait_recv()

                @pl.when(line > 0)
                def _():
                    self.downward(c, line + away).start()

                self.across(c, line + away).start()

    def arrived(self, c):
        for origin in range(self.lines):
            self.move(c, origin, 1 - self.column, 0, self.peer).wait_recv()

    def finish(self):
        line, lines = self.line, self.lines

        def one(c, carry):
            for origin in range(lines):
                self.across(c, origin).wait_send()

                @pl.when((origin <= line) & (line < lines - 1))
                def _():
                    self.upward(c, origin).wait_send()

                @pl.when((origin >= line) & (line > 0))
                def _():
                    self.downward(c, origin).wait_send()

            return carry

        lax.fori_loop(0, self.parts, one, 0)


class Scatter:
    def __init__(self, count, rows, term, xb, ub, db, sb, sums, sems):
        self.term, self.xb, self.ub, self.db, self.sb, self.sums = term, xb, ub, db, sb, sums
        self.rows, self.sems = rows, sems
        self.parts = term.shape[0]
        self.me, self.column, self.line, self.lines, self.peer = place(count)

    def mine(self, dest, column):
        return pl.ds(pl.multiple_of((dest * 2 + column) * self.rows, self.rows), self.rows)

    def across(self, c, dest):
        source = self.term.at[c, self.mine(dest, 1 - self.column), :]
        xs, xr = self.sems[:2]
        return send(source, self.xb.at[c, dest], xs.at[c, dest], xr.at[c, dest], self.peer)

    def upward(self, c, dest):
        us, ur = self.sems[2:4]
        return send(
            self.sb.at[c, dest], self.ub.at[c, dest], us.at[c, dest], ur.at[c, dest], self.me + 2
        )

    def downward(self, c, dest):
        ds, dr = self.sems[4:6]
        return send(
            self.sb.at[c, dest], self.db.at[c, dest], ds.at[c, dest], dr.at[c, dest], self.me - 2
        )

    def total(self, c, dest, arrived):
        total = self.term[c, self.mine(dest, self.column), :].astype(jnp.float32)
        total = total + self.xb[c, dest].astype(jnp.float32)
        for ref in arrived:
            total = total + ref[c, dest].astype(jnp.float32)
        return total

    def pass_on(self, c, dest, move, ref, is_end):
        self.across(c, dest).wait_recv()

        @pl.when(is_end)
        def _():
            self.sb[c, dest] = self.total(c, dest, ()).astype(self.sb.dtype)

        @pl.when(jnp.logical_not(is_end))
        def _():
            move(c, dest).wait_recv()
            self.sb[c, dest] = self.total(c, dest, (ref,)).astype(self.sb.dtype)

        move(c, dest).start()

    def run(self, produce):
        line, lines, parts = self.line, self.lines, self.parts

        def step(t, carry):
            @pl.when(t < parts)
            def _():
                produce(t)
                for away in range(lines - 1, -1, -1):

                    @pl.when(line - away >= 0)
                    def _():
                        self.across(t, line - away).start()

                    if away:

                        @pl.when(line + away < lines)
                        def _():
                            self.across(t, line + away).start()

            cu = t - 1 - line
            cd = t - lines + line
            for j in range(lines - 1):
                dest = lines - 1 - j

                @pl.when((cu >= 0) & (cu < parts) & (dest > line))
                def _():
                    self.pass_on(cu, dest, self.upward, self.ub, line == 0)

                @pl.when((cd >= 0) & (cd < parts) & (j < line))
                def _():
                    self.pass_on(cd, j, self.downward, self.db, line == lines - 1)

            c = t - lines

            @pl.when(c >= 0)
            def _():
                self.across(c, line).wait_recv()

                @pl.when(line == 0)
                def _():
                    self.downward(c, line).wait_recv()
                    self.sums[c] = self.total(c, line, (self.db,))

                @pl.when(line == lines - 1)
                def _():
                    self.upward(c, line).wait_recv()
                    self.sums[c] = self.total(c, line, (self.ub,))

                @pl.when((line > 0) & (line < lines - 1))
                def _():
                    self.upward(c, line).wait_recv()
                    self.downward(c, line).wait_recv()
                    self.sums[c] = self.total(c, line, (self.ub, self.db))

            return carry

        lax.fori_loop(0, parts + lines, step, 0)

        def one(c, carry):
            for dest in range(lines):
                self.across(c, dest).wait_send()

                @pl.when(dest > line)
                def _():
                    self.upward(c, dest).wait_send()

                @pl.when(dest < line)
                def _():
                    self.downward(c, dest).wait_send()

            return carry

        lax.fori_loop(0, parts, one, 0)


def front_kernel(count, own_ref, gain_ref, wq, wk, wv, q_ref, k_ref, v_ref, buf, w, acc, ws, *sems):
    rows, width = own_ref.shape
    parts, length, part = buf.shape
    wide, narrow = wq.shape[1], wk.shape[1]
    spans = ((wq, 0, wide), (wk, wide, narrow), (wv, wide + narrow, narrow))
    gather = Gather(count, rows, buf, sems)
    me, line, lines, peer = gather.me, gather.line, gather.lines, gather.peer

    def load(c, i):
        source, first, size = spans[i]
        return pltpu.make_async_copy(
            source.at[columns_of(c, part), :],
            w.at[columns_of(c, part), first : first + size],
            ws.at[c, i],
        )

    greet_start(me, line, lines, peer)

    def read(c):
        return own_ref[:, columns_of(c, part)].astype(jnp.float32)

    scale = row_scale(read, parts, width)
    own = pl.ds(pl.multiple_of(me * rows, rows), rows)

    def place_own(c, carry):
        normed = read(c) * scale * gain_ref[:, columns_of(c, part)]
        buf[c, own, :] = normed.astype(buf.dtype)
        return carry

    lax.fori_loop(0, parts, place_own, 0)
    greet_wait(line, lines)

    def load_all(c, carry):
        for i in range(3):
            load(c, i).start()
        return carry

    acc[...] = jnp.zeros_like(acc)

    def step(t, carry):
        gather.step(t)

        @pl.when(t == 0)
        def _():
            lax.fori_loop(0, parts, load_all, 0)

        c = t - lines

        @pl.when(c >= 0)
        def _():
            for i in range(3):
                load(c, i).wait()
            gather.arrived(c)
            tile = 256

            def some(n, carry):
                cols = columns_of(n, tile)
                acc[:, cols] += jnp.dot(
                    buf[c], w[columns_of(c, part), cols], preferred_element_type=jnp.float32
                )
                return carry

            lax.fori_loop(0, acc.shape[1] // tile, some, 0)

        return carry

    lax.fori_loop(0, parts + lines, step, 0)
    for (_, first, size), out in zip(spans, (q_ref, k_ref, v_ref)):
        out[...] = acc[:, first : first + size].astype(out.dtype)
    gather.finish()


def greet_start(me, line, lines, peer):
    signal_to(peer)

    @pl.when(line > 0)
    def _():
        signal_to(me - 2)

    @pl.when(line < lines - 1)
    def _():
        signal_to(me + 2)


def greet_wait(line, lines):
    beside = jnp.minimum(line, 1) + jnp.minimum(lines - 1 - line, 1)
    pl.semaphore_wait(pltpu.get_barrier_semaphore(), 1 + beside)


def project(residual, gain, query_weight, key_weight, value_weight):
    count = lax.axis_size("mp")
    rows, width = residual.shape
    part = chunk_width(width)
    parts, lines, length = width // part, count // 2, count * rows
    sizes = (query_weight.shape[1], key_weight.shape[1], value_weight.shape[1])
    vmem = pl.BlockSpec(memory_space=pltpu.VMEM)
    hbm = pl.BlockSpec(memory_space=pl.ANY)
    return pl.pallas_call(
        functools.partial(front_kernel, count),
        out_shape=[jax.ShapeDtypeStruct((length, size), residual.dtype) for size in sizes],
        in_specs=[vmem, vmem, hbm, hbm, hbm],
        out_specs=[vmem] * 3,
        scratch_shapes=[
            pltpu.VMEM((parts, length, part), jnp.bfloat16),
            pltpu.VMEM((width, sum(sizes)), jnp.bfloat16),
            pltpu.VMEM((length, sum(sizes)), jnp.float32),
            pltpu.SemaphoreType.DMA((parts, 3)),
        ]
        + [pltpu.SemaphoreType.DMA((parts, lines))] * 6,
        compiler_params=pltpu.CompilerParams(
            collective_id=3, has_side_effects=True, vmem_limit_bytes=32 * 1024 * 1024
        ),
    )(residual, gain.reshape(1, width), query_weight, key_weight, value_weight)


def butterfly(values):
    values = list(values)
    apart = 1
    while apart < len(values):
        for low in range(len(values)):
            if low // apart % 2 == 0:
                a, b = values[low], values[low + apart]
                values[low], values[low + apart] = a + b, a - b
        apart *= 2
    return values


def tail_kernel(
    count, blocks, rot, resid, att_gain, feed_gain, out_gain, wo, wg, wu, wd, out_ref,
    wo_buf, term, xb, ub, db, sb, sums, first, feed, gu, acc, act, got, mixed, spread, spun, dbuf,
    wo_sem, gu_sem, d_sem, a_send, a_recv, b_send, b_recv, *sems,
):
    rows, width = resid.shape
    parts, length, part = term.shape
    hidden = wg.shape[1]
    slots, d_slots = gu.shape[0], dbuf.shape[0]
    halves = rows // 16
    local = blocks // count
    inner = hidden // local
    scatter = Scatter(count, rows, term, xb, ub, db, sb, sums, sems[:6])
    gather = Gather(count, rows, feed, sems[6:])
    me, lines = scatter.me, scatter.lines

    for k in range(1, count):
        signal_to(lax.rem(me + k, count))

    def load_wo(c):
        cols = columns_of(c, part)
        return pltpu.make_async_copy(wo.at[:, cols], wo_buf.at[:, cols], wo_sem.at[c])

    def load_gu(c, i):
        slot = lax.rem(c, slots)
        source = (wg, wu)[i].at[columns_of(c, part), :]
        return pltpu.make_async_copy(source, gu.at[slot, i], gu_sem.at[slot, i])

    def load_d(c):
        slot = lax.rem(c, d_slots)
        return pltpu.make_async_copy(wd.at[:, columns_of(c, part)], dbuf.at[slot], d_sem.at[slot])

    for c in range(parts):
        load_wo(c).start()
    for c in range(slots):
        for i in range(2):
            load_gu(c, i).start()
    for c in range(d_slots):
        load_d(c).start()
    pl.semaphore_wait(pltpu.get_barrier_semaphore(), count - 1)

    tile = 384

    def attention_part(c):
        load_wo(c).wait()

        def some(n, carry):
            cols = pl.ds(pl.multiple_of(c * part + n * tile, tile), tile)
            value = jnp.dot(rot[...], wo_buf[:, cols], preferred_element_type=jnp.float32)
            term[c, :, columns_of(n, tile)] = value.astype(term.dtype)
            return carry

        lax.fori_loop(0, part // tile, some, 0)

    scatter.run(attention_part)

    att_scale = row_scale(lambda c: sums[c], parts, width)

    def add_residual(c, carry):
        cols = columns_of(c, part)
        value = sums[c] * att_scale * att_gain[:, cols]
        value = resid[:, cols].astype(jnp.float32) + value
        first[c] = value.astype(first.dtype)
        return carry

    lax.fori_loop(0, parts, add_residual, 0)
    feed_scale = row_scale(lambda c: first[c].astype(jnp.float32), parts, width)
    own = pl.ds(pl.multiple_of(me * rows, rows), rows)

    def place_own(c, carry):
        value = first[c].astype(jnp.float32) * feed_scale * feed_gain[:, columns_of(c, part)]
        feed[c, own, :] = value.astype(feed.dtype)
        return carry

    lax.fori_loop(0, parts, place_own, 0)

    def feed_step(t, carry):
        gather.step(t)
        c = t - lines

        @pl.when(t == 0)
        def _():
            acc[...] = jnp.zeros_like(acc)

        @pl.when(c >= 0)
        def _():
            for i in range(2):
                load_gu(c, i).wait()
            gather.arrived(c)
            slot = lax.rem(c, slots)

            def some(n, carry):
                cols = columns_of(n, tile)
                for i in range(2):
                    acc[i, :, cols] += jnp.dot(
                        feed[c], gu[slot, i, :, cols], preferred_element_type=jnp.float32
                    )
                return carry

            lax.fori_loop(0, hidden // tile, some, 0)

            @pl.when(c + slots < parts)
            def _():
                for i in range(2):
                    load_gu(c + slots, i).start()

        return carry

    lax.fori_loop(0, parts + lines, feed_step, 0)

    def half_rows(device, h):
        return pl.ds(pl.multiple_of(device * rows + h * 16, 16), 16)

    def to_mixer(h, k):
        other = lax.rem(me + k, count)
        return send(
            act.at[half_rows(other, h), :],
            got.at[me, pl.ds(h * 16, 16), :],
            a_send.at[h, k],
            a_recv.at[h, k],
            other,
        )

    def from_mixer(h, k):
        other = lax.rem(me + k, count)
        return send(
            spread.at[other, pl.ds(h * 16, 16), :],
            spun.at[half_rows(me, h), :],
            b_send.at[h, k],
            b_recv.at[h, k],
            other,
        )

    for h in range(halves):

        def activate(k, carry):
            here = half_rows(lax.rem(me + k, count), h)

            def some(n, carry):
                cols = columns_of(n, tile)
                value = jax.nn.gelu(acc[0, here, cols], approximate=True) * acc[1, here, cols]
                act[here, cols] = value.astype(act.dtype)
                return carry

            lax.fori_loop(0, hidden // tile, some, 0)

            @pl.when(k < count)
            def _():
                to_mixer(h, k).start()

            return carry

        lax.fori_loop(1, count + 1, activate, 0)
        got[me, h * 16 : h * 16 + 16, :] = act[half_rows(me, h), :]

    for h in range(halves):
        for k in range(1, count):
            to_mixer(h, k).wait_recv()

        def over_devices(n, carry):
            cols = columns_of(n, tile)
            held = [got[d, h * 16 : h * 16 + 16, cols].astype(jnp.float32) for d in range(count)]
            for d, value in enumerate(butterfly(held)):
                mixed[d, :, cols] = value
            return carry

        lax.fori_loop(0, hidden // tile, over_devices, 0)

        def within(k, carry):
            other = lax.rem(me + k, count)
            value = mixed[other]
            pieces = [value[:, a * inner : (a + 1) * inner] for a in range(local)]
            whole = jnp.concatenate(butterfly(pieces), axis=1) * float(blocks) ** (-0.5)
            spread[other, h * 16 : h * 16 + 16, :] = whole.astype(spread.dtype)

            @pl.when(k < count)
            def _():
                from_mixer(h, k).start()

            return carry

        lax.fori_loop(1, count + 1, within, 0)
        spun[half_rows(me, h), :] = spread[me, h * 16 : h * 16 + 16, :]

    for h in range(halves):
        for k in range(1, count):
            from_mixer(h, k).wait_recv()

    def down_part(c):
        load_d(c).wait()
        slot = lax.rem(c, d_slots)

        def some(n, carry):
            cols = columns_of(n, tile)
            value = jnp.dot(spun[...], dbuf[slot, :, cols], preferred_element_type=jnp.float32)
            term[c, :, cols] = value.astype(term.dtype)
            return carry

        lax.fori_loop(0, part // tile, some, 0)

        @pl.when(c + d_slots < parts)
        def _():
            load_d(c + d_slots).start()

    scatter.run(down_part)

    out_scale = row_scale(lambda c: sums[c], parts, width)

    def finish(c, carry):
        cols = columns_of(c, part)
        value = first[c].astype(jnp.float32) + sums[c] * out_scale * out_gain[:, cols]
        out_ref[:, cols] = value.astype(out_ref.dtype)
        return carry

    lax.fori_loop(0, parts, finish, 0)
    gather.finish()
    for h in range(halves):
        for k in range(1, count):
            to_mixer(h, k).wait_send()
            from_mixer(h, k).wait_send()


def tail(rotated, residual, gains, output_weight, gate_weight, up_weight, down_weight, blocks):
    count = lax.axis_size("mp")
    rows, width = residual.shape
    part = chunk_width(width)
    parts, lines, length = width // part, count // 2, count * rows
    hidden = gate_weight.shape[1]
    slots, halves = 2, rows // 16
    vmem = pl.BlockSpec(memory_space=pltpu.VMEM)
    hbm = pl.BlockSpec(memory_space=pl.ANY)
    bf16, f32 = jnp.bfloat16, jnp.float32
    sums = pltpu.VMEM((parts, lines, rows, part), bf16)
    dma = pltpu.SemaphoreType.DMA
    return pl.pallas_call(
        functools.partial(tail_kernel, count, blocks),
        out_shape=jax.ShapeDtypeStruct((rows, width), residual.dtype),
        in_specs=[vmem] * 5 + [hbm] * 4,
        out_specs=vmem,
        scratch_shapes=[
            pltpu.VMEM(output_weight.shape, bf16),
            pltpu.VMEM((parts, length, part), bf16),
            sums,
            sums,
            sums,
            sums,
            pltpu.VMEM((parts, rows, part), f32),
            pltpu.VMEM((parts, rows, part), bf16),
            pltpu.VMEM((parts, length, part), bf16),
            pltpu.VMEM((slots, 2, part, hidden), bf16),
            pltpu.VMEM((2, length, hidden), f32),
            pltpu.VMEM((length, hidden), bf16),
            pltpu.VMEM((count, rows, hidden), bf16),
            pltpu.VMEM((count, 16, hidden), f32),
            pltpu.VMEM((count, rows, hidden), bf16),
            pltpu.VMEM((length, hidden), bf16),
            pltpu.VMEM((slots, hidden, part), bf16),
            dma((parts,)),
            dma((slots, 2)),
            dma((slots,)),
        ]
        + [dma((halves, count))] * 4
        + [dma((parts, lines))] * 12,
        compiler_params=pltpu.CompilerParams(
            collective_id=4, has_side_effects=True, vmem_limit_bytes=60 * 1024 * 1024
        ),
    )(
        rotated,
        residual,
        *(gain.reshape(1, width) for gain in gains),
        output_weight,
        gate_weight,
        up_weight,
        down_weight,
    )


def partner(block, axis, apart):
    count = lax.axis_size(axis)
    route = []
    for low in range(count):
        high = low | 1 << apart
        if high != low and high < count:
            route += [(low, high), (high, low)]
    return lax.ppermute(block, axis, route)


def for_sending(value):
    return jax.tree.map(lambda a: a.astype(jnp.bfloat16) if a.dtype == jnp.float32 else a, value)


def from_behind(block, axis, distance):
    devices = range(lax.axis_size(axis))
    route = [(i - distance, i) for i in devices if i - distance in devices]
    return lax.ppermute(block, axis, route)


def normalize(values_in, gain_row):
    widened = values_in.astype(jnp.float32)
    mean_square = jnp.mean(widened * widened, axis=-1, keepdims=True)
    return widened * lax.rsqrt(mean_square + epsilon) * gain_row


def walsh_table(length):
    row_index = lax.broadcasted_iota(jnp.int32, (length, length), 0)
    column_index = lax.broadcasted_iota(jnp.int32, (length, length), 1)
    common = jnp.bitwise_and(row_index, column_index)
    parity = jnp.zeros((length, length), jnp.int32)
    for offset in range(max(length.bit_length() - 1, 0)):
        parity = parity + jnp.bitwise_and(jnp.right_shift(common, offset), 1)
    return (1 - 2 * jnp.bitwise_and(parity, 1)).astype(jnp.float32)


def angle_tables(positions, head_size):
    half_size = head_size // 2
    inverse = jnp.power(10000.0, -jnp.arange(half_size, dtype=jnp.float32) / half_size)
    angles = positions.astype(jnp.float32)[:, None] * inverse[None, :]
    return (jnp.cos(angles), jnp.sin(angles))


def rotary(linear, cosine_table, sine_table):
    row_count = linear.shape[0]
    half_size = cosine_table.shape[1]
    split_heads = linear.astype(jnp.float32).reshape(row_count, -1, 2 * half_size)
    front_half = split_heads[:, :, :half_size]
    back_half = split_heads[:, :, half_size:]
    cos_rows = cosine_table[:, None, :]
    sin_rows = sine_table[:, None, :]
    turned = jnp.concatenate(
        [
            front_half * cos_rows - back_half * sin_rows,
            back_half * cos_rows + front_half * sin_rows,
        ],
        axis=-1,
    )
    return turned.reshape(row_count, -1)


def join_pair(own_part, theirs, upper_bit, axis_number):
    lower_part = jnp.where(upper_bit == 1, theirs, own_part)
    upper_part = jnp.where(upper_bit == 1, own_part, theirs)
    return jnp.concatenate([lower_part, upper_part], axis=axis_number)


def attend(queries, key_rows, value_rows, allowed):
    scores = jnp.einsum("qgtd,kgd->gtqk", queries, key_rows, preferred_element_type=jnp.float32)
    scores = jnp.where(allowed[None, None], scores, -1e30)
    largest = jnp.max(scores, axis=-1, keepdims=True)
    exponent = jnp.exp(scores - largest)
    probabilities = (exponent / jnp.sum(exponent, axis=-1, keepdims=True)).astype(jnp.bfloat16)
    combined = jnp.einsum(
        "gtqk,kgd->qgtd", probabilities, value_rows, preferred_element_type=jnp.float32
    )
    return combined.astype(jnp.bfloat16)


def body(
    residual,
    positions,
    window_start,
    input_gain,
    attention_gain,
    feedforward_gain,
    output_gain,
    query_weight,
    key_weight,
    value_weight,
    output_weight,
    gate_weight,
    up_weight,
    down_weight,
):
    model_count = lax.axis_size("mp")
    model_index = lax.axis_index("mp")
    block_index = lax.axis_index("seq")
    own_rows, model_width = residual.shape
    block_length = own_rows * model_count
    fused = (
        own_rows % 16 == 0
        and model_count % 2 == 0
        and model_count >= 4
        and WAL % model_count == 0
        and gate_weight.shape[1] % 384 == 0
        and model_width % 768 == 0
    )
    if not fused:
        block_input = gather_rows(residual)
        normed = normalize(block_input, input_gain).astype(jnp.bfloat16)
    cosine_table, sine_table = angle_tables(positions, HD)
    query_scale = float(D // QH) ** (-0.5)
    paired = model_count == 2 * QH and not fused
    if paired:
        half_rows = block_length // 2
        quarter_rows = block_length // 4
        low_bit = model_index % 2
        query_first = low_bit * half_rows
        query_cosine = lax.dynamic_slice_in_dim(cosine_table, query_first, half_rows, 0)
        query_sine = lax.dynamic_slice_in_dim(sine_table, query_first, half_rows, 0)
        partner_columns = partner(query_weight, "mp", 0)
        full_query = join_pair(query_weight, partner_columns, low_bit, 1)
        query_normed = lax.dynamic_slice_in_dim(normed, query_first, half_rows, 0)
        query_linear = jnp.dot(query_normed, full_query, preferred_element_type=jnp.float32).astype(
            jnp.bfloat16
        )
        key_full = key_weight
        value_full = value_weight
        for bit_number in range(2):
            upper_bit = jnp.right_shift(model_index, bit_number) % 2
            partner_key, partner_value = (
                partner(for_sending(key_full), "mp", bit_number).astype(key_full.dtype),
                partner(for_sending(value_full), "mp", bit_number).astype(value_full.dtype),
            )
            key_full = join_pair(key_full, partner_key, upper_bit, 1)
            value_full = join_pair(value_full, partner_value, upper_bit, 1)
        quarter_first = model_index % 4 * quarter_rows
        quarter_normed = lax.dynamic_slice_in_dim(normed, quarter_first, quarter_rows, 0)
        quarter_cosine = lax.dynamic_slice_in_dim(cosine_table, quarter_first, quarter_rows, 0)
        quarter_sine = lax.dynamic_slice_in_dim(sine_table, quarter_first, quarter_rows, 0)
        key_linear = jnp.dot(quarter_normed, key_full, preferred_element_type=jnp.float32).astype(
            jnp.bfloat16
        )
        key_part = rotary(key_linear, quarter_cosine, quarter_sine).astype(jnp.bfloat16)
        value_part = jnp.dot(quarter_normed, value_full, preferred_element_type=jnp.float32).astype(
            jnp.bfloat16
        )
        for bit_number in range(2):
            upper_bit = jnp.right_shift(model_index, bit_number) % 2
            partner_key, partner_value = (
                partner(for_sending(key_part), "mp", bit_number).astype(key_part.dtype),
                partner(for_sending(value_part), "mp", bit_number).astype(value_part.dtype),
            )
            key_part = join_pair(key_part, partner_key, upper_bit, 0)
            value_part = join_pair(value_part, partner_value, upper_bit, 0)
        key_rows = key_part
        value_rows = value_part
        group_count = 1
        query_count = half_rows
        queries = (rotary(query_linear, query_cosine, query_sine) * query_scale).astype(
            jnp.bfloat16
        )
        queries = queries.reshape(query_count, 1, 1, HD)
        own_window = lax.dynamic_slice_in_dim(window_start, query_first, half_rows, 0)
    else:
        query_first = 0
        query_count = block_length
        group_count = key_weight.shape[1] // HD
        if fused:
            query_linear, key_linear, value_rows = project(
                residual, input_gain, query_weight, key_weight, value_weight
            )
        else:
            query_linear = jnp.dot(normed, query_weight, preferred_element_type=jnp.float32)
            query_linear = query_linear.astype(jnp.bfloat16)
            key_linear = jnp.dot(normed, key_weight, preferred_element_type=jnp.float32)
            key_linear = key_linear.astype(jnp.bfloat16)
            value_rows = jnp.dot(normed, value_weight, preferred_element_type=jnp.float32)
            value_rows = value_rows.astype(jnp.bfloat16)
        key_rows = rotary(key_linear, cosine_table, sine_table).astype(jnp.bfloat16)
        queries = (rotary(query_linear, cosine_table, sine_table) * query_scale).astype(
            jnp.bfloat16
        )
        queries = queries.reshape(query_count, group_count, 2, HD)
        own_window = window_start
    previous_key, previous_value = from_behind((key_rows, value_rows), "seq", 1)
    all_keys = jnp.concatenate([previous_key, key_rows], axis=0).reshape(
        2 * block_length, group_count, HD
    )
    all_values = jnp.concatenate([previous_value, value_rows], axis=0).reshape(
        2 * block_length, group_count, HD
    )
    key_index = (block_index - 1) * block_length + jnp.arange(2 * block_length, dtype=jnp.int32)
    query_index = (
        block_index * block_length + query_first + jnp.arange(query_count, dtype=jnp.int32)
    )
    allowed = (key_index[None, :] <= query_index[:, None]) & (
        key_index[None, :] >= own_window[:, None]
    )
    attended = attend(queries, all_keys, all_values, allowed)
    head_walsh = walsh_table(HD).astype(jnp.bfloat16)
    rotated = jnp.einsum(
        "qgtd,de->qgte", attended, head_walsh, preferred_element_type=jnp.float32
    ) * float(HD) ** (-0.5)
    rotated = rotated.astype(jnp.bfloat16).reshape(query_count, -1)
    if fused:
        return tail(
            rotated,
            residual,
            (attention_gain, feedforward_gain, output_gain),
            output_weight,
            gate_weight,
            up_weight,
            down_weight,
            WAL,
        )
    if paired:
        partner_rows = partner(output_weight, "mp", 0)
        full_output = join_pair(output_weight, partner_rows, low_bit, 0)
        half_term = jnp.dot(rotated, full_output, preferred_element_type=jnp.float32)
        padded = lax.dynamic_update_slice_in_dim(
            jnp.zeros((block_length, model_width), jnp.float32), half_term, query_first, 0
        )

        def attention_term(first_row, row_count):
            return lax.dynamic_slice_in_dim(padded, first_row, row_count, 0)

    else:

        def attention_term(first_row, row_count):
            picked = lax.dynamic_slice_in_dim(rotated, first_row, row_count, 0)
            return jnp.dot(picked, output_weight, preferred_element_type=jnp.float32)

    attention_rows = scatter_rows(attention_term(jnp.int32(0), lax.axis_size("mp") * own_rows))
    first_sum = (residual.astype(jnp.float32) + normalize(attention_rows, attention_gain)).astype(
        jnp.bfloat16
    )
    feed_own = normalize(first_sum, feedforward_gain).astype(jnp.bfloat16)
    feed_input = gather_rows(feed_own)
    local_count = WAL // model_count
    block_width = FF // WAL
    if own_rows % 16 == 0 and gate_weight.shape[1] % 384 == 0:
        gathered = hidden_rows(feed_input, gate_weight, up_weight)
        gathered = gathered.reshape(model_count, own_rows, local_count, block_width)
        exchanged = gathered.transpose(1, 0, 2, 3).reshape(own_rows, WAL, block_width)
    else:
        gate_out = jnp.dot(feed_input, gate_weight, preferred_element_type=jnp.float32)
        up_out = jnp.dot(feed_input, up_weight, preferred_element_type=jnp.float32)
        activated = (jax.nn.gelu(gate_out, approximate=True) * up_out).astype(jnp.bfloat16)
        grouped = activated.reshape(block_length, local_count, block_width)
        exchanged = lax.all_to_all(grouped, "mp", split_axis=0, concat_axis=1, tiled=True)
    walsh_scale = float(WAL) ** (-0.5)
    full_table = walsh_table(WAL).astype(jnp.bfloat16)
    mixed_rows = (
        jnp.einsum(
            "rab,ac->rcb",
            exchanged,
            full_table,
            preferred_element_type=jnp.float32,
        )
        * walsh_scale
    )
    spread = lax.all_to_all(
        mixed_rows.astype(jnp.bfloat16), "mp", split_axis=1, concat_axis=0, tiled=True
    )
    spread = spread.reshape(block_length, -1)
    picked = spread
    down_rows = scatter_rows(jnp.dot(picked, down_weight, preferred_element_type=jnp.float32))
    return (first_sum.astype(jnp.float32) + normalize(down_rows, output_gain)).astype(jnp.bfloat16)


def solution(mesh):
    placed = (
        P(("groups", "seq", "mp"), None),
        P(("groups", "seq")),
        P(("groups", "seq")),
        P(),
        P(),
        P(),
        P(),
        P(None, "mp"),
        P(None, "mp"),
        P(None, "mp"),
        P("mp", None),
        P(None, "mp"),
        P(None, "mp"),
        P("mp", None),
    )
    return jax.shard_map(
        body,
        mesh=mesh,
        in_specs=placed,
        out_specs=P(("groups", "seq", "mp"), None),
        check_vma=False,
    )
```

```python
import functools

import jax
import jax.numpy as jnp
from jax import lax
from jax.experimental import pallas as pl
from jax.experimental.pallas import tpu as pltpu
from jax.sharding import PartitionSpec as P

D = 5376
FF = 21504
QH = 32
HD = 128
WAL = 64


epsilon = 1e-06


MESH = pl.DeviceIdType.MESH


def block_of(ref, index, rows):
    return ref.at[pl.ds(pl.multiple_of(index * rows, rows), rows)]


def send(source, target, send_sem, recv_sem, device):
    return pltpu.make_async_remote_copy(
        src_ref=source,
        dst_ref=target,
        send_sem=send_sem,
        recv_sem=recv_sem,
        device_id={"mp": device},
        device_id_type=MESH,
    )


def place(count):
    me = lax.axis_index("mp")
    column = lax.rem(me, 2)
    line = lax.div(me, 2)
    return me, column, line, count // 2, me + 1 - 2 * column


def greet(me, line, lines, peer):
    barrier = pltpu.get_barrier_semaphore()
    pl.semaphore_signal(barrier, inc=1, device_id={"mp": peer}, device_id_type=MESH)

    @pl.when(line > 0)
    def _():
        pl.semaphore_signal(barrier, inc=1, device_id={"mp": me - 2}, device_id_type=MESH)

    @pl.when(line < lines - 1)
    def _():
        pl.semaphore_signal(barrier, inc=1, device_id={"mp": me + 2}, device_id_type=MESH)

    beside = jnp.minimum(line, 1) + jnp.minimum(lines - 1 - line, 1)
    pl.semaphore_wait(barrier, 1 + beside)


def gather_kernel(count, own_ref, all_ref, xs, xr, us, ur, ds, dr):
    rows = own_ref.shape[0]
    me, column, line, lines, peer = place(count)
    greet(me, line, lines, peer)

    def across(origin, source):
        there = block_of(all_ref, origin * 2 + column, rows)
        return send(source, there, xs.at[origin], xr.at[origin], peer)

    def upward(origin, source):
        there = block_of(all_ref, origin * 2 + column, rows)
        return send(source, there, us.at[origin], ur.at[origin], me + 2)

    def downward(origin, source):
        there = block_of(all_ref, origin * 2 + column, rows)
        return send(source, there, ds.at[origin], dr.at[origin], me - 2)

    @pl.when(line < lines - 1)
    def _():
        upward(line, own_ref).start()

    @pl.when(line > 0)
    def _():
        downward(line, own_ref).start()

    across(line, own_ref).start()
    all_ref[pl.ds(pl.multiple_of(me * rows, rows), rows), :] = own_ref[...]
    for step in range(1, lines):

        @pl.when(line - step >= 0)
        def _():
            origin = line - step
            held = block_of(all_ref, origin * 2 + column, rows)
            upward(origin, held).wait_recv()

            @pl.when(line < lines - 1)
            def _():
                upward(origin, held).start()

            across(origin, held).start()

        @pl.when(line + step < lines)
        def _():
            origin = line + step
            held = block_of(all_ref, origin * 2 + column, rows)
            downward(origin, held).wait_recv()

            @pl.when(line > 0)
            def _():
                downward(origin, held).start()

            across(origin, held).start()

    for origin in range(lines):
        across(origin, own_ref).wait_send()
        there = block_of(all_ref, origin * 2 + 1 - column, rows)
        send(own_ref, there, xs.at[origin], xr.at[origin], peer).wait_recv()

        @pl.when((origin <= line) & (line < lines - 1))
        def _():
            upward(origin, own_ref).wait_send()

        @pl.when((origin >= line) & (line > 0))
        def _():
            downward(origin, own_ref).wait_send()


def gather_rows(own):
    count = lax.axis_size("mp")
    rows, width = own.shape
    if rows % 16 or count % 2 or count < 4:
        return lax.all_gather(own, "mp", axis=0, tiled=True)
    lines = count // 2
    return pl.pallas_call(
        functools.partial(gather_kernel, count),
        out_shape=jax.ShapeDtypeStruct((count * rows, width), own.dtype),
        in_specs=[pl.BlockSpec(memory_space=pltpu.VMEM)],
        out_specs=pl.BlockSpec(memory_space=pltpu.VMEM),
        scratch_shapes=[pltpu.SemaphoreType.DMA((lines,))] * 6,
        compiler_params=pltpu.CompilerParams(
            collective_id=0, has_side_effects=True, vmem_limit_bytes=16 * 1024 * 1024
        ),
    )(own)


def scatter_kernel(count, term_ref, sum_ref, xb, ub, db, sb, xs, xr, us, ur, ds, dr):
    rows, width = sum_ref.shape
    me, column, line, lines, peer = place(count)
    step_width = 768 if width % 768 == 0 else 128
    greet(me, line, lines, peer)

    def across(dest):
        mine = block_of(term_ref, dest * 2 + 1 - column, rows)
        return send(mine, xb.at[dest], xs.at[dest], xr.at[dest], peer)

    def upward(dest):
        return send(sb.at[dest], ub.at[dest], us.at[dest], ur.at[dest], me + 2)

    def downward(dest):
        return send(sb.at[dest], db.at[dest], ds.at[dest], dr.at[dest], me - 2)

    for away in range(lines - 1, -1, -1):

        @pl.when(line - away >= 0)
        def _():
            across(line - away).start()

        if away:

            @pl.when(line + away < lines)
            def _():
                across(line + away).start()

    def add(dest, arrived, target, index):
        first = pl.multiple_of((dest * 2 + column) * rows, rows)

        def some(i, carry):
            cols = pl.ds(pl.multiple_of(i * step_width, step_width), step_width)
            total = term_ref[pl.ds(first, rows), cols].astype(jnp.float32)
            total = total + xb[dest, :, cols].astype(jnp.float32)
            for ref in arrived:
                total = total + ref[dest, :, cols].astype(jnp.float32)
            if index:
                target[dest, :, cols] = total.astype(target.dtype)
            else:
                target[:, cols] = total
            return carry

        lax.fori_loop(0, width // step_width, some, 0)

    def go_up(dest):
        @pl.when(dest > line)
        def _():
            across(dest).wait_recv()

            @pl.when(line > 0)
            def _():
                upward(dest).wait_recv()
                add(dest, (ub,), sb, True)

            @pl.when(line == 0)
            def _():
                add(dest, (), sb, True)

            upward(dest).start()

    def go_down(dest):
        @pl.when(dest < line)
        def _():
            across(dest).wait_recv()

            @pl.when(line < lines - 1)
            def _():
                downward(dest).wait_recv()
                add(dest, (db,), sb, True)

            @pl.when(line == lines - 1)
            def _():
                add(dest, (), sb, True)

            downward(dest).start()

    for j in range(lines - 1):

        @pl.when(2 * line < lines)
        def _():
            go_up(lines - 1 - j)
            go_down(j)

        @pl.when(2 * line >= lines)
        def _():
            go_down(j)
            go_up(lines - 1 - j)

    across(line).wait_recv()

    @pl.when(line > 0)
    def _():
        upward(line).wait_recv()

    @pl.when(line < lines - 1)
    def _():
        downward(line).wait_recv()

    @pl.when((line > 0) & (line < lines - 1))
    def _():
        add(line, (ub, db), sum_ref, False)

    @pl.when(line == 0)
    def _():
        add(line, (db,), sum_ref, False)

    @pl.when(line == lines - 1)
    def _():
        add(line, (ub,), sum_ref, False)

    for dest in range(lines):
        across(dest).wait_send()

        @pl.when(dest > line)
        def _():
            upward(dest).wait_send()

        @pl.when(dest < line)
        def _():
            downward(dest).wait_send()


def scatter_rows(term):
    count = lax.axis_size("mp")
    rows, width = term.shape[0] // count, term.shape[1]
    if rows % 16 or count % 2 or count < 4:
        return lax.psum_scatter(term, "mp", scatter_dimension=0, tiled=True)
    lines = count // 2
    blocks = pltpu.VMEM((lines, rows, width), jnp.bfloat16)
    return pl.pallas_call(
        functools.partial(scatter_kernel, count),
        out_shape=jax.ShapeDtypeStruct((rows, width), jnp.float32),
        in_specs=[pl.BlockSpec(memory_space=pltpu.VMEM)],
        out_specs=pl.BlockSpec(memory_space=pltpu.VMEM),
        scratch_shapes=[blocks] * 4 + [pltpu.SemaphoreType.DMA((lines,))] * 6,
        compiler_params=pltpu.CompilerParams(
            collective_id=1, has_side_effects=True, vmem_limit_bytes=24 * 1024 * 1024
        ),
    )(term.astype(jnp.bfloat16))


def hidden_kernel(count, tiles, feed_ref, gate_ref, up_ref, out_ref, act, got, ss, rs):
    rows = feed_ref.shape[0] // count
    width = gate_ref.shape[1]
    tile = pl.program_id(0)
    me = lax.axis_index("mp")

    @pl.when(tile == 0)
    def _():
        barrier = pltpu.get_barrier_semaphore()
        for k in range(1, count):
            other = lax.rem(me + k, count)
            pl.semaphore_signal(barrier, inc=1, device_id={"mp": other}, device_id_type=MESH)
        pl.semaphore_wait(barrier, count - 1)

    feed = feed_ref[...]
    gate_out = jnp.dot(feed, gate_ref[...], preferred_element_type=jnp.float32)
    up_out = jnp.dot(feed, up_ref[...], preferred_element_type=jnp.float32)
    act[tile] = (jax.nn.gelu(gate_out, approximate=True) * up_out).astype(jnp.bfloat16)

    def to(k, t):
        other = lax.rem(me + k, count)
        source = act.at[t, pl.ds(pl.multiple_of(other * rows, rows), rows), :]
        target = got.at[t, pl.ds(pl.multiple_of(me * rows, rows), rows), :]
        return send(source, target, ss.at[k, t], rs.at[k, t], other)

    for k in range(1, count):
        to(k, tile).start()
    own = pl.ds(pl.multiple_of(me * rows, rows), rows)
    got[tile, own, :] = act[tile, own, :]

    @pl.when(tile == tiles - 1)
    def _():
        for t in range(tiles):
            for k in range(1, count):
                to(k, t).wait_recv()
            out_ref[:, t * width : (t + 1) * width] = got[t]
        for t in range(tiles):
            for k in range(1, count):
                to(k, t).wait_send()


def hidden_rows(feed, gate_weight, up_weight):
    count = lax.axis_size("mp")
    length, depth = feed.shape
    hidden = gate_weight.shape[1]
    rows, tile = length // count, 384
    tiles = hidden // tile
    weights = pl.BlockSpec((depth, tile), lambda t: (0, t))
    return pl.pallas_call(
        functools.partial(hidden_kernel, count, tiles),
        grid=(tiles,),
        out_shape=jax.ShapeDtypeStruct((length, hidden), jnp.bfloat16),
        in_specs=[pl.BlockSpec((length, depth), lambda t: (0, 0)), weights, weights],
        out_specs=pl.BlockSpec((length, hidden), lambda t: (0, 0)),
        scratch_shapes=[
            pltpu.VMEM((tiles, length, tile), jnp.bfloat16),
            pltpu.VMEM((tiles, length, tile), jnp.bfloat16),
            pltpu.SemaphoreType.DMA((count, tiles)),
            pltpu.SemaphoreType.DMA((count, tiles)),
        ],
        compiler_params=pltpu.CompilerParams(
            collective_id=2,
            has_side_effects=True,
            dimension_semantics=("arbitrary",),
            vmem_limit_bytes=48 * 1024 * 1024,
        ),
    )(feed, gate_weight, up_weight)


PART = 256
STRIPE = 3 * PART
CYCLE = 7
LAG = 3
SLOTS = 5


def is_paired(c):
    return lax.rem(c, CYCLE) == CYCLE // 2


def signal_to(device):
    barrier = pltpu.get_barrier_semaphore()
    pl.semaphore_signal(barrier, inc=1, device_id={"mp": device}, device_id_type=MESH)


def row_scale(read, parts, width):
    def some(c, total):
        values = read(c)
        return total + jnp.sum(values * values, axis=-1, keepdims=True)

    first = read(0)
    total = lax.fori_loop(1, parts, some, jnp.sum(first * first, axis=-1, keepdims=True))
    return lax.rsqrt(total / width + epsilon)


def columns_of(c, width):
    return pl.ds(pl.multiple_of(c * width, width), width)


def wait_for(ref, sem, device):
    send(ref, ref, sem, sem, device).wait_recv()


def wait_sent(ref, sem, device):
    send(ref, ref, sem, sem, device).wait_send()


class Gather:
    def __init__(self, count, rows, buf, sems):
        self.buf, self.rows = buf, rows
        self.xs, self.ps, self.us, self.ds, self.xr, self.zr = sems
        self.parts = buf.shape[0]
        self.me, self.column, self.line, self.lines, self.peer = place(count)

    def block(self, c, origin, column):
        first, rows = origin * 2, self.rows
        if column is None:
            rows = 2 * rows
        else:
            first = first + column
        first = pl.multiple_of(first * self.rows, rows)
        return self.buf.at[c, pl.ds(first, rows), :]

    def across(self, c, origin, sem):
        there = self.block(c, origin, self.column)
        return send(there, there, sem.at[0], self.xr.at[c], self.peer)

    def upward(self, c, origin, both):
        there = self.block(c, origin, None if both else self.column)
        return send(there, there, self.us.at[0], self.zr.at[c, origin], self.me + 2)

    def downward(self, c, origin, both):
        there = self.block(c, origin, None if both else self.column)
        return send(there, there, self.ds.at[0], self.zr.at[c, origin], self.me - 2)

    def valid(self, c):
        return (c >= 0) & (c < self.parts)

    def both_ways(self, c, both):
        @pl.when(self.line < self.lines - 1)
        def _():
            self.upward(c, self.line, both).start()

        @pl.when(self.line > 0)
        def _():
            self.downward(c, self.line, both).start()

    def relay(self, c, away, both):
        line, lines = self.line, self.lines

        @pl.when(line - away >= 0)
        def _():
            self.upward(c, line - away, both).wait_recv()

            @pl.when(line < lines - 1)
            def _():
                self.upward(c, line - away, both).start()

            if not both:
                self.across(c, line - away, self.xs).start()

        @pl.when(line + away < lines)
        def _():
            self.downward(c, line + away, both).wait_recv()

            @pl.when(line > 0)
            def _():
                self.downward(c, line + away, both).start()

            if not both:
                self.across(c, line + away, self.xs).start()

    def step(self, t):
        line, lines = self.line, self.lines

        @pl.when((t < self.parts) & jnp.logical_not(is_paired(t)))
        def _():
            self.both_ways(t, False)
            self.across(t, line, self.xs).start()

        @pl.when((t < self.parts) & is_paired(t))
        def _():
            self.across(t, line, self.ps).start()

        c = t - LAG

        @pl.when(self.valid(c) & is_paired(c))
        def _():
            wait_for(self.block(c, line, 1 - self.column), self.xr.at[c], self.peer)
            self.both_ways(c, True)

        for away in range(1, lines):
            c = t - away * LAG

            @pl.when(self.valid(c) & jnp.logical_not(is_paired(c)))
            def _():
                self.relay(c, away, False)

            late = c - LAG

            @pl.when(self.valid(late) & is_paired(late))
            def _():
                self.relay(late, away, True)

    def arrived(self, c):
        @pl.when(jnp.logical_not(is_paired(c)))
        def _():
            wait_for(self.buf.at[c, 0 : self.lines * self.rows, :], self.xr.at[c], self.peer)

    def finish(self):
        line, lines, parts = self.line, self.lines, self.parts
        pairs = parts // CYCLE
        share = (parts + pairs) * self.rows // self.buf.shape[1]
        half = lines * self.rows
        wait_sent(self.buf.at[0 : parts - pairs, 0:half, :], self.xs.at[0], self.peer)
        wait_sent(self.buf.at[0:pairs, 0 : self.rows, :], self.ps.at[0], self.peer)
        for at in range(lines):

            @pl.when(line == at)
            def _():
                if at < lines - 1:
                    wait_sent(self.buf.at[0 : share * (at + 1)], self.us.at[0], self.peer)
                if at > 0:
                    wait_sent(self.buf.at[0 : share * (lines - at)], self.ds.at[0], self.peer)


class Scatter:
    def __init__(self, count, rows, term, xb, ub, db, sb, up, dp, sp, sums, sems):
        self.term, self.xb, self.ub, self.db, self.sb, self.sums = term, xb, ub, db, sb, sums
        self.up, self.dp, self.sp = up, dp, sp
        self.rows = rows
        self.xs, self.ps, self.us, self.ds, self.xr, self.ur, self.dr = sems
        self.parts = term.shape[0]
        self.me, self.column, self.line, self.lines, self.peer = place(count)

    def mine(self, dest, column):
        return pl.ds(pl.multiple_of((dest * 2 + column) * self.rows, self.rows), self.rows)

    def across(self, c, dest):
        source = self.term.at[c, self.mine(dest, 1 - self.column), :]
        return send(source, self.xb.at[c, dest], self.xs.at[0], self.xr.at[c], self.peer)

    def across_total(self, c):
        there, source = self.xb.at[c, self.line], self.sb.at[c, self.line]
        return send(source, there, self.ps.at[0], self.xr.at[c], self.peer)

    def slot(self, c, both):
        return lax.div(c, CYCLE) if both else c

    def upward(self, c, dest, both):
        at = self.slot(c, both)
        source, there = (self.sp, self.up) if both else (self.sb, self.ub)
        return send(
            source.at[at, dest], there.at[at, dest], self.us.at[0], self.ur.at[c], self.me + 2
        )

    def downward(self, c, dest, both):
        at = self.slot(c, both)
        source, there = (self.sp, self.dp) if both else (self.sb, self.db)
        return send(
            source.at[at, dest], there.at[at, dest], self.ds.at[0], self.dr.at[c], self.me - 2
        )

    def total(self, c, dest, arrived, both):
        if both:
            here = pl.ds(pl.multiple_of(dest * 2 * self.rows, 2 * self.rows), 2 * self.rows)
            total = self.term[c, here, :].astype(jnp.float32)
        else:
            total = self.term[c, self.mine(dest, self.column), :].astype(jnp.float32)
            total = total + self.xb[c, dest].astype(jnp.float32)
        for ref in arrived:
            total = total + ref[self.slot(c, both), dest].astype(jnp.float32)
        return total

    def pass_up(self, c, both):
        line, lines = self.line, self.lines
        ub = self.up if both else self.ub
        to = self.sp if both else self.sb
        at = self.slot(c, both)
        for here in range(lines):

            @pl.when(line == here)
            def _():
                if here:
                    wait_for(ub.at[at, here:lines], self.ur.at[c], self.peer)
                for dest in range(lines - 1, here, -1):
                    total = self.total(c, dest, (ub,) if here else (), both)
                    to[at, dest] = total.astype(to.dtype)
                    self.upward(c, dest, both).start()

    def pass_down(self, c, both):
        line, lines = self.line, self.lines
        db = self.dp if both else self.db
        to = self.sp if both else self.sb
        at = self.slot(c, both)
        for here in range(lines):

            @pl.when(line == here)
            def _():
                last = here == lines - 1
                if not last:
                    wait_for(db.at[at, 0 : here + 1], self.dr.at[c], self.peer)
                for dest in range(here):
                    total = self.total(c, dest, () if last else (db,), both)
                    to[at, dest] = total.astype(to.dtype)
                    self.downward(c, dest, both).start()

    def settle(self, c, both):
        line, lines = self.line, self.lines
        ub, db = (self.up, self.dp) if both else (self.ub, self.db)

        def store(arrived):
            total = self.total(c, line, arrived, both)
            if not both:
                self.sums[c] = total
                return
            own, other = total[: self.rows], total[self.rows :]

            @pl.when(self.column == 0)
            def _():
                self.sums[c] = own
                self.sb[c, line] = other.astype(self.sb.dtype)

            @pl.when(self.column == 1)
            def _():
                self.sums[c] = other
                self.sb[c, line] = own.astype(self.sb.dtype)

        @pl.when(line == 0)
        def _():
            store((db,))

        @pl.when(line == lines - 1)
        def _():
            store((ub,))

        @pl.when((line > 0) & (line < lines - 1))
        def _():
            store((ub, db))

        if both:
            self.across_total(c).start()

    def run(self, produce):
        line, lines, parts = self.line, self.lines, self.parts

        def valid(c, both):
            paired = is_paired(c)
            return (c >= 0) & (c < parts) & (paired if both else jnp.logical_not(paired))

        def step(t, carry):
            @pl.when((t < parts) & (lax.rem(t, STRIPE // PART) == 0))
            def _():
                produce(lax.div(t, STRIPE // PART))

            @pl.when(valid(t, False))
            def _():
                for away in range(lines - 1, -1, -1):

                    @pl.when(line - away >= 0)
                    def _():
                        self.across(t, line - away).start()

                    if away:

                        @pl.when(line + away < lines)
                        def _():
                            self.across(t, line + away).start()

            first = t - LAG

            @pl.when(valid(first, False))
            def _():
                wait_for(self.xb.at[first], self.xr.at[first], self.peer)

            cu, cd, c = t - LAG * (1 + line), t - LAG * (lines - line), t - LAG * lines
            for both in (False, True):

                @pl.when(valid(cu, both))
                def _():
                    self.pass_up(cu, both)

                @pl.when(valid(cd, both))
                def _():
                    self.pass_down(cd, both)

                @pl.when(valid(c, both))
                def _():
                    self.settle(c, both)

            late = c - LAG

            @pl.when(valid(late, True))
            def _():
                wait_for(self.xb.at[late, line], self.xr.at[late], self.peer)
                self.sums[late] += self.xb[late, line].astype(jnp.float32)

            return carry

        lax.fori_loop(0, parts + LAG * (lines + 1), step, 0)
        pairs = parts // CYCLE
        share = (parts + pairs) * self.rows // self.term.shape[1]
        half = lines * self.rows
        wait_sent(self.term.at[0 : parts - pairs, 0:half, :], self.xs.at[0], self.peer)
        wait_sent(self.xb.at[0:pairs, 0], self.ps.at[0], self.peer)
        for at in range(lines):

            @pl.when(line == at)
            def _():
                if at < lines - 1:
                    wait_sent(self.term.at[0 : share * (lines - 1 - at)], self.us.at[0], self.peer)
                if at > 0:
                    wait_sent(self.term.at[0 : share * at], self.ds.at[0], self.peer)


def butterfly(values):
    values = list(values)
    apart = 1
    while apart < len(values):
        for low in range(len(values)):
            if low // apart % 2 == 0:
                a, b = values[low], values[low + apart]
                values[low], values[low + apart] = a + b, a - b
        apart *= 2
    return values


def layer_kernel(
    count, blocks, head, scale, resid, tables, in_gain, att_gain, feed_gain, out_gain,
    wq, wk, wv, wo, wg, wu, wd, out_ref,
    rot, pairs_own, pairs_all, term, xb, ub, db, sb, up, dp, sp, sums, first, feed, gu, acc,
    act, got, mixed, spread, spun, dbuf,
    w_sem, wo_sem, gu_sem, d_sem, kv_sem, a_send, a_recv, b_send, b_recv, *sems,
):
    rows, width = resid.shape
    parts, length, part = term.shape
    hidden = wg.shape[1]
    slots, d_slots = gu.shape[0], dbuf.shape[0]
    halves = rows // 16
    local = blocks // count
    inner = hidden // local
    stripes = width // STRIPE
    scatter = Scatter(count, rows, term, xb, ub, db, sb, up, dp, sp, sums, sems[:7])
    gather = Gather(count, rows, feed, sems[7:])
    me, lines, peer = scatter.me, scatter.lines, scatter.peer
    seq = lax.axis_index("seq")
    spans = ((wq, 0), (wk, wq.shape[1]), (wv, wq.shape[1] + wk.shape[1]))
    joint = wq.shape[1] + wk.shape[1] + wv.shape[1]
    held = gu.shape[2] // joint

    def joint_columns(c):
        return pl.ds(pl.multiple_of(lax.rem(c, held) * joint, 128), joint)

    def load_joint(c, carry):
        slot, start = lax.div(c, held), lax.rem(c, held) * joint
        for source, at in spans:
            target = gu.at[slot, :, pl.ds(pl.multiple_of(start + at, 128), source.shape[1])]
            copy = source.at[columns_of(c, part), :]
            pltpu.make_async_copy(copy, target, w_sem.at[c]).start()
        return carry

    deep = wo.shape[0]
    layers = hidden // deep

    def wo_part(c):
        first = pl.multiple_of(lax.rem(c, layers) * deep, deep)
        return dbuf.at[lax.div(c, layers), pl.ds(first, deep), :]

    def load_wo(c):
        return pltpu.make_async_copy(wo.at[:, columns_of(c, STRIPE)], wo_part(c), wo_sem.at[c])

    def load_gu(c):
        slot = lax.rem(c, slots)
        for i, source in enumerate((wg, wu)):
            target = gu.at[slot, :, i * hidden : (i + 1) * hidden]
            copy = source.at[columns_of(c, part), :]
            pltpu.make_async_copy(copy, target, gu_sem.at[slot]).start()

    def load_d(c):
        slot = lax.rem(c, d_slots)
        return pltpu.make_async_copy(wd.at[:, columns_of(c, STRIPE)], dbuf.at[slot], d_sem.at[slot])

    for k in range(1, count):
        signal_to(lax.rem(me + k, count))
    barrier = pltpu.get_barrier_semaphore()
    pl.semaphore_signal(barrier, inc=1, device_id={"seq": 1 - seq}, device_id_type=MESH)
    lax.fori_loop(0, parts, load_joint, 0)

    own = pl.ds(pl.multiple_of(me * rows, rows), rows)

    def read(c):
        return resid[:, columns_of(c, part)].astype(jnp.float32)

    in_scale = row_scale(read, parts, width)

    def place_input(c, carry):
        normed = read(c) * in_scale * in_gain[columns_of(c, part)]
        feed[c, own, :] = normed.astype(feed.dtype)
        return carry

    lax.fori_loop(0, parts, place_input, 0)
    pl.semaphore_wait(barrier, count)

    def project_step(t, carry):
        gather.step(t)
        c = t - LAG * lines

        @pl.when(t == 0)
        def _():
            acc[:, 0:joint] = jnp.zeros((length, joint), jnp.float32)

        @pl.when(c >= 0)
        def _():
            weight = gu.at[lax.div(c, held), :, joint_columns(c)]
            pltpu.make_async_copy(weight, weight, w_sem.at[c]).wait()
            gather.arrived(c)
            acc[:, 0:joint] += jnp.dot(feed[c], weight[...], preferred_element_type=jnp.float32)

        return carry

    lax.fori_loop(0, parts + LAG * lines, project_step, 0)
    gather.finish()
    for c in range(slots):
        load_gu(c)
    for c in range(stripes):
        load_wo(c).start()

    def head_rows(first, n):
        at = first + n * head
        return acc[:, at : at + head].astype(jnp.bfloat16).astype(jnp.float32)

    def rope(value):
        return value * tables[0] + pltpu.roll(value, head // 2, 1) * tables[1]

    groups = wk.shape[1] // head
    for g in range(groups):
        lanes = slice(g * head, (g + 1) * head)
        pairs_own[0, :, lanes] = rope(head_rows(spans[1][1], g)).astype(pairs_own.dtype)
        pairs_own[1, :, lanes] = head_rows(spans[2][1], g).astype(pairs_own.dtype)

    there = pairs_all.at[:, 0:length, :]
    exchange = pltpu.make_async_remote_copy(
        src_ref=pairs_own,
        dst_ref=there,
        send_sem=kv_sem.at[0],
        recv_sem=kv_sem.at[1],
        device_id={"seq": 1 - seq},
        device_id_type=MESH,
    )

    @pl.when(seq == 0)
    def _():
        exchange.start()
        pairs_all[:, 0:length, :] = jnp.zeros((2, length, groups * head), pairs_all.dtype)

    pairs_all[:, length : 2 * length, :] = pairs_own[...]
    query = lax.broadcasted_iota(jnp.int32, (length, 2 * length), 0) + seq * length
    key = lax.broadcasted_iota(jnp.int32, (length, 2 * length), 1) + (seq - 1) * length
    allowed = (key <= query) & (key.astype(jnp.float32) >= tables[2, :, 0:1])
    table = walsh_table(head).astype(jnp.bfloat16)

    @pl.when(seq == 1)
    def _():
        exchange.wait_recv()

    for n in range(wq.shape[1] // head):
        lanes = slice(n // 2 * head, (n // 2 + 1) * head)
        queries = (rope(head_rows(0, n)) * scale).astype(jnp.bfloat16)
        scores = lax.dot_general(
            queries,
            pairs_all[0, :, lanes],
            (((1,), (1,)), ((), ())),
            preferred_element_type=jnp.float32,
        )
        scores = jnp.where(allowed, scores, -1e30)
        exponent = jnp.exp(scores - jnp.max(scores, axis=-1, keepdims=True))
        probabilities = exponent / jnp.sum(exponent, axis=-1, keepdims=True)
        attended = jnp.dot(
            probabilities.astype(jnp.bfloat16),
            pairs_all[1, :, lanes],
            preferred_element_type=jnp.float32,
        )
        rotated = jnp.dot(
            attended.astype(jnp.bfloat16), table, preferred_element_type=jnp.float32
        )
        rotated = rotated * float(head) ** (-0.5)
        rot[:, n * head : (n + 1) * head] = rotated.astype(rot.dtype)

    @pl.when(seq == 0)
    def _():
        exchange.wait_send()

    tile = 384

    def put_stripe(c, value):
        for i in range(STRIPE // part):
            piece = value[:, i * part : (i + 1) * part]
            term[c * (STRIPE // part) + i] = piece.astype(term.dtype)

    def attention_part(c):
        load_wo(c).wait()
        weight = wo_part(c)[...]
        put_stripe(c, jnp.dot(rot[...], weight, preferred_element_type=jnp.float32))

        @pl.when(c == stripes - 1)
        def _():
            for c in range(d_slots):
                load_d(c).start()

    scatter.run(attention_part)

    att_scale = row_scale(lambda c: sums[c], parts, width)

    def add_residual(c, carry):
        cols = columns_of(c, part)
        value = sums[c] * att_scale * att_gain[cols]
        value = resid[:, cols].astype(jnp.float32) + value
        first[c] = value.astype(first.dtype)
        return carry

    lax.fori_loop(0, parts, add_residual, 0)
    feed_scale = row_scale(lambda c: first[c].astype(jnp.float32), parts, width)

    def place_own(c, carry):
        value = first[c].astype(jnp.float32) * feed_scale * feed_gain[columns_of(c, part)]
        feed[c, own, :] = value.astype(feed.dtype)
        return carry

    lax.fori_loop(0, parts, place_own, 0)

    def feed_step(t, carry):
        gather.step(t)
        c = t - LAG * lines

        @pl.when(t == 0)
        def _():
            acc[...] = jnp.zeros_like(acc)

        @pl.when(c >= 0)
        def _():
            slot = lax.rem(c, slots)
            pltpu.make_async_copy(gu.at[slot], gu.at[slot], gu_sem.at[slot]).wait()
            gather.arrived(c)
            acc[...] += jnp.dot(feed[c], gu[slot], preferred_element_type=jnp.float32)

            @pl.when(c + slots < parts)
            def _():
                load_gu(c + slots)

        return carry

    lax.fori_loop(0, parts + LAG * lines, feed_step, 0)

    def half_rows(device, h):
        return pl.ds(pl.multiple_of(device * rows + h * 16, 16), 16)

    def to_mixer(h, k):
        other = lax.rem(me + k, count)
        source, there = act.at[half_rows(other, h), :], got.at[me, pl.ds(h * 16, 16), :]
        return send(source, there, a_send.at[h], a_recv.at[h], other)

    def from_mixer(h, k):
        other = lax.rem(me + k, count)
        source, there = spread.at[other, pl.ds(h * 16, 16), :], spun.at[half_rows(me, h), :]
        return send(source, there, b_send.at[h], b_recv.at[h], other)

    others = got.at[0 : count - 1, 0:16, :]
    for h in range(halves):

        def activate(k, carry):
            here = half_rows(lax.rem(me + k, count), h)

            def some(n, carry):
                cols = columns_of(n, tile)
                beside = pl.ds(pl.multiple_of(hidden + n * tile, 128), tile)
                value = jax.nn.gelu(acc[here, cols], approximate=True) * acc[here, beside]
                act[here, cols] = value.astype(act.dtype)
                return carry

            lax.fori_loop(0, hidden // tile, some, 0)

            @pl.when(k < count)
            def _():
                to_mixer(h, k).start()

            return carry

        lax.fori_loop(1, count + 1, activate, 0)
        got[me, h * 16 : h * 16 + 16, :] = act[half_rows(me, h), :]

    for h in range(halves):
        wait_for(others, a_recv.at[h], peer)

        def over_devices(n, carry):
            cols = columns_of(n, tile)
            held = [got[d, h * 16 : h * 16 + 16, cols].astype(jnp.float32) for d in range(count)]
            for d, value in enumerate(butterfly(held)):
                mixed[d, :, cols] = value
            return carry

        lax.fori_loop(0, hidden // tile, over_devices, 0)

        def within(k, carry):
            other = lax.rem(me + k, count)
            value = mixed[other]
            pieces = [value[:, a * inner : (a + 1) * inner] for a in range(local)]
            whole = jnp.concatenate(butterfly(pieces), axis=1) * float(blocks) ** (-0.5)
            spread[other, h * 16 : h * 16 + 16, :] = whole.astype(spread.dtype)

            @pl.when(k < count)
            def _():
                from_mixer(h, k).start()

            return carry

        lax.fori_loop(1, count + 1, within, 0)
        spun[half_rows(me, h), :] = spread[me, h * 16 : h * 16 + 16, :]

    for h in range(halves):
        wait_for(others, b_recv.at[h], peer)

    def down_part(c):
        load_d(c).wait()
        slot = lax.rem(c, d_slots)
        put_stripe(c, jnp.dot(spun[...], dbuf[slot], preferred_element_type=jnp.float32))

        @pl.when(c + d_slots < stripes)
        def _():
            load_d(c + d_slots).start()

    scatter.run(down_part)

    out_scale = row_scale(lambda c: sums[c], parts, width)

    def finish(c, carry):
        cols = columns_of(c, part)
        value = first[c].astype(jnp.float32) + sums[c] * out_scale * out_gain[cols]
        out_ref[:, cols] = value.astype(out_ref.dtype)
        return carry

    lax.fori_loop(0, parts, finish, 0)
    gather.finish()
    for h in range(halves):
        wait_sent(others, a_send.at[h], peer)
        wait_sent(others, b_send.at[h], peer)


def fused_layer(residual, tables, gains, weights, blocks, head, scale):
    count = lax.axis_size("mp")
    rows, width = residual.shape
    part = PART
    parts, lines, length = width // part, count // 2, count * rows
    query_weight, key_weight, _, _, gate_weight, _, _ = weights
    hidden, kept = gate_weight.shape[1], key_weight.shape[1]
    slots, d_slots, halves = SLOTS, 2, rows // 16
    vmem = pl.BlockSpec(memory_space=pltpu.VMEM)
    hbm = pl.BlockSpec(memory_space=pltpu.HBM)
    bf16, f32 = jnp.bfloat16, jnp.float32
    block = pltpu.VMEM((parts, lines, rows, part), bf16)
    paired = pltpu.VMEM((parts // CYCLE, lines, 2 * rows, part), bf16)
    dma = pltpu.SemaphoreType.DMA
    return pl.pallas_call(
        functools.partial(layer_kernel, count, blocks, head, scale),
        out_shape=jax.ShapeDtypeStruct((rows, width), residual.dtype),
        in_specs=[vmem] * 6 + [hbm] * 7,
        out_specs=vmem,
        scratch_shapes=[
            pltpu.VMEM((length, query_weight.shape[1]), bf16),
            pltpu.VMEM((2, length, kept), bf16),
            pltpu.VMEM((2, 2 * length, kept), bf16),
            pltpu.VMEM((parts, length, part), bf16),
            block,
            block,
            block,
            block,
            paired,
            paired,
            paired,
            pltpu.VMEM((parts, rows, part), f32),
            pltpu.VMEM((parts, rows, part), bf16),
            pltpu.VMEM((parts, length, part), bf16),
            pltpu.VMEM((slots, part, 2 * hidden), bf16),
            pltpu.VMEM((length, 2 * hidden), f32),
            pltpu.VMEM((length, hidden), bf16),
            pltpu.VMEM((count, rows, hidden), bf16),
            pltpu.VMEM((count, 16, hidden), f32),
            pltpu.VMEM((count, rows, hidden), bf16),
            pltpu.VMEM((length, hidden), bf16),
            pltpu.VMEM((d_slots, hidden, STRIPE), bf16),
            dma((parts,)),
            dma((width // STRIPE,)),
            dma((slots,)),
            dma((d_slots,)),
            dma((2,)),
        ]
        + [dma((halves,))] * 4
        + [dma((1,))] * 4
        + [dma((parts,))] * 3
        + [dma((1,))] * 4
        + [dma((parts,)), dma((parts, lines))],
        compiler_params=pltpu.CompilerParams(
            collective_id=4, has_side_effects=True, vmem_limit_bytes=56 * 1024 * 1024
        ),
    )(residual, tables, *gains, *weights)


def partner(block, axis, apart):
    count = lax.axis_size(axis)
    route = []
    for low in range(count):
        high = low | 1 << apart
        if high != low and high < count:
            route += [(low, high), (high, low)]
    return lax.ppermute(block, axis, route)


def for_sending(value):
    return jax.tree.map(lambda a: a.astype(jnp.bfloat16) if a.dtype == jnp.float32 else a, value)


def from_behind(block, axis, distance):
    devices = range(lax.axis_size(axis))
    route = [(i - distance, i) for i in devices if i - distance in devices]
    return lax.ppermute(block, axis, route)


def normalize(values_in, gain_row):
    widened = values_in.astype(jnp.float32)
    mean_square = jnp.mean(widened * widened, axis=-1, keepdims=True)
    return widened * lax.rsqrt(mean_square + epsilon) * gain_row


def walsh_table(length):
    row_index = lax.broadcasted_iota(jnp.int32, (length, length), 0)
    column_index = lax.broadcasted_iota(jnp.int32, (length, length), 1)
    common = jnp.bitwise_and(row_index, column_index)
    parity = jnp.zeros((length, length), jnp.int32)
    for offset in range(max(length.bit_length() - 1, 0)):
        parity = parity + jnp.bitwise_and(jnp.right_shift(common, offset), 1)
    return (1 - 2 * jnp.bitwise_and(parity, 1)).astype(jnp.float32)


def angle_tables(positions, head_size):
    half_size = head_size // 2
    inverse = jnp.power(10000.0, -jnp.arange(half_size, dtype=jnp.float32) / half_size)
    angles = positions.astype(jnp.float32)[:, None] * inverse[None, :]
    return (jnp.cos(angles), jnp.sin(angles))


def rotary(linear, cosine_table, sine_table):
    row_count = linear.shape[0]
    half_size = cosine_table.shape[1]
    split_heads = linear.astype(jnp.float32).reshape(row_count, -1, 2 * half_size)
    front_half = split_heads[:, :, :half_size]
    back_half = split_heads[:, :, half_size:]
    cos_rows = cosine_table[:, None, :]
    sin_rows = sine_table[:, None, :]
    turned = jnp.concatenate(
        [
            front_half * cos_rows - back_half * sin_rows,
            back_half * cos_rows + front_half * sin_rows,
        ],
        axis=-1,
    )
    return turned.reshape(row_count, -1)


def join_pair(own_part, theirs, upper_bit, axis_number):
    lower_part = jnp.where(upper_bit == 1, theirs, own_part)
    upper_part = jnp.where(upper_bit == 1, own_part, theirs)
    return jnp.concatenate([lower_part, upper_part], axis=axis_number)


def attend(queries, key_rows, value_rows, allowed):
    scores = jnp.einsum("qgtd,kgd->gtqk", queries, key_rows, preferred_element_type=jnp.float32)
    scores = jnp.where(allowed[None, None], scores, -1e30)
    largest = jnp.max(scores, axis=-1, keepdims=True)
    exponent = jnp.exp(scores - largest)
    probabilities = (exponent / jnp.sum(exponent, axis=-1, keepdims=True)).astype(jnp.bfloat16)
    combined = jnp.einsum(
        "gtqk,kgd->qgtd", probabilities, value_rows, preferred_element_type=jnp.float32
    )
    return combined.astype(jnp.bfloat16)


def body(
    residual,
    positions,
    window_start,
    input_gain,
    attention_gain,
    feedforward_gain,
    output_gain,
    query_weight,
    key_weight,
    value_weight,
    output_weight,
    gate_weight,
    up_weight,
    down_weight,
):
    model_count = lax.axis_size("mp")
    model_index = lax.axis_index("mp")
    block_index = lax.axis_index("seq")
    own_rows, model_width = residual.shape
    block_length = own_rows * model_count
    joint = query_weight.shape[1] + key_weight.shape[1] + value_weight.shape[1]
    fused = (
        own_rows % 16 == 0
        and model_count == 8
        and lax.axis_size("seq") == 2
        and query_weight.shape[1] == 2 * key_weight.shape[1]
        and joint % 128 == 0
        and model_width // PART <= SLOTS * (2 * gate_weight.shape[1] // joint)
        and gate_weight.shape[1] % 384 == 0
        and model_width % (CYCLE * STRIPE) == 0
        and model_width // STRIPE <= 2 * (gate_weight.shape[1] // output_weight.shape[0])
    )
    if fused:
        cosine_table, sine_table = angle_tables(positions, HD)
        return fused_layer(
            residual,
            jnp.stack(
                [
                    jnp.concatenate([cosine_table, cosine_table], axis=1),
                    jnp.concatenate([-sine_table, sine_table], axis=1),
                    jnp.broadcast_to(
                        window_start[:, None].astype(jnp.float32), (block_length, HD)
                    ),
                ]
            ),
            (input_gain, attention_gain, feedforward_gain, output_gain),
            (
                query_weight,
                key_weight,
                value_weight,
                output_weight,
                gate_weight,
                up_weight,
                down_weight,
            ),
            WAL,
            HD,
            float(D // QH) ** (-0.5),
        )
    block_input = gather_rows(residual)
    normed = normalize(block_input, input_gain).astype(jnp.bfloat16)
    cosine_table, sine_table = angle_tables(positions, HD)
    query_scale = float(D // QH) ** (-0.5)
    paired = model_count == 2 * QH
    if paired:
        half_rows = block_length // 2
        quarter_rows = block_length // 4
        low_bit = model_index % 2
        query_first = low_bit * half_rows
        query_cosine = lax.dynamic_slice_in_dim(cosine_table, query_first, half_rows, 0)
        query_sine = lax.dynamic_slice_in_dim(sine_table, query_first, half_rows, 0)
        partner_columns = partner(query_weight, "mp", 0)
        full_query = join_pair(query_weight, partner_columns, low_bit, 1)
        query_normed = lax.dynamic_slice_in_dim(normed, query_first, half_rows, 0)
        query_linear = jnp.dot(query_normed, full_query, preferred_element_type=jnp.float32).astype(
            jnp.bfloat16
        )
        key_full = key_weight
        value_full = value_weight
        for bit_number in range(2):
            upper_bit = jnp.right_shift(model_index, bit_number) % 2
            partner_key, partner_value = (
                partner(for_sending(key_full), "mp", bit_number).astype(key_full.dtype),
                partner(for_sending(value_full), "mp", bit_number).astype(value_full.dtype),
            )
            key_full = join_pair(key_full, partner_key, upper_bit, 1)
            value_full = join_pair(value_full, partner_value, upper_bit, 1)
        quarter_first = model_index % 4 * quarter_rows
        quarter_normed = lax.dynamic_slice_in_dim(normed, quarter_first, quarter_rows, 0)
        quarter_cosine = lax.dynamic_slice_in_dim(cosine_table, quarter_first, quarter_rows, 0)
        quarter_sine = lax.dynamic_slice_in_dim(sine_table, quarter_first, quarter_rows, 0)
        key_linear = jnp.dot(quarter_normed, key_full, preferred_element_type=jnp.float32).astype(
            jnp.bfloat16
        )
        key_part = rotary(key_linear, quarter_cosine, quarter_sine).astype(jnp.bfloat16)
        value_part = jnp.dot(quarter_normed, value_full, preferred_element_type=jnp.float32).astype(
            jnp.bfloat16
        )
        for bit_number in range(2):
            upper_bit = jnp.right_shift(model_index, bit_number) % 2
            partner_key, partner_value = (
                partner(for_sending(key_part), "mp", bit_number).astype(key_part.dtype),
                partner(for_sending(value_part), "mp", bit_number).astype(value_part.dtype),
            )
            key_part = join_pair(key_part, partner_key, upper_bit, 0)
            value_part = join_pair(value_part, partner_value, upper_bit, 0)
        key_rows = key_part
        value_rows = value_part
        group_count = 1
        query_count = half_rows
        queries = (rotary(query_linear, query_cosine, query_sine) * query_scale).astype(
            jnp.bfloat16
        )
        queries = queries.reshape(query_count, 1, 1, HD)
        own_window = lax.dynamic_slice_in_dim(window_start, query_first, half_rows, 0)
    else:
        query_first = 0
        query_count = block_length
        group_count = key_weight.shape[1] // HD
        query_linear = jnp.dot(normed, query_weight, preferred_element_type=jnp.float32)
        query_linear = query_linear.astype(jnp.bfloat16)
        key_linear = jnp.dot(normed, key_weight, preferred_element_type=jnp.float32)
        key_linear = key_linear.astype(jnp.bfloat16)
        value_rows = jnp.dot(normed, value_weight, preferred_element_type=jnp.float32)
        value_rows = value_rows.astype(jnp.bfloat16)
        key_rows = rotary(key_linear, cosine_table, sine_table).astype(jnp.bfloat16)
        queries = (rotary(query_linear, cosine_table, sine_table) * query_scale).astype(
            jnp.bfloat16
        )
        queries = queries.reshape(query_count, group_count, 2, HD)
        own_window = window_start
    previous_key, previous_value = from_behind((key_rows, value_rows), "seq", 1)
    all_keys = jnp.concatenate([previous_key, key_rows], axis=0).reshape(
        2 * block_length, group_count, HD
    )
    all_values = jnp.concatenate([previous_value, value_rows], axis=0).reshape(
        2 * block_length, group_count, HD
    )
    key_index = (block_index - 1) * block_length + jnp.arange(2 * block_length, dtype=jnp.int32)
    query_index = (
        block_index * block_length + query_first + jnp.arange(query_count, dtype=jnp.int32)
    )
    allowed = (key_index[None, :] <= query_index[:, None]) & (
        key_index[None, :] >= own_window[:, None]
    )
    attended = attend(queries, all_keys, all_values, allowed)
    head_walsh = walsh_table(HD).astype(jnp.bfloat16)
    rotated = jnp.einsum(
        "qgtd,de->qgte", attended, head_walsh, preferred_element_type=jnp.float32
    ) * float(HD) ** (-0.5)
    rotated = rotated.astype(jnp.bfloat16).reshape(query_count, -1)
    if paired:
        partner_rows = partner(output_weight, "mp", 0)
        full_output = join_pair(output_weight, partner_rows, low_bit, 0)
        half_term = jnp.dot(rotated, full_output, preferred_element_type=jnp.float32)
        padded = lax.dynamic_update_slice_in_dim(
            jnp.zeros((block_length, model_width), jnp.float32), half_term, query_first, 0
        )

        def attention_term(first_row, row_count):
            return lax.dynamic_slice_in_dim(padded, first_row, row_count, 0)

    else:

        def attention_term(first_row, row_count):
            picked = lax.dynamic_slice_in_dim(rotated, first_row, row_count, 0)
            return jnp.dot(picked, output_weight, preferred_element_type=jnp.float32)

    attention_rows = scatter_rows(attention_term(jnp.int32(0), lax.axis_size("mp") * own_rows))
    first_sum = (residual.astype(jnp.float32) + normalize(attention_rows, attention_gain)).astype(
        jnp.bfloat16
    )
    feed_own = normalize(first_sum, feedforward_gain).astype(jnp.bfloat16)
    feed_input = gather_rows(feed_own)
    local_count = WAL // model_count
    block_width = FF // WAL
    if own_rows % 16 == 0 and gate_weight.shape[1] % 384 == 0:
        gathered = hidden_rows(feed_input, gate_weight, up_weight)
        gathered = gathered.reshape(model_count, own_rows, local_count, block_width)
        exchanged = gathered.transpose(1, 0, 2, 3).reshape(own_rows, WAL, block_width)
    else:
        gate_out = jnp.dot(feed_input, gate_weight, preferred_element_type=jnp.float32)
        up_out = jnp.dot(feed_input, up_weight, preferred_element_type=jnp.float32)
        activated = (jax.nn.gelu(gate_out, approximate=True) * up_out).astype(jnp.bfloat16)
        grouped = activated.reshape(block_length, local_count, block_width)
        exchanged = lax.all_to_all(grouped, "mp", split_axis=0, concat_axis=1, tiled=True)
    walsh_scale = float(WAL) ** (-0.5)
    full_table = walsh_table(WAL).astype(jnp.bfloat16)
    mixed_rows = (
        jnp.einsum(
            "rab,ac->rcb",
            exchanged,
            full_table,
            preferred_element_type=jnp.float32,
        )
        * walsh_scale
    )
    spread = lax.all_to_all(
        mixed_rows.astype(jnp.bfloat16), "mp", split_axis=1, concat_axis=0, tiled=True
    )
    spread = spread.reshape(block_length, -1)
    picked = spread
    down_rows = scatter_rows(jnp.dot(picked, down_weight, preferred_element_type=jnp.float32))
    return (first_sum.astype(jnp.float32) + normalize(down_rows, output_gain)).astype(jnp.bfloat16)


def solution(mesh):
    placed = (
        P(("groups", "seq", "mp"), None),
        P(("groups", "seq")),
        P(("groups", "seq")),
        P(),
        P(),
        P(),
        P(),
        P(None, "mp"),
        P(None, "mp"),
        P(None, "mp"),
        P("mp", None),
        P(None, "mp"),
        P(None, "mp"),
        P("mp", None),
    )
    return jax.shard_map(
        body,
        mesh=mesh,
        in_specs=placed,
        out_specs=P(("groups", "seq", "mp"), None),
        check_vma=False,
    )
```

```python
import functools

import jax
import jax.numpy as jnp
from jax import lax
from jax.experimental import pallas as pl
from jax.experimental.pallas import tpu as pltpu
from jax.sharding import PartitionSpec as P

D = 5376
FF = 21504
QH = 32
HD = 128
WAL = 64


epsilon = 1e-06


MESH = pl.DeviceIdType.MESH


def block_of(ref, index, rows):
    return ref.at[pl.ds(pl.multiple_of(index * rows, rows), rows)]


def send(source, target, send_sem, recv_sem, device):
    return pltpu.make_async_remote_copy(
        src_ref=source,
        dst_ref=target,
        send_sem=send_sem,
        recv_sem=recv_sem,
        device_id={"mp": device},
        device_id_type=MESH,
    )


def place(count):
    me = lax.axis_index("mp")
    column = lax.rem(me, 2)
    line = lax.div(me, 2)
    return me, column, line, count // 2, me + 1 - 2 * column


def greet(me, line, lines, peer):
    barrier = pltpu.get_barrier_semaphore()
    pl.semaphore_signal(barrier, inc=1, device_id={"mp": peer}, device_id_type=MESH)

    @pl.when(line > 0)
    def _():
        pl.semaphore_signal(barrier, inc=1, device_id={"mp": me - 2}, device_id_type=MESH)

    @pl.when(line < lines - 1)
    def _():
        pl.semaphore_signal(barrier, inc=1, device_id={"mp": me + 2}, device_id_type=MESH)

    beside = jnp.minimum(line, 1) + jnp.minimum(lines - 1 - line, 1)
    pl.semaphore_wait(barrier, 1 + beside)


def gather_kernel(count, own_ref, all_ref, xs, xr, us, ur, ds, dr):
    rows = own_ref.shape[0]
    me, column, line, lines, peer = place(count)
    greet(me, line, lines, peer)

    def across(origin, source):
        there = block_of(all_ref, origin * 2 + column, rows)
        return send(source, there, xs.at[origin], xr.at[origin], peer)

    def upward(origin, source):
        there = block_of(all_ref, origin * 2 + column, rows)
        return send(source, there, us.at[origin], ur.at[origin], me + 2)

    def downward(origin, source):
        there = block_of(all_ref, origin * 2 + column, rows)
        return send(source, there, ds.at[origin], dr.at[origin], me - 2)

    @pl.when(line < lines - 1)
    def _():
        upward(line, own_ref).start()

    @pl.when(line > 0)
    def _():
        downward(line, own_ref).start()

    across(line, own_ref).start()
    all_ref[pl.ds(pl.multiple_of(me * rows, rows), rows), :] = own_ref[...]
    for step in range(1, lines):

        @pl.when(line - step >= 0)
        def _():
            origin = line - step
            held = block_of(all_ref, origin * 2 + column, rows)
            upward(origin, held).wait_recv()

            @pl.when(line < lines - 1)
            def _():
                upward(origin, held).start()

            across(origin, held).start()

        @pl.when(line + step < lines)
        def _():
            origin = line + step
            held = block_of(all_ref, origin * 2 + column, rows)
            downward(origin, held).wait_recv()

            @pl.when(line > 0)
            def _():
                downward(origin, held).start()

            across(origin, held).start()

    for origin in range(lines):
        across(origin, own_ref).wait_send()
        there = block_of(all_ref, origin * 2 + 1 - column, rows)
        send(own_ref, there, xs.at[origin], xr.at[origin], peer).wait_recv()

        @pl.when((origin <= line) & (line < lines - 1))
        def _():
            upward(origin, own_ref).wait_send()

        @pl.when((origin >= line) & (line > 0))
        def _():
            downward(origin, own_ref).wait_send()


def gather_rows(own):
    count = lax.axis_size("mp")
    rows, width = own.shape
    if rows % 16 or count % 2 or count < 4:
        return lax.all_gather(own, "mp", axis=0, tiled=True)
    lines = count // 2
    return pl.pallas_call(
        functools.partial(gather_kernel, count),
        out_shape=jax.ShapeDtypeStruct((count * rows, width), own.dtype),
        in_specs=[pl.BlockSpec(memory_space=pltpu.VMEM)],
        out_specs=pl.BlockSpec(memory_space=pltpu.VMEM),
        scratch_shapes=[pltpu.SemaphoreType.DMA((lines,))] * 6,
        compiler_params=pltpu.CompilerParams(
            collective_id=0, has_side_effects=True, vmem_limit_bytes=16 * 1024 * 1024
        ),
    )(own)


def scatter_kernel(count, term_ref, sum_ref, xb, ub, db, sb, xs, xr, us, ur, ds, dr):
    rows, width = sum_ref.shape
    me, column, line, lines, peer = place(count)
    step_width = 768 if width % 768 == 0 else 128
    greet(me, line, lines, peer)

    def across(dest):
        mine = block_of(term_ref, dest * 2 + 1 - column, rows)
        return send(mine, xb.at[dest], xs.at[dest], xr.at[dest], peer)

    def upward(dest):
        return send(sb.at[dest], ub.at[dest], us.at[dest], ur.at[dest], me + 2)

    def downward(dest):
        return send(sb.at[dest], db.at[dest], ds.at[dest], dr.at[dest], me - 2)

    for away in range(lines - 1, -1, -1):

        @pl.when(line - away >= 0)
        def _():
            across(line - away).start()

        if away:

            @pl.when(line + away < lines)
            def _():
                across(line + away).start()

    def add(dest, arrived, target, index):
        first = pl.multiple_of((dest * 2 + column) * rows, rows)

        def some(i, carry):
            cols = pl.ds(pl.multiple_of(i * step_width, step_width), step_width)
            total = term_ref[pl.ds(first, rows), cols].astype(jnp.float32)
            total = total + xb[dest, :, cols].astype(jnp.float32)
            for ref in arrived:
                total = total + ref[dest, :, cols].astype(jnp.float32)
            if index:
                target[dest, :, cols] = total.astype(target.dtype)
            else:
                target[:, cols] = total
            return carry

        lax.fori_loop(0, width // step_width, some, 0)

    def go_up(dest):
        @pl.when(dest > line)
        def _():
            across(dest).wait_recv()

            @pl.when(line > 0)
            def _():
                upward(dest).wait_recv()
                add(dest, (ub,), sb, True)

            @pl.when(line == 0)
            def _():
                add(dest, (), sb, True)

            upward(dest).start()

    def go_down(dest):
        @pl.when(dest < line)
        def _():
            across(dest).wait_recv()

            @pl.when(line < lines - 1)
            def _():
                downward(dest).wait_recv()
                add(dest, (db,), sb, True)

            @pl.when(line == lines - 1)
            def _():
                add(dest, (), sb, True)

            downward(dest).start()

    for j in range(lines - 1):

        @pl.when(2 * line < lines)
        def _():
            go_up(lines - 1 - j)
            go_down(j)

        @pl.when(2 * line >= lines)
        def _():
            go_down(j)
            go_up(lines - 1 - j)

    across(line).wait_recv()

    @pl.when(line > 0)
    def _():
        upward(line).wait_recv()

    @pl.when(line < lines - 1)
    def _():
        downward(line).wait_recv()

    @pl.when((line > 0) & (line < lines - 1))
    def _():
        add(line, (ub, db), sum_ref, False)

    @pl.when(line == 0)
    def _():
        add(line, (db,), sum_ref, False)

    @pl.when(line == lines - 1)
    def _():
        add(line, (ub,), sum_ref, False)

    for dest in range(lines):
        across(dest).wait_send()

        @pl.when(dest > line)
        def _():
            upward(dest).wait_send()

        @pl.when(dest < line)
        def _():
            downward(dest).wait_send()


def scatter_rows(term):
    count = lax.axis_size("mp")
    rows, width = term.shape[0] // count, term.shape[1]
    if rows % 16 or count % 2 or count < 4:
        return lax.psum_scatter(term, "mp", scatter_dimension=0, tiled=True)
    lines = count // 2
    blocks = pltpu.VMEM((lines, rows, width), jnp.bfloat16)
    return pl.pallas_call(
        functools.partial(scatter_kernel, count),
        out_shape=jax.ShapeDtypeStruct((rows, width), jnp.float32),
        in_specs=[pl.BlockSpec(memory_space=pltpu.VMEM)],
        out_specs=pl.BlockSpec(memory_space=pltpu.VMEM),
        scratch_shapes=[blocks] * 4 + [pltpu.SemaphoreType.DMA((lines,))] * 6,
        compiler_params=pltpu.CompilerParams(
            collective_id=1, has_side_effects=True, vmem_limit_bytes=24 * 1024 * 1024
        ),
    )(term.astype(jnp.bfloat16))


def hidden_kernel(count, tiles, feed_ref, gate_ref, up_ref, out_ref, act, got, ss, rs):
    rows = feed_ref.shape[0] // count
    width = gate_ref.shape[1]
    tile = pl.program_id(0)
    me = lax.axis_index("mp")

    @pl.when(tile == 0)
    def _():
        barrier = pltpu.get_barrier_semaphore()
        for k in range(1, count):
            other = lax.rem(me + k, count)
            pl.semaphore_signal(barrier, inc=1, device_id={"mp": other}, device_id_type=MESH)
        pl.semaphore_wait(barrier, count - 1)

    feed = feed_ref[...]
    gate_out = jnp.dot(feed, gate_ref[...], preferred_element_type=jnp.float32)
    up_out = jnp.dot(feed, up_ref[...], preferred_element_type=jnp.float32)
    act[tile] = (jax.nn.gelu(gate_out, approximate=True) * up_out).astype(jnp.bfloat16)

    def to(k, t):
        other = lax.rem(me + k, count)
        source = act.at[t, pl.ds(pl.multiple_of(other * rows, rows), rows), :]
        target = got.at[t, pl.ds(pl.multiple_of(me * rows, rows), rows), :]
        return send(source, target, ss.at[k, t], rs.at[k, t], other)

    for k in range(1, count):
        to(k, tile).start()
    own = pl.ds(pl.multiple_of(me * rows, rows), rows)
    got[tile, own, :] = act[tile, own, :]

    @pl.when(tile == tiles - 1)
    def _():
        for t in range(tiles):
            for k in range(1, count):
                to(k, t).wait_recv()
            out_ref[:, t * width : (t + 1) * width] = got[t]
        for t in range(tiles):
            for k in range(1, count):
                to(k, t).wait_send()


def hidden_rows(feed, gate_weight, up_weight):
    count = lax.axis_size("mp")
    length, depth = feed.shape
    hidden = gate_weight.shape[1]
    rows, tile = length // count, 384
    tiles = hidden // tile
    weights = pl.BlockSpec((depth, tile), lambda t: (0, t))
    return pl.pallas_call(
        functools.partial(hidden_kernel, count, tiles),
        grid=(tiles,),
        out_shape=jax.ShapeDtypeStruct((length, hidden), jnp.bfloat16),
        in_specs=[pl.BlockSpec((length, depth), lambda t: (0, 0)), weights, weights],
        out_specs=pl.BlockSpec((length, hidden), lambda t: (0, 0)),
        scratch_shapes=[
            pltpu.VMEM((tiles, length, tile), jnp.bfloat16),
            pltpu.VMEM((tiles, length, tile), jnp.bfloat16),
            pltpu.SemaphoreType.DMA((count, tiles)),
            pltpu.SemaphoreType.DMA((count, tiles)),
        ],
        compiler_params=pltpu.CompilerParams(
            collective_id=2,
            has_side_effects=True,
            dimension_semantics=("arbitrary",),
            vmem_limit_bytes=48 * 1024 * 1024,
        ),
    )(feed, gate_weight, up_weight)


PART = 256
STRIPE = 3 * PART
CYCLE = 7
LAG = 4
SUM_LAG = 3
SLOTS = 5


def is_paired(c):
    return lax.rem(c, CYCLE) == CYCLE // 2


def signal_to(device):
    barrier = pltpu.get_barrier_semaphore()
    pl.semaphore_signal(barrier, inc=1, device_id={"mp": device}, device_id_type=MESH)


def row_scale(read, parts, width):
    total = read(0) * read(0)
    for c in range(1, parts):
        total = total + read(c) * read(c)
    return lax.rsqrt(jnp.sum(total, axis=-1, keepdims=True) / width + epsilon)


def columns_of(c, width):
    return pl.ds(pl.multiple_of(c * width, width), width)


def wait_for(ref, sem, device):
    send(ref, ref, sem, sem, device).wait_recv()


def wait_sent(ref, sem, device):
    send(ref, ref, sem, sem, device).wait_send()


class Gather:
    def __init__(self, count, rows, buf, sems):
        self.buf, self.rows = buf, rows
        self.xs, self.ps, self.us, self.ds, self.xr, self.zr = sems
        self.parts = buf.shape[0]
        self.me, self.column, self.line, self.lines, self.peer = place(count)

    def block(self, c, origin, column):
        first, rows = origin * 2, self.rows
        if column is None:
            rows = 2 * rows
        else:
            first = first + column
        first = pl.multiple_of(first * self.rows, rows)
        return self.buf.at[c, pl.ds(first, rows), :]

    def across(self, c, origin, sem):
        there = self.block(c, origin, self.column)
        return send(there, there, sem.at[0], self.xr.at[c], self.peer)

    def upward(self, c, origin, both):
        there = self.block(c, origin, None if both else self.column)
        return send(there, there, self.us.at[0], self.zr.at[c, origin], self.me + 2)

    def downward(self, c, origin, both):
        there = self.block(c, origin, None if both else self.column)
        return send(there, there, self.ds.at[0], self.zr.at[c, origin], self.me - 2)

    def valid(self, c):
        return (c >= 0) & (c < self.parts)

    def both_ways(self, c, both):
        @pl.when(self.line < self.lines - 1)
        def _():
            self.upward(c, self.line, both).start()

        @pl.when(self.line > 0)
        def _():
            self.downward(c, self.line, both).start()

    def relay(self, c, away, both):
        line, lines = self.line, self.lines

        @pl.when(line - away >= 0)
        def _():
            self.upward(c, line - away, both).wait_recv()

            @pl.when(line < lines - 1)
            def _():
                self.upward(c, line - away, both).start()

            if not both:
                self.across(c, line - away, self.xs).start()

        @pl.when(line + away < lines)
        def _():
            self.downward(c, line + away, both).wait_recv()

            @pl.when(line > 0)
            def _():
                self.downward(c, line + away, both).start()

            if not both:
                self.across(c, line + away, self.xs).start()

    def open(self):
        def one(c, carry):
            @pl.when(jnp.logical_not(is_paired(c)))
            def _():
                self.both_ways(c, False)
                self.across(c, self.line, self.xs).start()

            @pl.when(is_paired(c))
            def _():
                self.across(c, self.line, self.ps).start()

            return carry

        lax.fori_loop(0, self.parts, one, 0)

    def behind(self):
        return LAG * (self.lines - 1)

    def step(self, t):
        line, lines = self.line, self.lines

        @pl.when(self.valid(t) & is_paired(t))
        def _():
            wait_for(self.block(t, line, 1 - self.column), self.xr.at[t], self.peer)
            self.both_ways(t, True)

        for away in range(1, lines):
            c = t - (away - 1) * LAG

            @pl.when(self.valid(c) & jnp.logical_not(is_paired(c)))
            def _():
                self.relay(c, away, False)

            late = c - LAG

            @pl.when(self.valid(late) & is_paired(late))
            def _():
                self.relay(late, away, True)

    def arrived(self, c):
        @pl.when(jnp.logical_not(is_paired(c)))
        def _():
            wait_for(self.buf.at[c, 0 : self.lines * self.rows, :], self.xr.at[c], self.peer)

    def finish(self):
        line, lines, parts = self.line, self.lines, self.parts
        pairs = parts // CYCLE
        share = (parts + pairs) * self.rows // self.buf.shape[1]
        half = lines * self.rows
        wait_sent(self.buf.at[0 : parts - pairs, 0:half, :], self.xs.at[0], self.peer)
        wait_sent(self.buf.at[0:pairs, 0 : self.rows, :], self.ps.at[0], self.peer)
        for at in range(lines):

            @pl.when(line == at)
            def _():
                if at < lines - 1:
                    wait_sent(self.buf.at[0 : share * (at + 1)], self.us.at[0], self.peer)
                if at > 0:
                    wait_sent(self.buf.at[0 : share * (lines - at)], self.ds.at[0], self.peer)


class Scatter:
    def __init__(self, count, rows, term, xb, ub, db, sb, up, dp, sp, sums, sems):
        self.term, self.xb, self.ub, self.db, self.sb, self.sums = term, xb, ub, db, sb, sums
        self.up, self.dp, self.sp = up, dp, sp
        self.rows = rows
        self.xs, self.ps, self.us, self.ds, self.xr, self.ur, self.dr = sems
        self.parts = term.shape[0]
        self.me, self.column, self.line, self.lines, self.peer = place(count)

    def mine(self, dest, column):
        return pl.ds(pl.multiple_of((dest * 2 + column) * self.rows, self.rows), self.rows)

    def across(self, c, dest):
        source = self.term.at[c, self.mine(dest, 1 - self.column), :]
        return send(source, self.xb.at[c, dest], self.xs.at[0], self.xr.at[c], self.peer)

    def across_total(self, c):
        there, source = self.xb.at[c, self.line], self.sb.at[c, self.line]
        return send(source, there, self.ps.at[0], self.xr.at[c], self.peer)

    def slot(self, c, both):
        return lax.div(c, CYCLE) if both else c

    def upward(self, c, dest, both):
        at = self.slot(c, both)
        source, there = (self.sp, self.up) if both else (self.sb, self.ub)
        return send(
            source.at[at, dest], there.at[at, dest], self.us.at[0], self.ur.at[c], self.me + 2
        )

    def downward(self, c, dest, both):
        at = self.slot(c, both)
        source, there = (self.sp, self.dp) if both else (self.sb, self.db)
        return send(
            source.at[at, dest], there.at[at, dest], self.ds.at[0], self.dr.at[c], self.me - 2
        )

    def total(self, c, dest, arrived, both):
        if both:
            here = pl.ds(pl.multiple_of(dest * 2 * self.rows, 2 * self.rows), 2 * self.rows)
            total = self.term[c, here, :].astype(jnp.float32)
        else:
            total = self.term[c, self.mine(dest, self.column), :].astype(jnp.float32)
            total = total + self.xb[c, dest].astype(jnp.float32)
        for ref in arrived:
            total = total + ref[self.slot(c, both), dest].astype(jnp.float32)
        return total

    def pass_up(self, c, both):
        line, lines = self.line, self.lines
        ub = self.up if both else self.ub
        to = self.sp if both else self.sb
        at = self.slot(c, both)
        for here in range(lines):

            @pl.when(line == here)
            def _():
                if here:
                    wait_for(ub.at[at, here:lines], self.ur.at[c], self.peer)
                for dest in range(lines - 1, here, -1):
                    total = self.total(c, dest, (ub,) if here else (), both)
                    to[at, dest] = total.astype(to.dtype)
                    self.upward(c, dest, both).start()

    def pass_down(self, c, both):
        line, lines = self.line, self.lines
        db = self.dp if both else self.db
        to = self.sp if both else self.sb
        at = self.slot(c, both)
        for here in range(lines):

            @pl.when(line == here)
            def _():
                last = here == lines - 1
                if not last:
                    wait_for(db.at[at, 0 : here + 1], self.dr.at[c], self.peer)
                for dest in range(here):
                    total = self.total(c, dest, () if last else (db,), both)
                    to[at, dest] = total.astype(to.dtype)
                    self.downward(c, dest, both).start()

    def settle(self, c, both):
        line, lines = self.line, self.lines
        ub, db = (self.up, self.dp) if both else (self.ub, self.db)

        def store(arrived):
            total = self.total(c, line, arrived, both)
            if not both:
                self.sums[c] = total
                return
            own, other = total[: self.rows], total[self.rows :]

            @pl.when(self.column == 0)
            def _():
                self.sums[c] = own
                self.sb[c, line] = other.astype(self.sb.dtype)

            @pl.when(self.column == 1)
            def _():
                self.sums[c] = other
                self.sb[c, line] = own.astype(self.sb.dtype)

        @pl.when(line == 0)
        def _():
            store((db,))

        @pl.when(line == lines - 1)
        def _():
            store((ub,))

        @pl.when((line > 0) & (line < lines - 1))
        def _():
            store((ub, db))

        if both:
            self.across_total(c).start()

    def run(self, produce):
        line, lines, parts = self.line, self.lines, self.parts

        def valid(c, both):
            paired = is_paired(c)
            return (c >= 0) & (c < parts) & (paired if both else jnp.logical_not(paired))

        def step(t, carry):
            @pl.when(t < parts)
            def _():
                produce(t)

            @pl.when(valid(t, False))
            def _():
                for away in range(lines - 1, -1, -1):

                    @pl.when(line - away >= 0)
                    def _():
                        self.across(t, line - away).start()

                    if away:

                        @pl.when(line + away < lines)
                        def _():
                            self.across(t, line + away).start()

            first = t - SUM_LAG

            @pl.when(valid(first, False))
            def _():
                wait_for(self.xb.at[first], self.xr.at[first], self.peer)

            cu, cd, c = t - SUM_LAG * (1 + line), t - SUM_LAG * (lines - line), t - SUM_LAG * lines
            for both in (False, True):

                @pl.when(valid(cu, both))
                def _():
                    self.pass_up(cu, both)

                @pl.when(valid(cd, both))
                def _():
                    self.pass_down(cd, both)

                @pl.when(valid(c, both))
                def _():
                    self.settle(c, both)

            late = c - SUM_LAG

            @pl.when(valid(late, True))
            def _():
                wait_for(self.xb.at[late, line], self.xr.at[late], self.peer)
                self.sums[late] += self.xb[late, line].astype(jnp.float32)

            return carry

        lax.fori_loop(0, parts + SUM_LAG * (lines + 1), step, 0)
        pairs = parts // CYCLE
        share = (parts + pairs) * self.rows // self.term.shape[1]
        half = lines * self.rows
        wait_sent(self.term.at[0 : parts - pairs, 0:half, :], self.xs.at[0], self.peer)
        wait_sent(self.xb.at[0:pairs, 0], self.ps.at[0], self.peer)
        for at in range(lines):

            @pl.when(line == at)
            def _():
                if at < lines - 1:
                    wait_sent(self.term.at[0 : share * (lines - 1 - at)], self.us.at[0], self.peer)
                if at > 0:
                    wait_sent(self.term.at[0 : share * at], self.ds.at[0], self.peer)


def butterfly(values):
    values = list(values)
    apart = 1
    while apart < len(values):
        for low in range(len(values)):
            if low // apart % 2 == 0:
                a, b = values[low], values[low + apart]
                values[low], values[low + apart] = a + b, a - b
        apart *= 2
    return values


def layer_kernel(
    count, blocks, head, scale, resid, tables, in_gain, att_gain, feed_gain, out_gain,
    wq, wk, wv, wo, wg, wu, wd, out_ref,
    rot, pairs_own, pairs_all, term, xb, ub, db, sb, up, dp, sp, sums, first, feed, gu, acc,
    act, got, mixed, spread, spun, dbuf,
    w_sem, wo_sem, gu_sem, d_sem, kv_sem, a_send, a_recv, b_send, b_recv, *sems,
):
    rows, width = resid.shape
    parts, length, part = feed.shape
    hidden = wg.shape[1]
    slots, d_slots = gu.shape[0], dbuf.shape[0]
    halves = rows // 16
    local = blocks // count
    inner = hidden // local
    stripes = width // STRIPE
    scatter = Scatter(count, 16, term, xb, ub, db, sb, up, dp, sp, sums, sems[:7])
    gather = Gather(count, rows, feed, sems[7:])
    me, lines, peer = scatter.me, scatter.lines, scatter.peer
    seq = lax.axis_index("seq")
    spans = ((wq, 0), (wk, wq.shape[1]), (wv, wq.shape[1] + wk.shape[1]))
    joint = wq.shape[1] + wk.shape[1] + wv.shape[1]
    held = gu.shape[2] // joint

    def joint_columns(c):
        return pl.ds(pl.multiple_of(lax.rem(c, held) * joint, 128), joint)

    def load_joint(c, carry):
        slot, start = lax.div(c, held), lax.rem(c, held) * joint
        for source, at in spans:
            target = gu.at[slot, :, pl.ds(pl.multiple_of(start + at, 128), source.shape[1])]
            copy = source.at[columns_of(c, part), :]
            pltpu.make_async_copy(copy, target, w_sem.at[c]).start()
        return carry

    deep = wo.shape[0]
    layers = hidden // deep

    def wo_part(c):
        first = pl.multiple_of(lax.rem(c, layers) * deep, deep)
        return dbuf.at[lax.div(c, layers), pl.ds(first, deep), :]

    def load_wo(c):
        return pltpu.make_async_copy(wo.at[:, columns_of(c, STRIPE)], wo_part(c), wo_sem.at[c])

    def load_gu(c):
        slot = lax.rem(c, slots)
        for i, source in enumerate((wg, wu)):
            target = gu.at[slot, :, i * hidden : (i + 1) * hidden]
            copy = source.at[columns_of(c, part), :]
            pltpu.make_async_copy(copy, target, gu_sem.at[slot]).start()

    def load_d(c):
        slot, cols = lax.rem(c, d_slots), columns_of(lax.rem(c, stripes), STRIPE)
        return pltpu.make_async_copy(wd.at[:, cols], dbuf.at[slot], d_sem.at[slot])

    for k in range(1, count):
        signal_to(lax.rem(me + k, count))
    barrier = pltpu.get_barrier_semaphore()
    pl.semaphore_signal(barrier, inc=1, device_id={"seq": 1 - seq}, device_id_type=MESH)
    lax.fori_loop(0, parts, load_joint, 0)

    own = pl.ds(pl.multiple_of(me * rows, rows), rows)

    def read(c):
        return resid[:, c * part : (c + 1) * part].astype(jnp.float32)

    in_scale = row_scale(read, parts, width)
    for c in range(parts):
        normed = read(c) * in_scale * in_gain[c * part : (c + 1) * part]
        feed[c, own, :] = normed.astype(feed.dtype)
    pl.semaphore_wait(barrier, count)

    def project_step(t, carry):
        gather.step(t)
        c = t - gather.behind()

        @pl.when(t == 0)
        def _():
            acc[:, 0:joint] = jnp.zeros((length, joint), jnp.float32)

        @pl.when(c >= 0)
        def _():
            weight = gu.at[lax.div(c, held), :, joint_columns(c)]
            pltpu.make_async_copy(weight, weight, w_sem.at[c]).wait()
            gather.arrived(c)
            acc[:, 0:joint] += jnp.dot(feed[c], weight[...], preferred_element_type=jnp.float32)

        return carry

    gather.open()
    lax.fori_loop(0, parts + gather.behind(), project_step, 0)
    gather.finish()
    for c in range(slots):
        load_gu(c)
    for c in range(stripes):
        load_wo(c).start()

    def head_rows(first, n):
        at = first + n * head
        return acc[:, at : at + head].astype(jnp.bfloat16).astype(jnp.float32)

    def rope(value):
        return value * tables[0] + pltpu.roll(value, head // 2, 1) * tables[1]

    groups = wk.shape[1] // head
    for g in range(groups):
        lanes = slice(g * head, (g + 1) * head)
        pairs_own[0, :, lanes] = rope(head_rows(spans[1][1], g)).astype(pairs_own.dtype)
        pairs_own[1, :, lanes] = head_rows(spans[2][1], g).astype(pairs_own.dtype)

    there = pairs_all.at[:, 0:length, :]
    exchange = pltpu.make_async_remote_copy(
        src_ref=pairs_own,
        dst_ref=there,
        send_sem=kv_sem.at[0],
        recv_sem=kv_sem.at[1],
        device_id={"seq": 1 - seq},
        device_id_type=MESH,
    )

    @pl.when(seq == 0)
    def _():
        exchange.start()
        pairs_all[:, 0:length, :] = jnp.zeros((2, length, groups * head), pairs_all.dtype)

    pairs_all[:, length : 2 * length, :] = pairs_own[...]
    query = lax.broadcasted_iota(jnp.int32, (length, 2 * length), 0) + seq * length
    key = lax.broadcasted_iota(jnp.int32, (length, 2 * length), 1) + (seq - 1) * length
    allowed = (key <= query) & (key.astype(jnp.float32) >= tables[2, :, 0:1])
    table = walsh_table(head).astype(jnp.bfloat16)

    @pl.when(seq == 1)
    def _():
        exchange.wait_recv()

    for n in range(wq.shape[1] // head):
        lanes = slice(n // 2 * head, (n // 2 + 1) * head)
        queries = (rope(head_rows(0, n)) * scale).astype(jnp.bfloat16)
        scores = lax.dot_general(
            queries,
            pairs_all[0, :, lanes],
            (((1,), (1,)), ((), ())),
            preferred_element_type=jnp.float32,
        )
        scores = jnp.where(allowed, scores, -1e30)
        exponent = jnp.exp(scores - jnp.max(scores, axis=-1, keepdims=True))
        probabilities = exponent / jnp.sum(exponent, axis=-1, keepdims=True)
        attended = jnp.dot(
            probabilities.astype(jnp.bfloat16),
            pairs_all[1, :, lanes],
            preferred_element_type=jnp.float32,
        )
        rotated = jnp.dot(
            attended.astype(jnp.bfloat16), table, preferred_element_type=jnp.float32
        )
        rotated = rotated * float(head) ** (-0.5)
        rotated = rotated.astype(rot.dtype)
        for d in range(count):
            for h in range(halves):
                piece = rotated[d * rows + h * 16 : d * rows + h * 16 + 16]
                rot[h, d * 16 : d * 16 + 16, n * head : (n + 1) * head] = piece

    @pl.when(seq == 0)
    def _():
        exchange.wait_send()

    tile = 384

    def attention_part(t):
        h, c = lax.div(t, stripes), lax.rem(t, stripes)

        @pl.when(h == 0)
        def _():
            load_wo(c).wait()

        value = jnp.dot(rot[h], wo_part(c)[...], preferred_element_type=jnp.float32)
        term[t] = value.astype(term.dtype)

        @pl.when(t == halves * stripes - 1)
        def _():
            for c in range(d_slots):
                load_d(c).start()

    scatter.run(attention_part)

    def at(h):
        return slice(h * 16, h * 16 + 16)

    def stripe(c):
        return slice(c * STRIPE, (c + 1) * STRIPE)

    for h in range(halves):
        att_scale = row_scale(lambda c: sums[h * stripes + c], stripes, width)
        for c in range(stripes):
            value = sums[h * stripes + c] * att_scale * att_gain[stripe(c)]
            value = resid[at(h), stripe(c)].astype(jnp.float32) + value
            first[c, at(h), :] = value.astype(first.dtype)
        feed_scale = row_scale(
            lambda c: first[c, at(h), :].astype(jnp.float32), stripes, width
        )
        own_half = pl.ds(pl.multiple_of(me * rows + h * 16, 16), 16)
        for c in range(stripes):
            value = first[c, at(h), :].astype(jnp.float32) * feed_scale * feed_gain[stripe(c)]
            value = value.astype(feed.dtype)
            for i in range(STRIPE // part):
                piece = value[:, i * part : (i + 1) * part]
                feed[c * (STRIPE // part) + i, own_half, :] = piece

    def feed_step(t, carry):
        gather.step(t)
        c = t - gather.behind()

        @pl.when(t == 0)
        def _():
            acc[...] = jnp.zeros_like(acc)

        @pl.when(c >= 0)
        def _():
            slot = lax.rem(c, slots)
            pltpu.make_async_copy(gu.at[slot], gu.at[slot], gu_sem.at[slot]).wait()
            gather.arrived(c)
            acc[...] += jnp.dot(feed[c], gu[slot], preferred_element_type=jnp.float32)

            @pl.when(c + slots < parts)
            def _():
                load_gu(c + slots)

        return carry

    gather.open()
    lax.fori_loop(0, parts + gather.behind(), feed_step, 0)

    def half_rows(device, h):
        return pl.ds(pl.multiple_of(device * rows + h * 16, 16), 16)

    def to_mixer(h, k):
        other = lax.rem(me + k, count)
        source, there = act.at[half_rows(other, h), :], got.at[me, pl.ds(h * 16, 16), :]
        return send(source, there, a_send.at[h], a_recv.at[h], other)

    def from_mixer(h, k):
        other = lax.rem(me + k, count)
        source, there = spread.at[other, pl.ds(h * 16, 16), :], spun.at[h, spun_rows, :]
        return send(source, there, b_send.at[h], b_recv.at[h], other)

    spun_rows = pl.ds(pl.multiple_of(me * 16, 16), 16)
    others = got.at[0 : count - 1, 0:16, :]
    for h in range(halves):

        def activate(k, carry):
            here = half_rows(lax.rem(me + k, count), h)

            def some(n, carry):
                cols = columns_of(n, tile)
                beside = pl.ds(pl.multiple_of(hidden + n * tile, 128), tile)
                value = jax.nn.gelu(acc[here, cols], approximate=True) * acc[here, beside]
                act[here, cols] = value.astype(act.dtype)
                return carry

            lax.fori_loop(0, hidden // tile, some, 0)

            @pl.when(k < count)
            def _():
                to_mixer(h, k).start()

            return carry

        lax.fori_loop(1, count + 1, activate, 0)
        got[me, h * 16 : h * 16 + 16, :] = act[half_rows(me, h), :]

    for h in range(halves):
        wait_for(others, a_recv.at[h], peer)

        def over_devices(n, carry):
            cols = columns_of(n, tile)
            held = [got[d, h * 16 : h * 16 + 16, cols].astype(jnp.float32) for d in range(count)]
            for d, value in enumerate(butterfly(held)):
                mixed[d, :, cols] = value
            return carry

        lax.fori_loop(0, hidden // tile, over_devices, 0)

        def within(k, carry):
            other = lax.rem(me + k, count)
            value = mixed[other]
            pieces = [value[:, a * inner : (a + 1) * inner] for a in range(local)]
            whole = jnp.concatenate(butterfly(pieces), axis=1) * float(blocks) ** (-0.5)
            spread[other, h * 16 : h * 16 + 16, :] = whole.astype(spread.dtype)

            @pl.when(k < count)
            def _():
                from_mixer(h, k).start()

            return carry

        lax.fori_loop(1, count + 1, within, 0)
        spun[h, spun_rows, :] = spread[me, h * 16 : h * 16 + 16, :]

    def down_part(t):
        for h in range(halves):

            @pl.when(t == h * stripes)
            def _():
                wait_for(others, b_recv.at[h], peer)

        load_d(t).wait()
        weight = dbuf[lax.rem(t, d_slots)]
        value = jnp.dot(spun[lax.div(t, stripes)], weight, preferred_element_type=jnp.float32)
        term[t] = value.astype(term.dtype)

        @pl.when(t + d_slots < halves * stripes)
        def _():
            load_d(t + d_slots).start()

    scatter.run(down_part)
    for h in range(halves):
        out_scale = row_scale(lambda c: sums[h * stripes + c], stripes, width)
        for c in range(stripes):
            value = sums[h * stripes + c] * out_scale * out_gain[stripe(c)]
            value = first[c, at(h), :].astype(jnp.float32) + value
            out_ref[at(h), stripe(c)] = value.astype(out_ref.dtype)

    gather.finish()
    for h in range(halves):
        wait_sent(others, a_send.at[h], peer)
        wait_sent(others, b_send.at[h], peer)


def fused_layer(residual, tables, gains, weights, blocks, head, scale):
    count = lax.axis_size("mp")
    rows, width = residual.shape
    part = PART
    parts, lines, length = width // part, count // 2, count * rows
    query_weight, key_weight, _, _, gate_weight, _, _ = weights
    hidden, kept = gate_weight.shape[1], key_weight.shape[1]
    slots, d_slots, halves = SLOTS, 2, rows // 16
    vmem = pl.BlockSpec(memory_space=pltpu.VMEM)
    hbm = pl.BlockSpec(memory_space=pltpu.HBM)
    bf16, f32 = jnp.bfloat16, jnp.float32
    stripes = width // STRIPE
    shares = halves * stripes
    block = pltpu.VMEM((shares, lines, 16, STRIPE), bf16)
    paired = pltpu.VMEM((shares // CYCLE, lines, 32, STRIPE), bf16)
    dma = pltpu.SemaphoreType.DMA
    return pl.pallas_call(
        functools.partial(layer_kernel, count, blocks, head, scale),
        out_shape=jax.ShapeDtypeStruct((rows, width), residual.dtype),
        in_specs=[vmem] * 6 + [hbm] * 7,
        out_specs=vmem,
        scratch_shapes=[
            pltpu.VMEM((halves, count * 16, query_weight.shape[1]), bf16),
            pltpu.VMEM((2, length, kept), bf16),
            pltpu.VMEM((2, 2 * length, kept), bf16),
            pltpu.VMEM((shares, count * 16, STRIPE), bf16),
            block,
            block,
            block,
            block,
            paired,
            paired,
            paired,
            pltpu.VMEM((shares, 16, STRIPE), f32),
            pltpu.VMEM((stripes, rows, STRIPE), bf16),
            pltpu.VMEM((parts, length, part), bf16),
            pltpu.VMEM((slots, part, 2 * hidden), bf16),
            pltpu.VMEM((length, 2 * hidden), f32),
            pltpu.VMEM((length, hidden), bf16),
            pltpu.VMEM((count, rows, hidden), bf16),
            pltpu.VMEM((count, 16, hidden), f32),
            pltpu.VMEM((count, rows, hidden), bf16),
            pltpu.VMEM((halves, count * 16, hidden), bf16),
            pltpu.VMEM((d_slots, hidden, STRIPE), bf16),
            dma((parts,)),
            dma((width // STRIPE,)),
            dma((slots,)),
            dma((d_slots,)),
            dma((2,)),
        ]
        + [dma((halves,))] * 4
        + [dma((1,))] * 4
        + [dma((shares,))] * 3
        + [dma((1,))] * 4
        + [dma((parts,)), dma((parts, lines))],
        compiler_params=pltpu.CompilerParams(
            collective_id=4, has_side_effects=True, vmem_limit_bytes=56 * 1024 * 1024
        ),
    )(residual, tables, *gains, *weights)


def partner(block, axis, apart):
    count = lax.axis_size(axis)
    route = []
    for low in range(count):
        high = low | 1 << apart
        if high != low and high < count:
            route += [(low, high), (high, low)]
    return lax.ppermute(block, axis, route)


def for_sending(value):
    return jax.tree.map(lambda a: a.astype(jnp.bfloat16) if a.dtype == jnp.float32 else a, value)


def from_behind(block, axis, distance):
    devices = range(lax.axis_size(axis))
    route = [(i - distance, i) for i in devices if i - distance in devices]
    return lax.ppermute(block, axis, route)


def normalize(values_in, gain_row):
    widened = values_in.astype(jnp.float32)
    mean_square = jnp.mean(widened * widened, axis=-1, keepdims=True)
    return widened * lax.rsqrt(mean_square + epsilon) * gain_row


def walsh_table(length):
    row_index = lax.broadcasted_iota(jnp.int32, (length, length), 0)
    column_index = lax.broadcasted_iota(jnp.int32, (length, length), 1)
    common = jnp.bitwise_and(row_index, column_index)
    parity = jnp.zeros((length, length), jnp.int32)
    for offset in range(max(length.bit_length() - 1, 0)):
        parity = parity + jnp.bitwise_and(jnp.right_shift(common, offset), 1)
    return (1 - 2 * jnp.bitwise_and(parity, 1)).astype(jnp.float32)


def angle_tables(positions, head_size):
    half_size = head_size // 2
    inverse = jnp.power(10000.0, -jnp.arange(half_size, dtype=jnp.float32) / half_size)
    angles = positions.astype(jnp.float32)[:, None] * inverse[None, :]
    return (jnp.cos(angles), jnp.sin(angles))


def rotary(linear, cosine_table, sine_table):
    row_count = linear.shape[0]
    half_size = cosine_table.shape[1]
    split_heads = linear.astype(jnp.float32).reshape(row_count, -1, 2 * half_size)
    front_half = split_heads[:, :, :half_size]
    back_half = split_heads[:, :, half_size:]
    cos_rows = cosine_table[:, None, :]
    sin_rows = sine_table[:, None, :]
    turned = jnp.concatenate(
        [
            front_half * cos_rows - back_half * sin_rows,
            back_half * cos_rows + front_half * sin_rows,
        ],
        axis=-1,
    )
    return turned.reshape(row_count, -1)


def join_pair(own_part, theirs, upper_bit, axis_number):
    lower_part = jnp.where(upper_bit == 1, theirs, own_part)
    upper_part = jnp.where(upper_bit == 1, own_part, theirs)
    return jnp.concatenate([lower_part, upper_part], axis=axis_number)


def attend(queries, key_rows, value_rows, allowed):
    scores = jnp.einsum("qgtd,kgd->gtqk", queries, key_rows, preferred_element_type=jnp.float32)
    scores = jnp.where(allowed[None, None], scores, -1e30)
    largest = jnp.max(scores, axis=-1, keepdims=True)
    exponent = jnp.exp(scores - largest)
    probabilities = (exponent / jnp.sum(exponent, axis=-1, keepdims=True)).astype(jnp.bfloat16)
    combined = jnp.einsum(
        "gtqk,kgd->qgtd", probabilities, value_rows, preferred_element_type=jnp.float32
    )
    return combined.astype(jnp.bfloat16)


def body(
    residual,
    positions,
    window_start,
    input_gain,
    attention_gain,
    feedforward_gain,
    output_gain,
    query_weight,
    key_weight,
    value_weight,
    output_weight,
    gate_weight,
    up_weight,
    down_weight,
):
    model_count = lax.axis_size("mp")
    model_index = lax.axis_index("mp")
    block_index = lax.axis_index("seq")
    own_rows, model_width = residual.shape
    block_length = own_rows * model_count
    joint = query_weight.shape[1] + key_weight.shape[1] + value_weight.shape[1]
    fused = (
        own_rows % 16 == 0
        and model_count == 8
        and lax.axis_size("seq") == 2
        and query_weight.shape[1] == 2 * key_weight.shape[1]
        and joint % 128 == 0
        and model_width // PART <= SLOTS * (2 * gate_weight.shape[1] // joint)
        and gate_weight.shape[1] % 384 == 0
        and model_width % (CYCLE * STRIPE) == 0
        and model_width // STRIPE <= 2 * (gate_weight.shape[1] // output_weight.shape[0])
    )
    if fused:
        cosine_table, sine_table = angle_tables(positions, HD)
        return fused_layer(
            residual,
            jnp.stack(
                [
                    jnp.concatenate([cosine_table, cosine_table], axis=1),
                    jnp.concatenate([-sine_table, sine_table], axis=1),
                    jnp.broadcast_to(
                        window_start[:, None].astype(jnp.float32), (block_length, HD)
                    ),
                ]
            ),
            (input_gain, attention_gain, feedforward_gain, output_gain),
            (
                query_weight,
                key_weight,
                value_weight,
                output_weight,
                gate_weight,
                up_weight,
                down_weight,
            ),
            WAL,
            HD,
            float(D // QH) ** (-0.5),
        )
    block_input = gather_rows(residual)
    normed = normalize(block_input, input_gain).astype(jnp.bfloat16)
    cosine_table, sine_table = angle_tables(positions, HD)
    query_scale = float(D // QH) ** (-0.5)
    paired = model_count == 2 * QH
    if paired:
        half_rows = block_length // 2
        quarter_rows = block_length // 4
        low_bit = model_index % 2
        query_first = low_bit * half_rows
        query_cosine = lax.dynamic_slice_in_dim(cosine_table, query_first, half_rows, 0)
        query_sine = lax.dynamic_slice_in_dim(sine_table, query_first, half_rows, 0)
        partner_columns = partner(query_weight, "mp", 0)
        full_query = join_pair(query_weight, partner_columns, low_bit, 1)
        query_normed = lax.dynamic_slice_in_dim(normed, query_first, half_rows, 0)
        query_linear = jnp.dot(query_normed, full_query, preferred_element_type=jnp.float32).astype(
            jnp.bfloat16
        )
        key_full = key_weight
        value_full = value_weight
        for bit_number in range(2):
            upper_bit = jnp.right_shift(model_index, bit_number) % 2
            partner_key, partner_value = (
                partner(for_sending(key_full), "mp", bit_number).astype(key_full.dtype),
                partner(for_sending(value_full), "mp", bit_number).astype(value_full.dtype),
            )
            key_full = join_pair(key_full, partner_key, upper_bit, 1)
            value_full = join_pair(value_full, partner_value, upper_bit, 1)
        quarter_first = model_index % 4 * quarter_rows
        quarter_normed = lax.dynamic_slice_in_dim(normed, quarter_first, quarter_rows, 0)
        quarter_cosine = lax.dynamic_slice_in_dim(cosine_table, quarter_first, quarter_rows, 0)
        quarter_sine = lax.dynamic_slice_in_dim(sine_table, quarter_first, quarter_rows, 0)
        key_linear = jnp.dot(quarter_normed, key_full, preferred_element_type=jnp.float32).astype(
            jnp.bfloat16
        )
        key_part = rotary(key_linear, quarter_cosine, quarter_sine).astype(jnp.bfloat16)
        value_part = jnp.dot(quarter_normed, value_full, preferred_element_type=jnp.float32).astype(
            jnp.bfloat16
        )
        for bit_number in range(2):
            upper_bit = jnp.right_shift(model_index, bit_number) % 2
            partner_key, partner_value = (
                partner(for_sending(key_part), "mp", bit_number).astype(key_part.dtype),
                partner(for_sending(value_part), "mp", bit_number).astype(value_part.dtype),
            )
            key_part = join_pair(key_part, partner_key, upper_bit, 0)
            value_part = join_pair(value_part, partner_value, upper_bit, 0)
        key_rows = key_part
        value_rows = value_part
        group_count = 1
        query_count = half_rows
        queries = (rotary(query_linear, query_cosine, query_sine) * query_scale).astype(
            jnp.bfloat16
        )
        queries = queries.reshape(query_count, 1, 1, HD)
        own_window = lax.dynamic_slice_in_dim(window_start, query_first, half_rows, 0)
    else:
        query_first = 0
        query_count = block_length
        group_count = key_weight.shape[1] // HD
        query_linear = jnp.dot(normed, query_weight, preferred_element_type=jnp.float32)
        query_linear = query_linear.astype(jnp.bfloat16)
        key_linear = jnp.dot(normed, key_weight, preferred_element_type=jnp.float32)
        key_linear = key_linear.astype(jnp.bfloat16)
        value_rows = jnp.dot(normed, value_weight, preferred_element_type=jnp.float32)
        value_rows = value_rows.astype(jnp.bfloat16)
        key_rows = rotary(key_linear, cosine_table, sine_table).astype(jnp.bfloat16)
        queries = (rotary(query_linear, cosine_table, sine_table) * query_scale).astype(
            jnp.bfloat16
        )
        queries = queries.reshape(query_count, group_count, 2, HD)
        own_window = window_start
    previous_key, previous_value = from_behind((key_rows, value_rows), "seq", 1)
    all_keys = jnp.concatenate([previous_key, key_rows], axis=0).reshape(
        2 * block_length, group_count, HD
    )
    all_values = jnp.concatenate([previous_value, value_rows], axis=0).reshape(
        2 * block_length, group_count, HD
    )
    key_index = (block_index - 1) * block_length + jnp.arange(2 * block_length, dtype=jnp.int32)
    query_index = (
        block_index * block_length + query_first + jnp.arange(query_count, dtype=jnp.int32)
    )
    allowed = (key_index[None, :] <= query_index[:, None]) & (
        key_index[None, :] >= own_window[:, None]
    )
    attended = attend(queries, all_keys, all_values, allowed)
    head_walsh = walsh_table(HD).astype(jnp.bfloat16)
    rotated = jnp.einsum(
        "qgtd,de->qgte", attended, head_walsh, preferred_element_type=jnp.float32
    ) * float(HD) ** (-0.5)
    rotated = rotated.astype(jnp.bfloat16).reshape(query_count, -1)
    if paired:
        partner_rows = partner(output_weight, "mp", 0)
        full_output = join_pair(output_weight, partner_rows, low_bit, 0)
        half_term = jnp.dot(rotated, full_output, preferred_element_type=jnp.float32)
        padded = lax.dynamic_update_slice_in_dim(
            jnp.zeros((block_length, model_width), jnp.float32), half_term, query_first, 0
        )

        def attention_term(first_row, row_count):
            return lax.dynamic_slice_in_dim(padded, first_row, row_count, 0)

    else:

        def attention_term(first_row, row_count):
            picked = lax.dynamic_slice_in_dim(rotated, first_row, row_count, 0)
            return jnp.dot(picked, output_weight, preferred_element_type=jnp.float32)

    attention_rows = scatter_rows(attention_term(jnp.int32(0), lax.axis_size("mp") * own_rows))
    first_sum = (residual.astype(jnp.float32) + normalize(attention_rows, attention_gain)).astype(
        jnp.bfloat16
    )
    feed_own = normalize(first_sum, feedforward_gain).astype(jnp.bfloat16)
    feed_input = gather_rows(feed_own)
    local_count = WAL // model_count
    block_width = FF // WAL
    if own_rows % 16 == 0 and gate_weight.shape[1] % 384 == 0:
        gathered = hidden_rows(feed_input, gate_weight, up_weight)
        gathered = gathered.reshape(model_count, own_rows, local_count, block_width)
        exchanged = gathered.transpose(1, 0, 2, 3).reshape(own_rows, WAL, block_width)
    else:
        gate_out = jnp.dot(feed_input, gate_weight, preferred_element_type=jnp.float32)
        up_out = jnp.dot(feed_input, up_weight, preferred_element_type=jnp.float32)
        activated = (jax.nn.gelu(gate_out, approximate=True) * up_out).astype(jnp.bfloat16)
        grouped = activated.reshape(block_length, local_count, block_width)
        exchanged = lax.all_to_all(grouped, "mp", split_axis=0, concat_axis=1, tiled=True)
    walsh_scale = float(WAL) ** (-0.5)
    full_table = walsh_table(WAL).astype(jnp.bfloat16)
    mixed_rows = (
        jnp.einsum(
            "rab,ac->rcb",
            exchanged,
            full_table,
            preferred_element_type=jnp.float32,
        )
        * walsh_scale
    )
    spread = lax.all_to_all(
        mixed_rows.astype(jnp.bfloat16), "mp", split_axis=1, concat_axis=0, tiled=True
    )
    spread = spread.reshape(block_length, -1)
    picked = spread
    down_rows = scatter_rows(jnp.dot(picked, down_weight, preferred_element_type=jnp.float32))
    return (first_sum.astype(jnp.float32) + normalize(down_rows, output_gain)).astype(jnp.bfloat16)


def solution(mesh):
    placed = (
        P(("groups", "seq", "mp"), None),
        P(("groups", "seq")),
        P(("groups", "seq")),
        P(),
        P(),
        P(),
        P(),
        P(None, "mp"),
        P(None, "mp"),
        P(None, "mp"),
        P("mp", None),
        P(None, "mp"),
        P(None, "mp"),
        P("mp", None),
    )
    return jax.shard_map(
        body,
        mesh=mesh,
        in_specs=placed,
        out_specs=P(("groups", "seq", "mp"), None),
        check_vma=False,
    )
```

```python
import functools

import jax
import jax.numpy as jnp
from jax import lax
from jax.experimental import pallas as pl
from jax.experimental.pallas import tpu as pltpu
from jax.sharding import PartitionSpec as P

D = 5376
FF = 21504
QH = 32
HD = 128
WAL = 64


epsilon = 1e-06


MESH = pl.DeviceIdType.MESH


def block_of(ref, index, rows):
    return ref.at[pl.ds(pl.multiple_of(index * rows, rows), rows)]


def send(source, target, send_sem, recv_sem, device):
    return pltpu.make_async_remote_copy(
        src_ref=source,
        dst_ref=target,
        send_sem=send_sem,
        recv_sem=recv_sem,
        device_id={"mp": device},
        device_id_type=MESH,
    )


def place(count):
    me = lax.axis_index("mp")
    column = lax.rem(me, 2)
    line = lax.div(me, 2)
    return me, column, line, count // 2, me + 1 - 2 * column


def greet(me, line, lines, peer):
    barrier = pltpu.get_barrier_semaphore()
    pl.semaphore_signal(barrier, inc=1, device_id={"mp": peer}, device_id_type=MESH)

    @pl.when(line > 0)
    def _():
        pl.semaphore_signal(barrier, inc=1, device_id={"mp": me - 2}, device_id_type=MESH)

    @pl.when(line < lines - 1)
    def _():
        pl.semaphore_signal(barrier, inc=1, device_id={"mp": me + 2}, device_id_type=MESH)

    beside = jnp.minimum(line, 1) + jnp.minimum(lines - 1 - line, 1)
    pl.semaphore_wait(barrier, 1 + beside)


def gather_kernel(count, own_ref, all_ref, xs, xr, us, ur, ds, dr):
    rows = own_ref.shape[0]
    me, column, line, lines, peer = place(count)
    greet(me, line, lines, peer)

    def across(origin, source):
        there = block_of(all_ref, origin * 2 + column, rows)
        return send(source, there, xs.at[origin], xr.at[origin], peer)

    def upward(origin, source):
        there = block_of(all_ref, origin * 2 + column, rows)
        return send(source, there, us.at[origin], ur.at[origin], me + 2)

    def downward(origin, source):
        there = block_of(all_ref, origin * 2 + column, rows)
        return send(source, there, ds.at[origin], dr.at[origin], me - 2)

    @pl.when(line < lines - 1)
    def _():
        upward(line, own_ref).start()

    @pl.when(line > 0)
    def _():
        downward(line, own_ref).start()

    across(line, own_ref).start()
    all_ref[pl.ds(pl.multiple_of(me * rows, rows), rows), :] = own_ref[...]
    for step in range(1, lines):

        @pl.when(line - step >= 0)
        def _():
            origin = line - step
            held = block_of(all_ref, origin * 2 + column, rows)
            upward(origin, held).wait_recv()

            @pl.when(line < lines - 1)
            def _():
                upward(origin, held).start()

            across(origin, held).start()

        @pl.when(line + step < lines)
        def _():
            origin = line + step
            held = block_of(all_ref, origin * 2 + column, rows)
            downward(origin, held).wait_recv()

            @pl.when(line > 0)
            def _():
                downward(origin, held).start()

            across(origin, held).start()

    for origin in range(lines):
        across(origin, own_ref).wait_send()
        there = block_of(all_ref, origin * 2 + 1 - column, rows)
        send(own_ref, there, xs.at[origin], xr.at[origin], peer).wait_recv()

        @pl.when((origin <= line) & (line < lines - 1))
        def _():
            upward(origin, own_ref).wait_send()

        @pl.when((origin >= line) & (line > 0))
        def _():
            downward(origin, own_ref).wait_send()


def gather_rows(own):
    count = lax.axis_size("mp")
    rows, width = own.shape
    if rows % 16 or count % 2 or count < 4:
        return lax.all_gather(own, "mp", axis=0, tiled=True)
    lines = count // 2
    return pl.pallas_call(
        functools.partial(gather_kernel, count),
        out_shape=jax.ShapeDtypeStruct((count * rows, width), own.dtype),
        in_specs=[pl.BlockSpec(memory_space=pltpu.VMEM)],
        out_specs=pl.BlockSpec(memory_space=pltpu.VMEM),
        scratch_shapes=[pltpu.SemaphoreType.DMA((lines,))] * 6,
        compiler_params=pltpu.CompilerParams(
            collective_id=0, has_side_effects=True, vmem_limit_bytes=16 * 1024 * 1024
        ),
    )(own)


def scatter_kernel(count, term_ref, sum_ref, xb, ub, db, sb, xs, xr, us, ur, ds, dr):
    rows, width = sum_ref.shape
    me, column, line, lines, peer = place(count)
    step_width = 768 if width % 768 == 0 else 128
    greet(me, line, lines, peer)

    def across(dest):
        mine = block_of(term_ref, dest * 2 + 1 - column, rows)
        return send(mine, xb.at[dest], xs.at[dest], xr.at[dest], peer)

    def upward(dest):
        return send(sb.at[dest], ub.at[dest], us.at[dest], ur.at[dest], me + 2)

    def downward(dest):
        return send(sb.at[dest], db.at[dest], ds.at[dest], dr.at[dest], me - 2)

    for away in range(lines - 1, -1, -1):

        @pl.when(line - away >= 0)
        def _():
            across(line - away).start()

        if away:

            @pl.when(line + away < lines)
            def _():
                across(line + away).start()

    def add(dest, arrived, target, index):
        first = pl.multiple_of((dest * 2 + column) * rows, rows)

        def some(i, carry):
            cols = pl.ds(pl.multiple_of(i * step_width, step_width), step_width)
            total = term_ref[pl.ds(first, rows), cols].astype(jnp.float32)
            total = total + xb[dest, :, cols].astype(jnp.float32)
            for ref in arrived:
                total = total + ref[dest, :, cols].astype(jnp.float32)
            if index:
                target[dest, :, cols] = total.astype(target.dtype)
            else:
                target[:, cols] = total
            return carry

        lax.fori_loop(0, width // step_width, some, 0)

    def go_up(dest):
        @pl.when(dest > line)
        def _():
            across(dest).wait_recv()

            @pl.when(line > 0)
            def _():
                upward(dest).wait_recv()
                add(dest, (ub,), sb, True)

            @pl.when(line == 0)
            def _():
                add(dest, (), sb, True)

            upward(dest).start()

    def go_down(dest):
        @pl.when(dest < line)
        def _():
            across(dest).wait_recv()

            @pl.when(line < lines - 1)
            def _():
                downward(dest).wait_recv()
                add(dest, (db,), sb, True)

            @pl.when(line == lines - 1)
            def _():
                add(dest, (), sb, True)

            downward(dest).start()

    for j in range(lines - 1):

        @pl.when(2 * line < lines)
        def _():
            go_up(lines - 1 - j)
            go_down(j)

        @pl.when(2 * line >= lines)
        def _():
            go_down(j)
            go_up(lines - 1 - j)

    across(line).wait_recv()

    @pl.when(line > 0)
    def _():
        upward(line).wait_recv()

    @pl.when(line < lines - 1)
    def _():
        downward(line).wait_recv()

    @pl.when((line > 0) & (line < lines - 1))
    def _():
        add(line, (ub, db), sum_ref, False)

    @pl.when(line == 0)
    def _():
        add(line, (db,), sum_ref, False)

    @pl.when(line == lines - 1)
    def _():
        add(line, (ub,), sum_ref, False)

    for dest in range(lines):
        across(dest).wait_send()

        @pl.when(dest > line)
        def _():
            upward(dest).wait_send()

        @pl.when(dest < line)
        def _():
            downward(dest).wait_send()


def scatter_rows(term):
    count = lax.axis_size("mp")
    rows, width = term.shape[0] // count, term.shape[1]
    if rows % 16 or count % 2 or count < 4:
        return lax.psum_scatter(term, "mp", scatter_dimension=0, tiled=True)
    lines = count // 2
    blocks = pltpu.VMEM((lines, rows, width), jnp.bfloat16)
    return pl.pallas_call(
        functools.partial(scatter_kernel, count),
        out_shape=jax.ShapeDtypeStruct((rows, width), jnp.float32),
        in_specs=[pl.BlockSpec(memory_space=pltpu.VMEM)],
        out_specs=pl.BlockSpec(memory_space=pltpu.VMEM),
        scratch_shapes=[blocks] * 4 + [pltpu.SemaphoreType.DMA((lines,))] * 6,
        compiler_params=pltpu.CompilerParams(
            collective_id=1, has_side_effects=True, vmem_limit_bytes=24 * 1024 * 1024
        ),
    )(term.astype(jnp.bfloat16))


def hidden_kernel(count, tiles, feed_ref, gate_ref, up_ref, out_ref, act, got, ss, rs):
    rows = feed_ref.shape[0] // count
    width = gate_ref.shape[1]
    tile = pl.program_id(0)
    me = lax.axis_index("mp")

    @pl.when(tile == 0)
    def _():
        barrier = pltpu.get_barrier_semaphore()
        for k in range(1, count):
            other = lax.rem(me + k, count)
            pl.semaphore_signal(barrier, inc=1, device_id={"mp": other}, device_id_type=MESH)
        pl.semaphore_wait(barrier, count - 1)

    feed = feed_ref[...]
    gate_out = jnp.dot(feed, gate_ref[...], preferred_element_type=jnp.float32)
    up_out = jnp.dot(feed, up_ref[...], preferred_element_type=jnp.float32)
    act[tile] = (jax.nn.gelu(gate_out, approximate=True) * up_out).astype(jnp.bfloat16)

    def to(k, t):
        other = lax.rem(me + k, count)
        source = act.at[t, pl.ds(pl.multiple_of(other * rows, rows), rows), :]
        target = got.at[t, pl.ds(pl.multiple_of(me * rows, rows), rows), :]
        return send(source, target, ss.at[k, t], rs.at[k, t], other)

    for k in range(1, count):
        to(k, tile).start()
    own = pl.ds(pl.multiple_of(me * rows, rows), rows)
    got[tile, own, :] = act[tile, own, :]

    @pl.when(tile == tiles - 1)
    def _():
        for t in range(tiles):
            for k in range(1, count):
                to(k, t).wait_recv()
            out_ref[:, t * width : (t + 1) * width] = got[t]
        for t in range(tiles):
            for k in range(1, count):
                to(k, t).wait_send()


def hidden_rows(feed, gate_weight, up_weight):
    count = lax.axis_size("mp")
    length, depth = feed.shape
    hidden = gate_weight.shape[1]
    rows, tile = length // count, 384
    tiles = hidden // tile
    weights = pl.BlockSpec((depth, tile), lambda t: (0, t))
    return pl.pallas_call(
        functools.partial(hidden_kernel, count, tiles),
        grid=(tiles,),
        out_shape=jax.ShapeDtypeStruct((length, hidden), jnp.bfloat16),
        in_specs=[pl.BlockSpec((length, depth), lambda t: (0, 0)), weights, weights],
        out_specs=pl.BlockSpec((length, hidden), lambda t: (0, 0)),
        scratch_shapes=[
            pltpu.VMEM((tiles, length, tile), jnp.bfloat16),
            pltpu.VMEM((tiles, length, tile), jnp.bfloat16),
            pltpu.SemaphoreType.DMA((count, tiles)),
            pltpu.SemaphoreType.DMA((count, tiles)),
        ],
        compiler_params=pltpu.CompilerParams(
            collective_id=2,
            has_side_effects=True,
            dimension_semantics=("arbitrary",),
            vmem_limit_bytes=48 * 1024 * 1024,
        ),
    )(feed, gate_weight, up_weight)


PART = 256
STRIPE = 3 * PART
CYCLE = 7
LAG = 4
SUM_LAG = 3
SLOTS = 5


def is_paired(c):
    return lax.rem(c, CYCLE) == CYCLE // 2


def signal_to(device):
    barrier = pltpu.get_barrier_semaphore()
    pl.semaphore_signal(barrier, inc=1, device_id={"mp": device}, device_id_type=MESH)


def row_scale(read, parts, width):
    total = read(0) * read(0)
    for c in range(1, parts):
        total = total + read(c) * read(c)
    return lax.rsqrt(jnp.sum(total, axis=-1, keepdims=True) / width + epsilon)


def columns_of(c, width):
    return pl.ds(pl.multiple_of(c * width, width), width)


def wait_for(ref, sem, device):
    send(ref, ref, sem, sem, device).wait_recv()


def wait_sent(ref, sem, device):
    send(ref, ref, sem, sem, device).wait_send()


class Gather:
    def __init__(self, count, rows, buf, sems):
        self.buf, self.rows = buf, rows
        self.xs, self.ps, self.us, self.ds, self.xr, self.zr = sems
        self.parts = buf.shape[0]
        self.me, self.column, self.line, self.lines, self.peer = place(count)

    def block(self, c, origin, column):
        first, rows = origin * 2, self.rows
        if column is None:
            rows = 2 * rows
        else:
            first = first + column
        first = pl.multiple_of(first * self.rows, rows)
        return self.buf.at[c, pl.ds(first, rows), :]

    def across(self, c, origin, sem):
        there = self.block(c, origin, self.column)
        return send(there, there, sem.at[0], self.xr.at[c], self.peer)

    def upward(self, c, origin, both):
        there = self.block(c, origin, None if both else self.column)
        return send(there, there, self.us.at[0], self.zr.at[c, origin], self.me + 2)

    def downward(self, c, origin, both):
        there = self.block(c, origin, None if both else self.column)
        return send(there, there, self.ds.at[0], self.zr.at[c, origin], self.me - 2)

    def valid(self, c):
        return (c >= 0) & (c < self.parts)

    def both_ways(self, c, both):
        @pl.when(self.line < self.lines - 1)
        def _():
            self.upward(c, self.line, both).start()

        @pl.when(self.line > 0)
        def _():
            self.downward(c, self.line, both).start()

    def relay(self, c, away, both):
        line, lines = self.line, self.lines

        @pl.when(line - away >= 0)
        def _():
            self.upward(c, line - away, both).wait_recv()

            @pl.when(line < lines - 1)
            def _():
                self.upward(c, line - away, both).start()

            if not both:
                self.across(c, line - away, self.xs).start()

        @pl.when(line + away < lines)
        def _():
            self.downward(c, line + away, both).wait_recv()

            @pl.when(line > 0)
            def _():
                self.downward(c, line + away, both).start()

            if not both:
                self.across(c, line + away, self.xs).start()

    def open(self):
        def one(c, carry):
            @pl.when(jnp.logical_not(is_paired(c)))
            def _():
                self.both_ways(c, False)
                self.across(c, self.line, self.xs).start()

            @pl.when(is_paired(c))
            def _():
                self.across(c, self.line, self.ps).start()

            return carry

        lax.fori_loop(0, self.parts, one, 0)

    def behind(self):
        return LAG * (self.lines - 1)

    def step(self, t):
        line, lines = self.line, self.lines

        @pl.when(self.valid(t) & is_paired(t))
        def _():
            wait_for(self.block(t, line, 1 - self.column), self.xr.at[t], self.peer)
            self.both_ways(t, True)

        for away in range(1, lines):
            c = t - (away - 1) * LAG

            @pl.when(self.valid(c) & jnp.logical_not(is_paired(c)))
            def _():
                self.relay(c, away, False)

            late = c - LAG

            @pl.when(self.valid(late) & is_paired(late))
            def _():
                self.relay(late, away, True)

    def arrived(self, c):
        @pl.when(jnp.logical_not(is_paired(c)))
        def _():
            wait_for(self.buf.at[c, 0 : self.lines * self.rows, :], self.xr.at[c], self.peer)

    def finish(self):
        line, lines, parts = self.line, self.lines, self.parts
        pairs = parts // CYCLE
        share = (parts + pairs) * self.rows // self.buf.shape[1]
        half = lines * self.rows
        wait_sent(self.buf.at[0 : parts - pairs, 0:half, :], self.xs.at[0], self.peer)
        wait_sent(self.buf.at[0:pairs, 0 : self.rows, :], self.ps.at[0], self.peer)
        for at in range(lines):

            @pl.when(line == at)
            def _():
                if at < lines - 1:
                    wait_sent(self.buf.at[0 : share * (at + 1)], self.us.at[0], self.peer)
                if at > 0:
                    wait_sent(self.buf.at[0 : share * (lines - at)], self.ds.at[0], self.peer)


class Scatter:
    def __init__(self, count, rows, term, xb, ub, db, sb, up, dp, sp, sums, sems):
        self.term, self.xb, self.ub, self.db, self.sb, self.sums = term, xb, ub, db, sb, sums
        self.up, self.dp, self.sp = up, dp, sp
        self.rows = rows
        self.xs, self.ps, self.us, self.ds, self.xr, self.xo, self.ur, self.dr = sems
        self.parts = term.shape[0]
        self.me, self.column, self.line, self.lines, self.peer = place(count)

    def mine(self, dest, column):
        return pl.ds(pl.multiple_of((dest * 2 + column) * self.rows, self.rows), self.rows)

    def across(self, c, dest, arrive):
        source = self.term.at[c, self.mine(dest, 1 - self.column), :]
        return send(source, self.xb.at[c, dest], self.xs.at[0], arrive.at[c], self.peer)

    def across_total(self, c):
        there, source = self.xb.at[c, self.line], self.sb.at[c, self.line]
        return send(source, there, self.ps.at[0], self.xr.at[c], self.peer)

    def slot(self, c, both):
        return lax.div(c, CYCLE) if both else c

    def upward(self, c, dest, both):
        at = self.slot(c, both)
        source, there = (self.sp, self.up) if both else (self.sb, self.ub)
        return send(
            source.at[at, dest], there.at[at, dest], self.us.at[0], self.ur.at[c], self.me + 2
        )

    def downward(self, c, dest, both):
        at = self.slot(c, both)
        source, there = (self.sp, self.dp) if both else (self.sb, self.db)
        return send(
            source.at[at, dest], there.at[at, dest], self.ds.at[0], self.dr.at[c], self.me - 2
        )

    def total(self, c, dest, arrived, both):
        if both:
            here = pl.ds(pl.multiple_of(dest * 2 * self.rows, 2 * self.rows), 2 * self.rows)
            total = self.term[c, here, :].astype(jnp.float32)
        else:
            total = self.term[c, self.mine(dest, self.column), :].astype(jnp.float32)
            total = total + self.xb[c, dest].astype(jnp.float32)
        for ref in arrived:
            total = total + ref[self.slot(c, both), dest].astype(jnp.float32)
        return total

    def pass_up(self, c, both):
        line, lines = self.line, self.lines
        ub = self.up if both else self.ub
        to = self.sp if both else self.sb
        at = self.slot(c, both)
        for here in range(lines):

            @pl.when(line == here)
            def _():
                if here:
                    wait_for(ub.at[at, here:lines], self.ur.at[c], self.peer)
                for dest in range(lines - 1, here, -1):
                    total = self.total(c, dest, (ub,) if here else (), both)
                    to[at, dest] = total.astype(to.dtype)
                    self.upward(c, dest, both).start()

    def pass_down(self, c, both):
        line, lines = self.line, self.lines
        db = self.dp if both else self.db
        to = self.sp if both else self.sb
        at = self.slot(c, both)
        for here in range(lines):

            @pl.when(line == here)
            def _():
                last = here == lines - 1
                if not last:
                    wait_for(db.at[at, 0 : here + 1], self.dr.at[c], self.peer)
                for dest in range(here):
                    total = self.total(c, dest, () if last else (db,), both)
                    to[at, dest] = total.astype(to.dtype)
                    self.downward(c, dest, both).start()

    def settle(self, c, both):
        line, lines = self.line, self.lines
        ub, db = (self.up, self.dp) if both else (self.ub, self.db)
        if not both:
            wait_for(self.xb.at[c, line], self.xo.at[c], self.peer)

        def store(arrived):
            total = self.total(c, line, arrived, both)
            if not both:
                self.sums[c] = total
                return
            own, other = total[: self.rows], total[self.rows :]

            @pl.when(self.column == 0)
            def _():
                self.sums[c] = own
                self.sb[c, line] = other.astype(self.sb.dtype)

            @pl.when(self.column == 1)
            def _():
                self.sums[c] = other
                self.sb[c, line] = own.astype(self.sb.dtype)

        @pl.when(line == 0)
        def _():
            store((db,))

        @pl.when(line == lines - 1)
        def _():
            store((ub,))

        @pl.when((line > 0) & (line < lines - 1))
        def _():
            store((ub, db))

        if both:
            self.across_total(c).start()

    def run(self, produce):
        line, lines, parts = self.line, self.lines, self.parts

        def valid(c, both):
            paired = is_paired(c)
            return (c >= 0) & (c < parts) & (paired if both else jnp.logical_not(paired))

        def step(t, carry):
            @pl.when(t < parts)
            def _():
                produce(t)

            @pl.when(valid(t, False))
            def _():
                for away in range(lines - 1, 0, -1):

                    @pl.when(line - away >= 0)
                    def _():
                        self.across(t, line - away, self.xr).start()

                    @pl.when(line + away < lines)
                    def _():
                        self.across(t, line + away, self.xr).start()

            near = t - SUM_LAG * (lines - 1)

            @pl.when(valid(near, False))
            def _():
                self.across(near, line, self.xo).start()

            first = t - SUM_LAG

            @pl.when(valid(first, False))
            def _():
                wait_for(self.xb.at[first, 0 : lines - 1], self.xr.at[first], self.peer)

            cu, cd, c = t - SUM_LAG * (1 + line), t - SUM_LAG * (lines - line), t - SUM_LAG * lines
            for both in (False, True):

                @pl.when(valid(cu, both))
                def _():
                    self.pass_up(cu, both)

                @pl.when(valid(cd, both))
                def _():
                    self.pass_down(cd, both)

                @pl.when(valid(c, both))
                def _():
                    self.settle(c, both)

            late = c - SUM_LAG

            @pl.when(valid(late, True))
            def _():
                wait_for(self.xb.at[late, line], self.xr.at[late], self.peer)
                self.sums[late] += self.xb[late, line].astype(jnp.float32)

            return carry

        lax.fori_loop(0, parts + SUM_LAG * (lines + 1), step, 0)
        pairs = parts // CYCLE
        share = (parts + pairs) * self.rows // self.term.shape[1]
        half = lines * self.rows
        wait_sent(self.term.at[0 : parts - pairs, 0:half, :], self.xs.at[0], self.peer)
        wait_sent(self.xb.at[0:pairs, 0], self.ps.at[0], self.peer)
        for at in range(lines):

            @pl.when(line == at)
            def _():
                if at < lines - 1:
                    wait_sent(self.term.at[0 : share * (lines - 1 - at)], self.us.at[0], self.peer)
                if at > 0:
                    wait_sent(self.term.at[0 : share * at], self.ds.at[0], self.peer)


def butterfly(values):
    values = list(values)
    apart = 1
    while apart < len(values):
        for low in range(len(values)):
            if low // apart % 2 == 0:
                a, b = values[low], values[low + apart]
                values[low], values[low + apart] = a + b, a - b
        apart *= 2
    return values


def layer_kernel(
    count, blocks, head, scale, resid, tables, in_gain, att_gain, feed_gain, out_gain,
    wq, wk, wv, wo, wg, wu, wd, out_ref,
    rot, pairs_own, pairs_all, term, xb, ub, db, sb, up, dp, sp, sums, first, feed, gu, acc,
    act, got, mixed, spread, spun, dbuf,
    w_sem, wo_sem, gu_sem, d_sem, kv_sem, a_send, a_recv, b_send, b_recv, *sems,
):
    rows, width = resid.shape
    parts, length, part = feed.shape
    hidden = wg.shape[1]
    slots, d_slots = gu.shape[0], dbuf.shape[0]
    halves = rows // 16
    local = blocks // count
    inner = hidden // local
    stripes = width // STRIPE
    scatter = Scatter(count, 16, term, xb, ub, db, sb, up, dp, sp, sums, sems[:8])
    gather = Gather(count, rows, feed, sems[8:])
    me, lines, peer = scatter.me, scatter.lines, scatter.peer
    seq = lax.axis_index("seq")
    spans = ((wq, 0), (wk, wq.shape[1]), (wv, wq.shape[1] + wk.shape[1]))
    joint = wq.shape[1] + wk.shape[1] + wv.shape[1]
    held = gu.shape[2] // joint

    def joint_columns(c):
        return pl.ds(pl.multiple_of(lax.rem(c, held) * joint, 128), joint)

    def load_joint(c, carry):
        slot, start = lax.div(c, held), lax.rem(c, held) * joint
        for source, at in spans:
            target = gu.at[slot, :, pl.ds(pl.multiple_of(start + at, 128), source.shape[1])]
            copy = source.at[columns_of(c, part), :]
            pltpu.make_async_copy(copy, target, w_sem.at[c]).start()
        return carry

    deep = wo.shape[0]
    layers = hidden // deep

    def wo_part(c):
        first = pl.multiple_of(lax.rem(c, layers) * deep, deep)
        return dbuf.at[lax.div(c, layers), pl.ds(first, deep), :]

    def load_wo(c):
        return pltpu.make_async_copy(wo.at[:, columns_of(c, STRIPE)], wo_part(c), wo_sem.at[c])

    def load_gu(c):
        slot = lax.rem(c, slots)
        for i, source in enumerate((wg, wu)):
            target = gu.at[slot, :, i * hidden : (i + 1) * hidden]
            copy = source.at[columns_of(c, part), :]
            pltpu.make_async_copy(copy, target, gu_sem.at[slot]).start()

    def load_d(c):
        slot, cols = lax.rem(c, d_slots), columns_of(lax.rem(c, stripes), STRIPE)
        return pltpu.make_async_copy(wd.at[:, cols], dbuf.at[slot], d_sem.at[slot])

    for k in range(1, count):
        signal_to(lax.rem(me + k, count))
    barrier = pltpu.get_barrier_semaphore()
    pl.semaphore_signal(barrier, inc=1, device_id={"seq": 1 - seq}, device_id_type=MESH)
    lax.fori_loop(0, parts, load_joint, 0)

    own = pl.ds(pl.multiple_of(me * rows, rows), rows)

    def read(c):
        return resid[:, c * part : (c + 1) * part].astype(jnp.float32)

    in_scale = row_scale(read, parts, width)
    for c in range(parts):
        normed = read(c) * in_scale * in_gain[c * part : (c + 1) * part]
        feed[c, own, :] = normed.astype(feed.dtype)
    pl.semaphore_wait(barrier, count)

    def project_step(t, carry):
        gather.step(t)
        c = t - gather.behind()

        @pl.when(t == 0)
        def _():
            acc[:, 0:joint] = jnp.zeros((length, joint), jnp.float32)

        @pl.when(c >= 0)
        def _():
            weight = gu.at[lax.div(c, held), :, joint_columns(c)]
            pltpu.make_async_copy(weight, weight, w_sem.at[c]).wait()
            gather.arrived(c)
            acc[:, 0:joint] += jnp.dot(feed[c], weight[...], preferred_element_type=jnp.float32)

        return carry

    gather.open()
    lax.fori_loop(0, parts + gather.behind(), project_step, 0)
    gather.finish()
    for c in range(slots):
        load_gu(c)
    for c in range(stripes):
        load_wo(c).start()

    def head_rows(first, n):
        at = first + n * head
        return acc[:, at : at + head].astype(jnp.bfloat16).astype(jnp.float32)

    def rope(value):
        return value * tables[0] + pltpu.roll(value, head // 2, 1) * tables[1]

    groups = wk.shape[1] // head
    for g in range(groups):
        lanes = slice(g * head, (g + 1) * head)
        pairs_own[0, :, lanes] = rope(head_rows(spans[1][1], g)).astype(pairs_own.dtype)
        pairs_own[1, :, lanes] = head_rows(spans[2][1], g).astype(pairs_own.dtype)

    there = pairs_all.at[:, 0:length, :]
    exchange = pltpu.make_async_remote_copy(
        src_ref=pairs_own,
        dst_ref=there,
        send_sem=kv_sem.at[0],
        recv_sem=kv_sem.at[1],
        device_id={"seq": 1 - seq},
        device_id_type=MESH,
    )

    @pl.when(seq == 0)
    def _():
        exchange.start()
        pairs_all[:, 0:length, :] = jnp.zeros((2, length, groups * head), pairs_all.dtype)

    pairs_all[:, length : 2 * length, :] = pairs_own[...]
    query = lax.broadcasted_iota(jnp.int32, (length, 2 * length), 0) + seq * length
    key = lax.broadcasted_iota(jnp.int32, (length, 2 * length), 1) + (seq - 1) * length
    allowed = (key <= query) & (key.astype(jnp.float32) >= tables[2, :, 0:1])
    table = walsh_table(head).astype(jnp.bfloat16)

    @pl.when(seq == 1)
    def _():
        exchange.wait_recv()

    for n in range(wq.shape[1] // head):
        lanes = slice(n // 2 * head, (n // 2 + 1) * head)
        queries = (rope(head_rows(0, n)) * scale).astype(jnp.bfloat16)
        scores = lax.dot_general(
            queries,
            pairs_all[0, :, lanes],
            (((1,), (1,)), ((), ())),
            preferred_element_type=jnp.float32,
        )
        scores = jnp.where(allowed, scores, -1e30)
        exponent = jnp.exp(scores - jnp.max(scores, axis=-1, keepdims=True))
        probabilities = exponent / jnp.sum(exponent, axis=-1, keepdims=True)
        attended = jnp.dot(
            probabilities.astype(jnp.bfloat16),
            pairs_all[1, :, lanes],
            preferred_element_type=jnp.float32,
        )
        rotated = jnp.dot(
            attended.astype(jnp.bfloat16), table, preferred_element_type=jnp.float32
        )
        rotated = rotated * float(head) ** (-0.5)
        rotated = rotated.astype(rot.dtype)
        for d in range(count):
            for h in range(halves):
                piece = rotated[d * rows + h * 16 : d * rows + h * 16 + 16]
                rot[h, d * 16 : d * 16 + 16, n * head : (n + 1) * head] = piece

    @pl.when(seq == 0)
    def _():
        exchange.wait_send()

    tile = 384

    def attention_part(t):
        h, c = lax.div(t, stripes), lax.rem(t, stripes)

        @pl.when(h == 0)
        def _():
            load_wo(c).wait()

        value = jnp.dot(rot[h], wo_part(c)[...], preferred_element_type=jnp.float32)
        term[t] = value.astype(term.dtype)

        @pl.when(t == halves * stripes - 1)
        def _():
            for c in range(d_slots):
                load_d(c).start()

    scatter.run(attention_part)

    def at(h):
        return slice(h * 16, h * 16 + 16)

    def stripe(c):
        return slice(c * STRIPE, (c + 1) * STRIPE)

    for h in range(halves):
        att_scale = row_scale(lambda c: sums[h * stripes + c], stripes, width)
        for c in range(stripes):
            value = sums[h * stripes + c] * att_scale * att_gain[stripe(c)]
            value = resid[at(h), stripe(c)].astype(jnp.float32) + value
            first[c, at(h), :] = value.astype(first.dtype)
        feed_scale = row_scale(
            lambda c: first[c, at(h), :].astype(jnp.float32), stripes, width
        )
        own_half = pl.ds(pl.multiple_of(me * rows + h * 16, 16), 16)
        for c in range(stripes):
            value = first[c, at(h), :].astype(jnp.float32) * feed_scale * feed_gain[stripe(c)]
            value = value.astype(feed.dtype)
            for i in range(STRIPE // part):
                piece = value[:, i * part : (i + 1) * part]
                feed[c * (STRIPE // part) + i, own_half, :] = piece

    def feed_step(t, carry):
        gather.step(t)
        c = t - gather.behind()

        @pl.when(t == 0)
        def _():
            acc[...] = jnp.zeros_like(acc)

        @pl.when(c >= 0)
        def _():
            slot = lax.rem(c, slots)
            pltpu.make_async_copy(gu.at[slot], gu.at[slot], gu_sem.at[slot]).wait()
            gather.arrived(c)
            acc[...] += jnp.dot(feed[c], gu[slot], preferred_element_type=jnp.float32)

            @pl.when(c + slots < parts)
            def _():
                load_gu(c + slots)

        return carry

    gather.open()
    lax.fori_loop(0, parts + gather.behind(), feed_step, 0)

    def half_rows(device, h):
        return pl.ds(pl.multiple_of(device * rows + h * 16, 16), 16)

    def to_mixer(h, k):
        other = lax.rem(me + k, count)
        source, there = act.at[half_rows(other, h), :], got.at[me, pl.ds(h * 16, 16), :]
        return send(source, there, a_send.at[h], a_recv.at[h], other)

    def from_mixer(h, k):
        other = lax.rem(me + k, count)
        source, there = spread.at[other, pl.ds(h * 16, 16), :], spun.at[h, spun_rows, :]
        return send(source, there, b_send.at[h], b_recv.at[h], other)

    spun_rows = pl.ds(pl.multiple_of(me * 16, 16), 16)
    others = got.at[0 : count - 1, 0:16, :]
    for h in range(halves):

        def activate(k, carry):
            here = half_rows(lax.rem(me + k, count), h)

            def some(n, carry):
                cols = columns_of(n, tile)
                beside = pl.ds(pl.multiple_of(hidden + n * tile, 128), tile)
                value = jax.nn.gelu(acc[here, cols], approximate=True) * acc[here, beside]
                act[here, cols] = value.astype(act.dtype)
                return carry

            lax.fori_loop(0, hidden // tile, some, 0)

            @pl.when(k < count)
            def _():
                to_mixer(h, k).start()

            return carry

        lax.fori_loop(1, count + 1, activate, 0)
        got[me, h * 16 : h * 16 + 16, :] = act[half_rows(me, h), :]

    for h in range(halves):
        wait_for(others, a_recv.at[h], peer)

        def over_devices(n, carry):
            cols = columns_of(n, tile)
            held = [got[d, h * 16 : h * 16 + 16, cols].astype(jnp.float32) for d in range(count)]
            for d, value in enumerate(butterfly(held)):
                mixed[d, :, cols] = value
            return carry

        lax.fori_loop(0, hidden // tile, over_devices, 0)

        def within(k, carry):
            other = lax.rem(me + k, count)
            value = mixed[other]
            pieces = [value[:, a * inner : (a + 1) * inner] for a in range(local)]
            whole = jnp.concatenate(butterfly(pieces), axis=1) * float(blocks) ** (-0.5)
            spread[other, h * 16 : h * 16 + 16, :] = whole.astype(spread.dtype)

            @pl.when(k < count)
            def _():
                from_mixer(h, k).start()

            return carry

        lax.fori_loop(1, count + 1, within, 0)
        spun[h, spun_rows, :] = spread[me, h * 16 : h * 16 + 16, :]

    def down_part(t):
        for h in range(halves):

            @pl.when(t == h * stripes)
            def _():
                wait_for(others, b_recv.at[h], peer)

        load_d(t).wait()
        weight = dbuf[lax.rem(t, d_slots)]
        value = jnp.dot(spun[lax.div(t, stripes)], weight, preferred_element_type=jnp.float32)
        term[t] = value.astype(term.dtype)

        @pl.when(t + d_slots < halves * stripes)
        def _():
            load_d(t + d_slots).start()

    scatter.run(down_part)
    for h in range(halves):
        out_scale = row_scale(lambda c: sums[h * stripes + c], stripes, width)
        for c in range(stripes):
            value = sums[h * stripes + c] * out_scale * out_gain[stripe(c)]
            value = first[c, at(h), :].astype(jnp.float32) + value
            out_ref[at(h), stripe(c)] = value.astype(out_ref.dtype)

    gather.finish()
    for h in range(halves):
        wait_sent(others, a_send.at[h], peer)
        wait_sent(others, b_send.at[h], peer)


def fused_layer(residual, tables, gains, weights, blocks, head, scale):
    count = lax.axis_size("mp")
    rows, width = residual.shape
    part = PART
    parts, lines, length = width // part, count // 2, count * rows
    query_weight, key_weight, _, _, gate_weight, _, _ = weights
    hidden, kept = gate_weight.shape[1], key_weight.shape[1]
    slots, d_slots, halves = SLOTS, 2, rows // 16
    vmem = pl.BlockSpec(memory_space=pltpu.VMEM)
    hbm = pl.BlockSpec(memory_space=pltpu.HBM)
    bf16, f32 = jnp.bfloat16, jnp.float32
    stripes = width // STRIPE
    shares = halves * stripes
    block = pltpu.VMEM((shares, lines, 16, STRIPE), bf16)
    paired = pltpu.VMEM((shares // CYCLE, lines, 32, STRIPE), bf16)
    dma = pltpu.SemaphoreType.DMA
    return pl.pallas_call(
        functools.partial(layer_kernel, count, blocks, head, scale),
        out_shape=jax.ShapeDtypeStruct((rows, width), residual.dtype),
        in_specs=[vmem] * 6 + [hbm] * 7,
        out_specs=vmem,
        scratch_shapes=[
            pltpu.VMEM((halves, count * 16, query_weight.shape[1]), bf16),
            pltpu.VMEM((2, length, kept), bf16),
            pltpu.VMEM((2, 2 * length, kept), bf16),
            pltpu.VMEM((shares, count * 16, STRIPE), bf16),
            block,
            block,
            block,
            block,
            paired,
            paired,
            paired,
            pltpu.VMEM((shares, 16, STRIPE), f32),
            pltpu.VMEM((stripes, rows, STRIPE), bf16),
            pltpu.VMEM((parts, length, part), bf16),
            pltpu.VMEM((slots, part, 2 * hidden), bf16),
            pltpu.VMEM((length, 2 * hidden), f32),
            pltpu.VMEM((length, hidden), bf16),
            pltpu.VMEM((count, rows, hidden), bf16),
            pltpu.VMEM((count, 16, hidden), f32),
            pltpu.VMEM((count, rows, hidden), bf16),
            pltpu.VMEM((halves, count * 16, hidden), bf16),
            pltpu.VMEM((d_slots, hidden, STRIPE), bf16),
            dma((parts,)),
            dma((width // STRIPE,)),
            dma((slots,)),
            dma((d_slots,)),
            dma((2,)),
        ]
        + [dma((halves,))] * 4
        + [dma((1,))] * 4
        + [dma((shares,))] * 4
        + [dma((1,))] * 4
        + [dma((parts,)), dma((parts, lines))],
        compiler_params=pltpu.CompilerParams(
            collective_id=4, has_side_effects=True, vmem_limit_bytes=56 * 1024 * 1024
        ),
    )(residual, tables, *gains, *weights)


def partner(block, axis, apart):
    count = lax.axis_size(axis)
    route = []
    for low in range(count):
        high = low | 1 << apart
        if high != low and high < count:
            route += [(low, high), (high, low)]
    return lax.ppermute(block, axis, route)


def for_sending(value):
    return jax.tree.map(lambda a: a.astype(jnp.bfloat16) if a.dtype == jnp.float32 else a, value)


def from_behind(block, axis, distance):
    devices = range(lax.axis_size(axis))
    route = [(i - distance, i) for i in devices if i - distance in devices]
    return lax.ppermute(block, axis, route)


def normalize(values_in, gain_row):
    widened = values_in.astype(jnp.float32)
    mean_square = jnp.mean(widened * widened, axis=-1, keepdims=True)
    return widened * lax.rsqrt(mean_square + epsilon) * gain_row


def walsh_table(length):
    row_index = lax.broadcasted_iota(jnp.int32, (length, length), 0)
    column_index = lax.broadcasted_iota(jnp.int32, (length, length), 1)
    common = jnp.bitwise_and(row_index, column_index)
    parity = jnp.zeros((length, length), jnp.int32)
    for offset in range(max(length.bit_length() - 1, 0)):
        parity = parity + jnp.bitwise_and(jnp.right_shift(common, offset), 1)
    return (1 - 2 * jnp.bitwise_and(parity, 1)).astype(jnp.float32)


def angle_tables(positions, head_size):
    half_size = head_size // 2
    inverse = jnp.power(10000.0, -jnp.arange(half_size, dtype=jnp.float32) / half_size)
    angles = positions.astype(jnp.float32)[:, None] * inverse[None, :]
    return (jnp.cos(angles), jnp.sin(angles))


def rotary(linear, cosine_table, sine_table):
    row_count = linear.shape[0]
    half_size = cosine_table.shape[1]
    split_heads = linear.astype(jnp.float32).reshape(row_count, -1, 2 * half_size)
    front_half = split_heads[:, :, :half_size]
    back_half = split_heads[:, :, half_size:]
    cos_rows = cosine_table[:, None, :]
    sin_rows = sine_table[:, None, :]
    turned = jnp.concatenate(
        [
            front_half * cos_rows - back_half * sin_rows,
            back_half * cos_rows + front_half * sin_rows,
        ],
        axis=-1,
    )
    return turned.reshape(row_count, -1)


def join_pair(own_part, theirs, upper_bit, axis_number):
    lower_part = jnp.where(upper_bit == 1, theirs, own_part)
    upper_part = jnp.where(upper_bit == 1, own_part, theirs)
    return jnp.concatenate([lower_part, upper_part], axis=axis_number)


def attend(queries, key_rows, value_rows, allowed):
    scores = jnp.einsum("qgtd,kgd->gtqk", queries, key_rows, preferred_element_type=jnp.float32)
    scores = jnp.where(allowed[None, None], scores, -1e30)
    largest = jnp.max(scores, axis=-1, keepdims=True)
    exponent = jnp.exp(scores - largest)
    probabilities = (exponent / jnp.sum(exponent, axis=-1, keepdims=True)).astype(jnp.bfloat16)
    combined = jnp.einsum(
        "gtqk,kgd->qgtd", probabilities, value_rows, preferred_element_type=jnp.float32
    )
    return combined.astype(jnp.bfloat16)


def body(
    residual,
    positions,
    window_start,
    input_gain,
    attention_gain,
    feedforward_gain,
    output_gain,
    query_weight,
    key_weight,
    value_weight,
    output_weight,
    gate_weight,
    up_weight,
    down_weight,
):
    model_count = lax.axis_size("mp")
    model_index = lax.axis_index("mp")
    block_index = lax.axis_index("seq")
    own_rows, model_width = residual.shape
    block_length = own_rows * model_count
    joint = query_weight.shape[1] + key_weight.shape[1] + value_weight.shape[1]
    fused = (
        own_rows % 16 == 0
        and model_count == 8
        and lax.axis_size("seq") == 2
        and query_weight.shape[1] == 2 * key_weight.shape[1]
        and joint % 128 == 0
        and model_width // PART <= SLOTS * (2 * gate_weight.shape[1] // joint)
        and gate_weight.shape[1] % 384 == 0
        and model_width % (CYCLE * STRIPE) == 0
        and model_width // STRIPE <= 2 * (gate_weight.shape[1] // output_weight.shape[0])
    )
    if fused:
        cosine_table, sine_table = angle_tables(positions, HD)
        return fused_layer(
            residual,
            jnp.stack(
                [
                    jnp.concatenate([cosine_table, cosine_table], axis=1),
                    jnp.concatenate([-sine_table, sine_table], axis=1),
                    jnp.broadcast_to(
                        window_start[:, None].astype(jnp.float32), (block_length, HD)
                    ),
                ]
            ),
            (input_gain, attention_gain, feedforward_gain, output_gain),
            (
                query_weight,
                key_weight,
                value_weight,
                output_weight,
                gate_weight,
                up_weight,
                down_weight,
            ),
            WAL,
            HD,
            float(D // QH) ** (-0.5),
        )
    block_input = gather_rows(residual)
    normed = normalize(block_input, input_gain).astype(jnp.bfloat16)
    cosine_table, sine_table = angle_tables(positions, HD)
    query_scale = float(D // QH) ** (-0.5)
    paired = model_count == 2 * QH
    if paired:
        half_rows = block_length // 2
        quarter_rows = block_length // 4
        low_bit = model_index % 2
        query_first = low_bit * half_rows
        query_cosine = lax.dynamic_slice_in_dim(cosine_table, query_first, half_rows, 0)
        query_sine = lax.dynamic_slice_in_dim(sine_table, query_first, half_rows, 0)
        partner_columns = partner(query_weight, "mp", 0)
        full_query = join_pair(query_weight, partner_columns, low_bit, 1)
        query_normed = lax.dynamic_slice_in_dim(normed, query_first, half_rows, 0)
        query_linear = jnp.dot(query_normed, full_query, preferred_element_type=jnp.float32).astype(
            jnp.bfloat16
        )
        key_full = key_weight
        value_full = value_weight
        for bit_number in range(2):
            upper_bit = jnp.right_shift(model_index, bit_number) % 2
            partner_key, partner_value = (
                partner(for_sending(key_full), "mp", bit_number).astype(key_full.dtype),
                partner(for_sending(value_full), "mp", bit_number).astype(value_full.dtype),
            )
            key_full = join_pair(key_full, partner_key, upper_bit, 1)
            value_full = join_pair(value_full, partner_value, upper_bit, 1)
        quarter_first = model_index % 4 * quarter_rows
        quarter_normed = lax.dynamic_slice_in_dim(normed, quarter_first, quarter_rows, 0)
        quarter_cosine = lax.dynamic_slice_in_dim(cosine_table, quarter_first, quarter_rows, 0)
        quarter_sine = lax.dynamic_slice_in_dim(sine_table, quarter_first, quarter_rows, 0)
        key_linear = jnp.dot(quarter_normed, key_full, preferred_element_type=jnp.float32).astype(
            jnp.bfloat16
        )
        key_part = rotary(key_linear, quarter_cosine, quarter_sine).astype(jnp.bfloat16)
        value_part = jnp.dot(quarter_normed, value_full, preferred_element_type=jnp.float32).astype(
            jnp.bfloat16
        )
        for bit_number in range(2):
            upper_bit = jnp.right_shift(model_index, bit_number) % 2
            partner_key, partner_value = (
                partner(for_sending(key_part), "mp", bit_number).astype(key_part.dtype),
                partner(for_sending(value_part), "mp", bit_number).astype(value_part.dtype),
            )
            key_part = join_pair(key_part, partner_key, upper_bit, 0)
            value_part = join_pair(value_part, partner_value, upper_bit, 0)
        key_rows = key_part
        value_rows = value_part
        group_count = 1
        query_count = half_rows
        queries = (rotary(query_linear, query_cosine, query_sine) * query_scale).astype(
            jnp.bfloat16
        )
        queries = queries.reshape(query_count, 1, 1, HD)
        own_window = lax.dynamic_slice_in_dim(window_start, query_first, half_rows, 0)
    else:
        query_first = 0
        query_count = block_length
        group_count = key_weight.shape[1] // HD
        query_linear = jnp.dot(normed, query_weight, preferred_element_type=jnp.float32)
        query_linear = query_linear.astype(jnp.bfloat16)
        key_linear = jnp.dot(normed, key_weight, preferred_element_type=jnp.float32)
        key_linear = key_linear.astype(jnp.bfloat16)
        value_rows = jnp.dot(normed, value_weight, preferred_element_type=jnp.float32)
        value_rows = value_rows.astype(jnp.bfloat16)
        key_rows = rotary(key_linear, cosine_table, sine_table).astype(jnp.bfloat16)
        queries = (rotary(query_linear, cosine_table, sine_table) * query_scale).astype(
            jnp.bfloat16
        )
        queries = queries.reshape(query_count, group_count, 2, HD)
        own_window = window_start
    previous_key, previous_value = from_behind((key_rows, value_rows), "seq", 1)
    all_keys = jnp.concatenate([previous_key, key_rows], axis=0).reshape(
        2 * block_length, group_count, HD
    )
    all_values = jnp.concatenate([previous_value, value_rows], axis=0).reshape(
        2 * block_length, group_count, HD
    )
    key_index = (block_index - 1) * block_length + jnp.arange(2 * block_length, dtype=jnp.int32)
    query_index = (
        block_index * block_length + query_first + jnp.arange(query_count, dtype=jnp.int32)
    )
    allowed = (key_index[None, :] <= query_index[:, None]) & (
        key_index[None, :] >= own_window[:, None]
    )
    attended = attend(queries, all_keys, all_values, allowed)
    head_walsh = walsh_table(HD).astype(jnp.bfloat16)
    rotated = jnp.einsum(
        "qgtd,de->qgte", attended, head_walsh, preferred_element_type=jnp.float32
    ) * float(HD) ** (-0.5)
    rotated = rotated.astype(jnp.bfloat16).reshape(query_count, -1)
    if paired:
        partner_rows = partner(output_weight, "mp", 0)
        full_output = join_pair(output_weight, partner_rows, low_bit, 0)
        half_term = jnp.dot(rotated, full_output, preferred_element_type=jnp.float32)
        padded = lax.dynamic_update_slice_in_dim(
            jnp.zeros((block_length, model_width), jnp.float32), half_term, query_first, 0
        )

        def attention_term(first_row, row_count):
            return lax.dynamic_slice_in_dim(padded, first_row, row_count, 0)

    else:

        def attention_term(first_row, row_count):
            picked = lax.dynamic_slice_in_dim(rotated, first_row, row_count, 0)
            return jnp.dot(picked, output_weight, preferred_element_type=jnp.float32)

    attention_rows = scatter_rows(attention_term(jnp.int32(0), lax.axis_size("mp") * own_rows))
    first_sum = (residual.astype(jnp.float32) + normalize(attention_rows, attention_gain)).astype(
        jnp.bfloat16
    )
    feed_own = normalize(first_sum, feedforward_gain).astype(jnp.bfloat16)
    feed_input = gather_rows(feed_own)
    local_count = WAL // model_count
    block_width = FF // WAL
    if own_rows % 16 == 0 and gate_weight.shape[1] % 384 == 0:
        gathered = hidden_rows(feed_input, gate_weight, up_weight)
        gathered = gathered.reshape(model_count, own_rows, local_count, block_width)
        exchanged = gathered.transpose(1, 0, 2, 3).reshape(own_rows, WAL, block_width)
    else:
        gate_out = jnp.dot(feed_input, gate_weight, preferred_element_type=jnp.float32)
        up_out = jnp.dot(feed_input, up_weight, preferred_element_type=jnp.float32)
        activated = (jax.nn.gelu(gate_out, approximate=True) * up_out).astype(jnp.bfloat16)
        grouped = activated.reshape(block_length, local_count, block_width)
        exchanged = lax.all_to_all(grouped, "mp", split_axis=0, concat_axis=1, tiled=True)
    walsh_scale = float(WAL) ** (-0.5)
    full_table = walsh_table(WAL).astype(jnp.bfloat16)
    mixed_rows = (
        jnp.einsum(
            "rab,ac->rcb",
            exchanged,
            full_table,
            preferred_element_type=jnp.float32,
        )
        * walsh_scale
    )
    spread = lax.all_to_all(
        mixed_rows.astype(jnp.bfloat16), "mp", split_axis=1, concat_axis=0, tiled=True
    )
    spread = spread.reshape(block_length, -1)
    picked = spread
    down_rows = scatter_rows(jnp.dot(picked, down_weight, preferred_element_type=jnp.float32))
    return (first_sum.astype(jnp.float32) + normalize(down_rows, output_gain)).astype(jnp.bfloat16)


def solution(mesh):
    placed = (
        P(("groups", "seq", "mp"), None),
        P(("groups", "seq")),
        P(("groups", "seq")),
        P(),
        P(),
        P(),
        P(),
        P(None, "mp"),
        P(None, "mp"),
        P(None, "mp"),
        P("mp", None),
        P(None, "mp"),
        P(None, "mp"),
        P("mp", None),
    )
    return jax.shard_map(
        body,
        mesh=mesh,
        in_specs=placed,
        out_specs=P(("groups", "seq", "mp"), None),
        check_vma=False,
    )
```

```python
import functools

import jax
import jax.numpy as jnp
from jax import lax
from jax.experimental import pallas as pl
from jax.experimental.pallas import tpu as pltpu
from jax.sharding import PartitionSpec as P

D = 5376
FF = 21504
QH = 32
HD = 128
WAL = 64


epsilon = 1e-06


MESH = pl.DeviceIdType.MESH


def block_of(ref, index, rows):
    return ref.at[pl.ds(pl.multiple_of(index * rows, rows), rows)]


def send(source, target, send_sem, recv_sem, device):
    return pltpu.make_async_remote_copy(
        src_ref=source,
        dst_ref=target,
        send_sem=send_sem,
        recv_sem=recv_sem,
        device_id={"mp": device},
        device_id_type=MESH,
    )


def place(count):
    me = lax.axis_index("mp")
    column = lax.rem(me, 2)
    line = lax.div(me, 2)
    return me, column, line, count // 2, me + 1 - 2 * column


def greet(me, line, lines, peer):
    barrier = pltpu.get_barrier_semaphore()
    pl.semaphore_signal(barrier, inc=1, device_id={"mp": peer}, device_id_type=MESH)

    @pl.when(line > 0)
    def _():
        pl.semaphore_signal(barrier, inc=1, device_id={"mp": me - 2}, device_id_type=MESH)

    @pl.when(line < lines - 1)
    def _():
        pl.semaphore_signal(barrier, inc=1, device_id={"mp": me + 2}, device_id_type=MESH)

    beside = jnp.minimum(line, 1) + jnp.minimum(lines - 1 - line, 1)
    pl.semaphore_wait(barrier, 1 + beside)


def gather_kernel(count, own_ref, all_ref, xs, xr, us, ur, ds, dr):
    rows = own_ref.shape[0]
    me, column, line, lines, peer = place(count)
    greet(me, line, lines, peer)

    def across(origin, source):
        there = block_of(all_ref, origin * 2 + column, rows)
        return send(source, there, xs.at[origin], xr.at[origin], peer)

    def upward(origin, source):
        there = block_of(all_ref, origin * 2 + column, rows)
        return send(source, there, us.at[origin], ur.at[origin], me + 2)

    def downward(origin, source):
        there = block_of(all_ref, origin * 2 + column, rows)
        return send(source, there, ds.at[origin], dr.at[origin], me - 2)

    @pl.when(line < lines - 1)
    def _():
        upward(line, own_ref).start()

    @pl.when(line > 0)
    def _():
        downward(line, own_ref).start()

    across(line, own_ref).start()
    all_ref[pl.ds(pl.multiple_of(me * rows, rows), rows), :] = own_ref[...]
    for step in range(1, lines):

        @pl.when(line - step >= 0)
        def _():
            origin = line - step
            held = block_of(all_ref, origin * 2 + column, rows)
            upward(origin, held).wait_recv()

            @pl.when(line < lines - 1)
            def _():
                upward(origin, held).start()

            across(origin, held).start()

        @pl.when(line + step < lines)
        def _():
            origin = line + step
            held = block_of(all_ref, origin * 2 + column, rows)
            downward(origin, held).wait_recv()

            @pl.when(line > 0)
            def _():
                downward(origin, held).start()

            across(origin, held).start()

    for origin in range(lines):
        across(origin, own_ref).wait_send()
        there = block_of(all_ref, origin * 2 + 1 - column, rows)
        send(own_ref, there, xs.at[origin], xr.at[origin], peer).wait_recv()

        @pl.when((origin <= line) & (line < lines - 1))
        def _():
            upward(origin, own_ref).wait_send()

        @pl.when((origin >= line) & (line > 0))
        def _():
            downward(origin, own_ref).wait_send()


def gather_rows(own):
    count = lax.axis_size("mp")
    rows, width = own.shape
    if rows % 16 or count % 2 or count < 4:
        return lax.all_gather(own, "mp", axis=0, tiled=True)
    lines = count // 2
    return pl.pallas_call(
        functools.partial(gather_kernel, count),
        out_shape=jax.ShapeDtypeStruct((count * rows, width), own.dtype),
        in_specs=[pl.BlockSpec(memory_space=pltpu.VMEM)],
        out_specs=pl.BlockSpec(memory_space=pltpu.VMEM),
        scratch_shapes=[pltpu.SemaphoreType.DMA((lines,))] * 6,
        compiler_params=pltpu.CompilerParams(
            collective_id=0, has_side_effects=True, vmem_limit_bytes=16 * 1024 * 1024
        ),
    )(own)


def scatter_kernel(count, term_ref, sum_ref, xb, ub, db, sb, xs, xr, us, ur, ds, dr):
    rows, width = sum_ref.shape
    me, column, line, lines, peer = place(count)
    step_width = 768 if width % 768 == 0 else 128
    greet(me, line, lines, peer)

    def across(dest):
        mine = block_of(term_ref, dest * 2 + 1 - column, rows)
        return send(mine, xb.at[dest], xs.at[dest], xr.at[dest], peer)

    def upward(dest):
        return send(sb.at[dest], ub.at[dest], us.at[dest], ur.at[dest], me + 2)

    def downward(dest):
        return send(sb.at[dest], db.at[dest], ds.at[dest], dr.at[dest], me - 2)

    for away in range(lines - 1, -1, -1):

        @pl.when(line - away >= 0)
        def _():
            across(line - away).start()

        if away:

            @pl.when(line + away < lines)
            def _():
                across(line + away).start()

    def add(dest, arrived, target, index):
        first = pl.multiple_of((dest * 2 + column) * rows, rows)

        def some(i, carry):
            cols = pl.ds(pl.multiple_of(i * step_width, step_width), step_width)
            total = term_ref[pl.ds(first, rows), cols].astype(jnp.float32)
            total = total + xb[dest, :, cols].astype(jnp.float32)
            for ref in arrived:
                total = total + ref[dest, :, cols].astype(jnp.float32)
            if index:
                target[dest, :, cols] = total.astype(target.dtype)
            else:
                target[:, cols] = total
            return carry

        lax.fori_loop(0, width // step_width, some, 0)

    def go_up(dest):
        @pl.when(dest > line)
        def _():
            across(dest).wait_recv()

            @pl.when(line > 0)
            def _():
                upward(dest).wait_recv()
                add(dest, (ub,), sb, True)

            @pl.when(line == 0)
            def _():
                add(dest, (), sb, True)

            upward(dest).start()

    def go_down(dest):
        @pl.when(dest < line)
        def _():
            across(dest).wait_recv()

            @pl.when(line < lines - 1)
            def _():
                downward(dest).wait_recv()
                add(dest, (db,), sb, True)

            @pl.when(line == lines - 1)
            def _():
                add(dest, (), sb, True)

            downward(dest).start()

    for j in range(lines - 1):

        @pl.when(2 * line < lines)
        def _():
            go_up(lines - 1 - j)
            go_down(j)

        @pl.when(2 * line >= lines)
        def _():
            go_down(j)
            go_up(lines - 1 - j)

    across(line).wait_recv()

    @pl.when(line > 0)
    def _():
        upward(line).wait_recv()

    @pl.when(line < lines - 1)
    def _():
        downward(line).wait_recv()

    @pl.when((line > 0) & (line < lines - 1))
    def _():
        add(line, (ub, db), sum_ref, False)

    @pl.when(line == 0)
    def _():
        add(line, (db,), sum_ref, False)

    @pl.when(line == lines - 1)
    def _():
        add(line, (ub,), sum_ref, False)

    for dest in range(lines):
        across(dest).wait_send()

        @pl.when(dest > line)
        def _():
            upward(dest).wait_send()

        @pl.when(dest < line)
        def _():
            downward(dest).wait_send()


def scatter_rows(term):
    count = lax.axis_size("mp")
    rows, width = term.shape[0] // count, term.shape[1]
    if rows % 16 or count % 2 or count < 4:
        return lax.psum_scatter(term, "mp", scatter_dimension=0, tiled=True)
    lines = count // 2
    blocks = pltpu.VMEM((lines, rows, width), jnp.bfloat16)
    return pl.pallas_call(
        functools.partial(scatter_kernel, count),
        out_shape=jax.ShapeDtypeStruct((rows, width), jnp.float32),
        in_specs=[pl.BlockSpec(memory_space=pltpu.VMEM)],
        out_specs=pl.BlockSpec(memory_space=pltpu.VMEM),
        scratch_shapes=[blocks] * 4 + [pltpu.SemaphoreType.DMA((lines,))] * 6,
        compiler_params=pltpu.CompilerParams(
            collective_id=1, has_side_effects=True, vmem_limit_bytes=24 * 1024 * 1024
        ),
    )(term.astype(jnp.bfloat16))


def hidden_kernel(count, tiles, feed_ref, gate_ref, up_ref, out_ref, act, got, ss, rs):
    rows = feed_ref.shape[0] // count
    width = gate_ref.shape[1]
    tile = pl.program_id(0)
    me = lax.axis_index("mp")

    @pl.when(tile == 0)
    def _():
        barrier = pltpu.get_barrier_semaphore()
        for k in range(1, count):
            other = lax.rem(me + k, count)
            pl.semaphore_signal(barrier, inc=1, device_id={"mp": other}, device_id_type=MESH)
        pl.semaphore_wait(barrier, count - 1)

    feed = feed_ref[...]
    gate_out = jnp.dot(feed, gate_ref[...], preferred_element_type=jnp.float32)
    up_out = jnp.dot(feed, up_ref[...], preferred_element_type=jnp.float32)
    act[tile] = (jax.nn.gelu(gate_out, approximate=True) * up_out).astype(jnp.bfloat16)

    def to(k, t):
        other = lax.rem(me + k, count)
        source = act.at[t, pl.ds(pl.multiple_of(other * rows, rows), rows), :]
        target = got.at[t, pl.ds(pl.multiple_of(me * rows, rows), rows), :]
        return send(source, target, ss.at[k, t], rs.at[k, t], other)

    for k in range(1, count):
        to(k, tile).start()
    own = pl.ds(pl.multiple_of(me * rows, rows), rows)
    got[tile, own, :] = act[tile, own, :]

    @pl.when(tile == tiles - 1)
    def _():
        for t in range(tiles):
            for k in range(1, count):
                to(k, t).wait_recv()
            out_ref[:, t * width : (t + 1) * width] = got[t]
        for t in range(tiles):
            for k in range(1, count):
                to(k, t).wait_send()


def hidden_rows(feed, gate_weight, up_weight):
    count = lax.axis_size("mp")
    length, depth = feed.shape
    hidden = gate_weight.shape[1]
    rows, tile = length // count, 384
    tiles = hidden // tile
    weights = pl.BlockSpec((depth, tile), lambda t: (0, t))
    return pl.pallas_call(
        functools.partial(hidden_kernel, count, tiles),
        grid=(tiles,),
        out_shape=jax.ShapeDtypeStruct((length, hidden), jnp.bfloat16),
        in_specs=[pl.BlockSpec((length, depth), lambda t: (0, 0)), weights, weights],
        out_specs=pl.BlockSpec((length, hidden), lambda t: (0, 0)),
        scratch_shapes=[
            pltpu.VMEM((tiles, length, tile), jnp.bfloat16),
            pltpu.VMEM((tiles, length, tile), jnp.bfloat16),
            pltpu.SemaphoreType.DMA((count, tiles)),
            pltpu.SemaphoreType.DMA((count, tiles)),
        ],
        compiler_params=pltpu.CompilerParams(
            collective_id=2,
            has_side_effects=True,
            dimension_semantics=("arbitrary",),
            vmem_limit_bytes=48 * 1024 * 1024,
        ),
    )(feed, gate_weight, up_weight)


PART = 256
STRIPE = 3 * PART
CYCLE = 7
LAG = 4
SUM_LAG = 3
SLOTS = 5


def is_paired(c):
    return lax.rem(c, CYCLE) == CYCLE // 2


def signal_to(device):
    barrier = pltpu.get_barrier_semaphore()
    pl.semaphore_signal(barrier, inc=1, device_id={"mp": device}, device_id_type=MESH)


def row_scale(read, parts, width):
    total = read(0) * read(0)
    for c in range(1, parts):
        total = total + read(c) * read(c)
    return lax.rsqrt(jnp.sum(total, axis=-1, keepdims=True) / width + epsilon)


def columns_of(c, width):
    return pl.ds(pl.multiple_of(c * width, width), width)


def wait_for(ref, sem, device):
    send(ref, ref, sem, sem, device).wait_recv()


def wait_sent(ref, sem, device):
    send(ref, ref, sem, sem, device).wait_send()


class Gather:
    def __init__(self, count, rows, buf, sems):
        self.buf, self.rows = buf, rows
        self.xs, self.ps, self.us, self.ds, self.xr, self.zr = sems
        self.parts = buf.shape[0]
        self.me, self.column, self.line, self.lines, self.peer = place(count)

    def block(self, c, origin, column):
        first, rows = origin * 2, self.rows
        if column is None:
            rows = 2 * rows
        else:
            first = first + column
        first = pl.multiple_of(first * self.rows, rows)
        return self.buf.at[c, pl.ds(first, rows), :]

    def across(self, c, origin, sem):
        there = self.block(c, origin, self.column)
        return send(there, there, sem.at[0], self.xr.at[c], self.peer)

    def upward(self, c, origin, both):
        there = self.block(c, origin, None if both else self.column)
        return send(there, there, self.us.at[0], self.zr.at[c, origin], self.me + 2)

    def downward(self, c, origin, both):
        there = self.block(c, origin, None if both else self.column)
        return send(there, there, self.ds.at[0], self.zr.at[c, origin], self.me - 2)

    def valid(self, c):
        return (c >= 0) & (c < self.parts)

    def both_ways(self, c, both):
        @pl.when(self.line < self.lines - 1)
        def _():
            self.upward(c, self.line, both).start()

        @pl.when(self.line > 0)
        def _():
            self.downward(c, self.line, both).start()

    def relay(self, c, away, both):
        line, lines = self.line, self.lines

        @pl.when(line - away >= 0)
        def _():
            self.upward(c, line - away, both).wait_recv()

            @pl.when(line < lines - 1)
            def _():
                self.upward(c, line - away, both).start()

            if not both:
                self.across(c, line - away, self.xs).start()

        @pl.when(line + away < lines)
        def _():
            self.downward(c, line + away, both).wait_recv()

            @pl.when(line > 0)
            def _():
                self.downward(c, line + away, both).start()

            if not both:
                self.across(c, line + away, self.xs).start()

    def open(self):
        def one(c, carry):
            @pl.when(jnp.logical_not(is_paired(c)))
            def _():
                self.both_ways(c, False)
                self.across(c, self.line, self.xs).start()

            @pl.when(is_paired(c))
            def _():
                self.across(c, self.line, self.ps).start()

            return carry

        lax.fori_loop(0, self.parts, one, 0)

    def behind(self):
        return LAG * (self.lines - 1)

    def step(self, t):
        line, lines = self.line, self.lines

        @pl.when(self.valid(t) & is_paired(t))
        def _():
            wait_for(self.block(t, line, 1 - self.column), self.xr.at[t], self.peer)
            self.both_ways(t, True)

        for away in range(1, lines):
            c = t - (away - 1) * LAG

            @pl.when(self.valid(c) & jnp.logical_not(is_paired(c)))
            def _():
                self.relay(c, away, False)

            late = c - LAG

            @pl.when(self.valid(late) & is_paired(late))
            def _():
                self.relay(late, away, True)

    def arrived(self, c):
        @pl.when(jnp.logical_not(is_paired(c)))
        def _():
            wait_for(self.buf.at[c, 0 : self.lines * self.rows, :], self.xr.at[c], self.peer)

    def finish(self):
        line, lines, parts = self.line, self.lines, self.parts
        pairs = parts // CYCLE
        share = (parts + pairs) * self.rows // self.buf.shape[1]
        half = lines * self.rows
        wait_sent(self.buf.at[0 : parts - pairs, 0:half, :], self.xs.at[0], self.peer)
        wait_sent(self.buf.at[0:pairs, 0 : self.rows, :], self.ps.at[0], self.peer)
        for at in range(lines):

            @pl.when(line == at)
            def _():
                if at < lines - 1:
                    wait_sent(self.buf.at[0 : share * (at + 1)], self.us.at[0], self.peer)
                if at > 0:
                    wait_sent(self.buf.at[0 : share * (lines - at)], self.ds.at[0], self.peer)


class Scatter:
    def __init__(self, count, rows, term, xb, ub, db, sb, up, dp, sp, sums, sems):
        self.term, self.xb, self.ub, self.db, self.sb, self.sums = term, xb, ub, db, sb, sums
        self.up, self.dp, self.sp = up, dp, sp
        self.rows = rows
        self.xs, self.ps, self.us, self.ds, self.xr, self.xo, self.ur, self.dr = sems
        self.parts = term.shape[0]
        self.me, self.column, self.line, self.lines, self.peer = place(count)

    def mine(self, dest, column):
        return pl.ds(pl.multiple_of((dest * 2 + column) * self.rows, self.rows), self.rows)

    def across(self, c, dest, arrive):
        source = self.term.at[c, self.mine(dest, 1 - self.column), :]
        return send(source, self.xb.at[c, dest], self.xs.at[0], arrive.at[c], self.peer)

    def across_total(self, c):
        there, source = self.xb.at[c, self.line], self.sb.at[c, self.line]
        return send(source, there, self.ps.at[0], self.xr.at[c], self.peer)

    def slot(self, c, both):
        return lax.div(c, CYCLE) if both else c

    def upward(self, c, dest, both):
        at = self.slot(c, both)
        source, there = (self.sp, self.up) if both else (self.sb, self.ub)
        return send(
            source.at[at, dest], there.at[at, dest], self.us.at[0], self.ur.at[c], self.me + 2
        )

    def downward(self, c, dest, both):
        at = self.slot(c, both)
        source, there = (self.sp, self.dp) if both else (self.sb, self.db)
        return send(
            source.at[at, dest], there.at[at, dest], self.ds.at[0], self.dr.at[c], self.me - 2
        )

    def total(self, c, dest, arrived, both):
        if both:
            here = pl.ds(pl.multiple_of(dest * 2 * self.rows, 2 * self.rows), 2 * self.rows)
            total = self.term[c, here, :].astype(jnp.float32)
        else:
            total = self.term[c, self.mine(dest, self.column), :].astype(jnp.float32)
            total = total + self.xb[c, dest].astype(jnp.float32)
        for ref in arrived:
            total = total + ref[self.slot(c, both), dest].astype(jnp.float32)
        return total

    def pass_up(self, c, both):
        line, lines = self.line, self.lines
        ub = self.up if both else self.ub
        to = self.sp if both else self.sb
        at = self.slot(c, both)
        for here in range(lines):

            @pl.when(line == here)
            def _():
                if here:
                    wait_for(ub.at[at, here:lines], self.ur.at[c], self.peer)
                for dest in range(lines - 1, here, -1):
                    total = self.total(c, dest, (ub,) if here else (), both)
                    to[at, dest] = total.astype(to.dtype)
                    self.upward(c, dest, both).start()

    def pass_down(self, c, both):
        line, lines = self.line, self.lines
        db = self.dp if both else self.db
        to = self.sp if both else self.sb
        at = self.slot(c, both)
        for here in range(lines):

            @pl.when(line == here)
            def _():
                last = here == lines - 1
                if not last:
                    wait_for(db.at[at, 0 : here + 1], self.dr.at[c], self.peer)
                for dest in range(here):
                    total = self.total(c, dest, () if last else (db,), both)
                    to[at, dest] = total.astype(to.dtype)
                    self.downward(c, dest, both).start()

    def settle(self, c, both):
        line, lines = self.line, self.lines
        ub, db = (self.up, self.dp) if both else (self.ub, self.db)
        if not both:
            wait_for(self.xb.at[c, line], self.xo.at[c], self.peer)

        def store(arrived):
            total = self.total(c, line, arrived, both)
            if not both:
                self.sums[c] = total
                return
            own, other = total[: self.rows], total[self.rows :]

            @pl.when(self.column == 0)
            def _():
                self.sums[c] = own
                self.sb[c, line] = other.astype(self.sb.dtype)

            @pl.when(self.column == 1)
            def _():
                self.sums[c] = other
                self.sb[c, line] = own.astype(self.sb.dtype)

        @pl.when(line == 0)
        def _():
            store((db,))

        @pl.when(line == lines - 1)
        def _():
            store((ub,))

        @pl.when((line > 0) & (line < lines - 1))
        def _():
            store((ub, db))

        if both:
            self.across_total(c).start()

    def run(self, produce):
        line, lines, parts = self.line, self.lines, self.parts

        def valid(c, both):
            paired = is_paired(c)
            return (c >= 0) & (c < parts) & (paired if both else jnp.logical_not(paired))

        def step(t, carry):
            @pl.when(t < parts)
            def _():
                produce(t)

            @pl.when(valid(t, False))
            def _():
                for away in range(lines - 1, 0, -1):

                    @pl.when(line - away >= 0)
                    def _():
                        self.across(t, line - away, self.xr).start()

                    @pl.when(line + away < lines)
                    def _():
                        self.across(t, line + away, self.xr).start()

            near = t - SUM_LAG * (lines - 1)

            @pl.when(valid(near, False))
            def _():
                self.across(near, line, self.xo).start()

            first = t - SUM_LAG

            @pl.when(valid(first, False))
            def _():
                wait_for(self.xb.at[first, 0 : lines - 1], self.xr.at[first], self.peer)

            cu, cd, c = t - SUM_LAG * (1 + line), t - SUM_LAG * (lines - line), t - SUM_LAG * lines
            for both in (False, True):

                @pl.when(valid(cu, both))
                def _():
                    self.pass_up(cu, both)

                @pl.when(valid(cd, both))
                def _():
                    self.pass_down(cd, both)

                @pl.when(valid(c, both))
                def _():
                    self.settle(c, both)

            late = c - SUM_LAG

            @pl.when(valid(late, True))
            def _():
                wait_for(self.xb.at[late, line], self.xr.at[late], self.peer)
                self.sums[late] += self.xb[late, line].astype(jnp.float32)

            return carry

        lax.fori_loop(0, parts + SUM_LAG * (lines + 1), step, 0)
        pairs = parts // CYCLE
        share = (parts + pairs) * self.rows // self.term.shape[1]
        half = lines * self.rows
        wait_sent(self.term.at[0 : parts - pairs, 0:half, :], self.xs.at[0], self.peer)
        wait_sent(self.xb.at[0:pairs, 0], self.ps.at[0], self.peer)
        for at in range(lines):

            @pl.when(line == at)
            def _():
                if at < lines - 1:
                    wait_sent(self.term.at[0 : share * (lines - 1 - at)], self.us.at[0], self.peer)
                if at > 0:
                    wait_sent(self.term.at[0 : share * at], self.ds.at[0], self.peer)


def butterfly(values):
    values = list(values)
    apart = 1
    while apart < len(values):
        for low in range(len(values)):
            if low // apart % 2 == 0:
                a, b = values[low], values[low + apart]
                values[low], values[low + apart] = a + b, a - b
        apart *= 2
    return values


def layer_kernel(
    count, blocks, head, scale, resid, tables, in_gain, att_gain, feed_gain, out_gain,
    wq, wk, wv, wo, wg, wu, wd, out_ref,
    rot, pairs_own, pairs_all, term, xb, ub, db, sb, up, dp, sp, sums, first, feed, gu, acc,
    act, got, mixed, spread, spun, dbuf,
    w_sem, wo_sem, gu_sem, d_sem, kv_sem, a_send, a_recv, b_send, b_recv, *sems,
):
    rows, width = resid.shape
    parts, length, part = feed.shape
    hidden = wg.shape[1]
    slots, d_slots = gu.shape[0], dbuf.shape[0]
    halves = rows // 16
    local = blocks // count
    inner = hidden // local
    stripes = width // STRIPE
    scatter = Scatter(count, 16, term, xb, ub, db, sb, up, dp, sp, sums, sems[:8])
    gather = Gather(count, rows, feed, sems[8:])
    me, lines, peer = scatter.me, scatter.lines, scatter.peer
    seq = lax.axis_index("seq")
    spans = ((wq, 0), (wk, wq.shape[1]), (wv, wq.shape[1] + wk.shape[1]))
    joint = wq.shape[1] + wk.shape[1] + wv.shape[1]
    held = gu.shape[2] // joint

    def joint_columns(c):
        return pl.ds(pl.multiple_of(lax.rem(c, held) * joint, 128), joint)

    def load_joint(c, carry):
        slot, start = lax.div(c, held), lax.rem(c, held) * joint
        for source, at in spans:
            target = gu.at[slot, :, pl.ds(pl.multiple_of(start + at, 128), source.shape[1])]
            copy = source.at[columns_of(c, part), :]
            pltpu.make_async_copy(copy, target, w_sem.at[c]).start()
        return carry

    deep = wo.shape[0]
    layers = hidden // deep

    def wo_part(c):
        first = pl.multiple_of(lax.rem(c, layers) * deep, deep)
        return dbuf.at[lax.div(c, layers), pl.ds(first, deep), :]

    def load_wo(c):
        return pltpu.make_async_copy(wo.at[:, columns_of(c, STRIPE)], wo_part(c), wo_sem.at[c])

    def load_gu(c):
        slot = lax.rem(c, slots)
        for i, source in enumerate((wg, wu)):
            target = gu.at[slot, :, i * hidden : (i + 1) * hidden]
            copy = source.at[columns_of(c, part), :]
            pltpu.make_async_copy(copy, target, gu_sem.at[slot]).start()

    def load_d(c):
        slot, cols = lax.rem(c, d_slots), columns_of(lax.rem(c, stripes), STRIPE)
        return pltpu.make_async_copy(wd.at[:, cols], dbuf.at[slot], d_sem.at[slot])

    for k in range(1, count):
        signal_to(lax.rem(me + k, count))
    barrier = pltpu.get_barrier_semaphore()
    pl.semaphore_signal(barrier, inc=1, device_id={"seq": 1 - seq}, device_id_type=MESH)
    lax.fori_loop(0, parts, load_joint, 0)

    own = pl.ds(pl.multiple_of(me * rows, rows), rows)

    def read(c):
        return resid[:, c * part : (c + 1) * part].astype(jnp.float32)

    in_scale = row_scale(read, parts, width)
    for c in range(parts):
        normed = read(c) * in_scale * in_gain[c * part : (c + 1) * part]
        feed[c, own, :] = normed.astype(feed.dtype)
    pl.semaphore_wait(barrier, count)

    def project_step(t, carry):
        gather.step(t)
        c = t - gather.behind()

        @pl.when(t == 0)
        def _():
            acc[:, 0:joint] = jnp.zeros((length, joint), jnp.float32)

        @pl.when(c >= 0)
        def _():
            weight = gu.at[lax.div(c, held), :, joint_columns(c)]
            pltpu.make_async_copy(weight, weight, w_sem.at[c]).wait()
            gather.arrived(c)
            acc[:, 0:joint] += jnp.dot(feed[c], weight[...], preferred_element_type=jnp.float32)

        return carry

    gather.open()
    lax.fori_loop(0, parts + gather.behind(), project_step, 0)
    gather.finish()
    for c in range(slots):
        load_gu(c)
    for c in range(stripes):
        load_wo(c).start()

    def head_rows(first, n):
        at = first + n * head
        return acc[:, at : at + head].astype(jnp.bfloat16).astype(jnp.float32)

    def rope(value):
        return value * tables[0] + pltpu.roll(value, head // 2, 1) * tables[1]

    groups = wk.shape[1] // head
    for g in range(groups):
        lanes = slice(g * head, (g + 1) * head)
        pairs_own[0, :, lanes] = rope(head_rows(spans[1][1], g)).astype(pairs_own.dtype)
        pairs_own[1, :, lanes] = head_rows(spans[2][1], g).astype(pairs_own.dtype)

    there = pairs_all.at[:, 0:length, :]
    exchange = pltpu.make_async_remote_copy(
        src_ref=pairs_own,
        dst_ref=there,
        send_sem=kv_sem.at[0],
        recv_sem=kv_sem.at[1],
        device_id={"seq": 1 - seq},
        device_id_type=MESH,
    )

    @pl.when(seq == 0)
    def _():
        exchange.start()
        pairs_all[:, 0:length, :] = jnp.zeros((2, length, groups * head), pairs_all.dtype)

    pairs_all[:, length : 2 * length, :] = pairs_own[...]
    query = lax.broadcasted_iota(jnp.int32, (length, 2 * length), 0) + seq * length
    key = lax.broadcasted_iota(jnp.int32, (length, 2 * length), 1) + (seq - 1) * length
    allowed = (key <= query) & (key.astype(jnp.float32) >= tables[2, :, 0:1])
    table = walsh_table(head).astype(jnp.bfloat16)

    @pl.when(seq == 1)
    def _():
        exchange.wait_recv()

    for n in range(wq.shape[1] // head):
        lanes = slice(n // 2 * head, (n // 2 + 1) * head)
        queries = (rope(head_rows(0, n)) * scale).astype(jnp.bfloat16)
        scores = lax.dot_general(
            queries,
            pairs_all[0, :, lanes],
            (((1,), (1,)), ((), ())),
            preferred_element_type=jnp.float32,
        )
        scores = jnp.where(allowed, scores, -1e30)
        exponent = jnp.exp(scores - jnp.max(scores, axis=-1, keepdims=True))
        probabilities = exponent * (1.0 / jnp.sum(exponent, axis=-1, keepdims=True))
        attended = jnp.dot(
            probabilities.astype(jnp.bfloat16),
            pairs_all[1, :, lanes],
            preferred_element_type=jnp.float32,
        )
        rotated = jnp.dot(
            attended.astype(jnp.bfloat16), table, preferred_element_type=jnp.float32
        )
        rotated = rotated * float(head) ** (-0.5)
        rotated = rotated.astype(rot.dtype)
        for d in range(count):
            for h in range(halves):
                piece = rotated[d * rows + h * 16 : d * rows + h * 16 + 16]
                rot[h, d * 16 : d * 16 + 16, n * head : (n + 1) * head] = piece

    @pl.when(seq == 0)
    def _():
        exchange.wait_send()

    tile = 384

    def attention_part(t):
        h, c = lax.div(t, stripes), lax.rem(t, stripes)

        @pl.when(h == 0)
        def _():
            load_wo(c).wait()

        value = jnp.dot(rot[h], wo_part(c)[...], preferred_element_type=jnp.float32)
        term[t] = value.astype(term.dtype)

        @pl.when(t == halves * stripes - 1)
        def _():
            for c in range(d_slots):
                load_d(c).start()

    scatter.run(attention_part)

    def at(h):
        return slice(h * 16, h * 16 + 16)

    def stripe(c):
        return slice(c * STRIPE, (c + 1) * STRIPE)

    for h in range(halves):
        att_scale = row_scale(lambda c: sums[h * stripes + c], stripes, width)
        for c in range(stripes):
            value = sums[h * stripes + c] * att_scale * att_gain[stripe(c)]
            value = resid[at(h), stripe(c)].astype(jnp.float32) + value
            first[c, at(h), :] = value.astype(first.dtype)
        feed_scale = row_scale(
            lambda c: first[c, at(h), :].astype(jnp.float32), stripes, width
        )
        own_half = pl.ds(pl.multiple_of(me * rows + h * 16, 16), 16)
        for c in range(stripes):
            value = first[c, at(h), :].astype(jnp.float32) * feed_scale * feed_gain[stripe(c)]
            value = value.astype(feed.dtype)
            for i in range(STRIPE // part):
                piece = value[:, i * part : (i + 1) * part]
                feed[c * (STRIPE // part) + i, own_half, :] = piece

    def feed_step(t, carry):
        gather.step(t)
        c = t - gather.behind()

        @pl.when(t == 0)
        def _():
            acc[...] = jnp.zeros_like(acc)

        @pl.when(c >= 0)
        def _():
            slot = lax.rem(c, slots)
            pltpu.make_async_copy(gu.at[slot], gu.at[slot], gu_sem.at[slot]).wait()
            gather.arrived(c)
            acc[...] += jnp.dot(feed[c], gu[slot], preferred_element_type=jnp.float32)

            @pl.when(c + slots < parts)
            def _():
                load_gu(c + slots)

        return carry

    gather.open()
    lax.fori_loop(0, parts + gather.behind(), feed_step, 0)

    def half_rows(device, h):
        return pl.ds(pl.multiple_of(device * rows + h * 16, 16), 16)

    def to_mixer(h, k):
        other = lax.rem(me + k, count)
        source, there = act.at[half_rows(other, h), :], got.at[me, pl.ds(h * 16, 16), :]
        return send(source, there, a_send.at[h], a_recv.at[h], other)

    def from_mixer(h, k):
        other = lax.rem(me + k, count)
        source, there = spread.at[other, pl.ds(h * 16, 16), :], spun.at[h, spun_rows, :]
        return send(source, there, b_send.at[h], b_recv.at[h], other)

    spun_rows = pl.ds(pl.multiple_of(me * 16, 16), 16)
    others = got.at[0 : count - 1, 0:16, :]
    for h in range(halves):

        def activate(k, carry):
            here = half_rows(lax.rem(me + k, count), h)

            def some(n, carry):
                cols = columns_of(n, tile)
                beside = pl.ds(pl.multiple_of(hidden + n * tile, 128), tile)
                value = jax.nn.gelu(acc[here, cols], approximate=True) * acc[here, beside]
                act[here, cols] = value.astype(act.dtype)
                return carry

            lax.fori_loop(0, hidden // tile, some, 0)

            @pl.when(k < count)
            def _():
                to_mixer(h, k).start()

            return carry

        lax.fori_loop(1, count + 1, activate, 0)
        got[me, h * 16 : h * 16 + 16, :] = act[half_rows(me, h), :]

    for h in range(halves):
        wait_for(others, a_recv.at[h], peer)

        def over_devices(n, carry):
            cols = columns_of(n, tile)
            held = [got[d, h * 16 : h * 16 + 16, cols].astype(jnp.float32) for d in range(count)]
            for d, value in enumerate(butterfly(held)):
                mixed[d, :, cols] = value
            return carry

        lax.fori_loop(0, hidden // tile, over_devices, 0)

        def within(k, carry):
            other = lax.rem(me + k, count)
            value = mixed[other]
            pieces = [value[:, a * inner : (a + 1) * inner] for a in range(local)]
            whole = jnp.concatenate(butterfly(pieces), axis=1) * float(blocks) ** (-0.5)
            spread[other, h * 16 : h * 16 + 16, :] = whole.astype(spread.dtype)

            @pl.when(k < count)
            def _():
                from_mixer(h, k).start()

            return carry

        lax.fori_loop(1, count + 1, within, 0)
        spun[h, spun_rows, :] = spread[me, h * 16 : h * 16 + 16, :]

    def down_part(t):
        for h in range(halves):

            @pl.when(t == h * stripes)
            def _():
                wait_for(others, b_recv.at[h], peer)

        load_d(t).wait()
        weight = dbuf[lax.rem(t, d_slots)]
        value = jnp.dot(spun[lax.div(t, stripes)], weight, preferred_element_type=jnp.float32)
        term[t] = value.astype(term.dtype)

        @pl.when(t + d_slots < halves * stripes)
        def _():
            load_d(t + d_slots).start()

    scatter.run(down_part)
    for h in range(halves):
        out_scale = row_scale(lambda c: sums[h * stripes + c], stripes, width)
        for c in range(stripes):
            value = sums[h * stripes + c] * out_scale * out_gain[stripe(c)]
            value = first[c, at(h), :].astype(jnp.float32) + value
            out_ref[at(h), stripe(c)] = value.astype(out_ref.dtype)

    gather.finish()
    for h in range(halves):
        wait_sent(others, a_send.at[h], peer)
        wait_sent(others, b_send.at[h], peer)


def fused_layer(residual, tables, gains, weights, blocks, head, scale):
    count = lax.axis_size("mp")
    rows, width = residual.shape
    part = PART
    parts, lines, length = width // part, count // 2, count * rows
    query_weight, key_weight, _, _, gate_weight, _, _ = weights
    hidden, kept = gate_weight.shape[1], key_weight.shape[1]
    slots, d_slots, halves = SLOTS, 2, rows // 16
    vmem = pl.BlockSpec(memory_space=pltpu.VMEM)
    hbm = pl.BlockSpec(memory_space=pltpu.HBM)
    bf16, f32 = jnp.bfloat16, jnp.float32
    stripes = width // STRIPE
    shares = halves * stripes
    block = pltpu.VMEM((shares, lines, 16, STRIPE), bf16)
    paired = pltpu.VMEM((shares // CYCLE, lines, 32, STRIPE), bf16)
    dma = pltpu.SemaphoreType.DMA
    return pl.pallas_call(
        functools.partial(layer_kernel, count, blocks, head, scale),
        out_shape=jax.ShapeDtypeStruct((rows, width), residual.dtype),
        in_specs=[vmem] * 6 + [hbm] * 7,
        out_specs=vmem,
        scratch_shapes=[
            pltpu.VMEM((halves, count * 16, query_weight.shape[1]), bf16),
            pltpu.VMEM((2, length, kept), bf16),
            pltpu.VMEM((2, 2 * length, kept), bf16),
            pltpu.VMEM((shares, count * 16, STRIPE), bf16),
            block,
            block,
            block,
            block,
            paired,
            paired,
            paired,
            pltpu.VMEM((shares, 16, STRIPE), f32),
            pltpu.VMEM((stripes, rows, STRIPE), bf16),
            pltpu.VMEM((parts, length, part), bf16),
            pltpu.VMEM((slots, part, 2 * hidden), bf16),
            pltpu.VMEM((length, 2 * hidden), f32),
            pltpu.VMEM((length, hidden), bf16),
            pltpu.VMEM((count, rows, hidden), bf16),
            pltpu.VMEM((count, 16, hidden), f32),
            pltpu.VMEM((count, rows, hidden), bf16),
            pltpu.VMEM((halves, count * 16, hidden), bf16),
            pltpu.VMEM((d_slots, hidden, STRIPE), bf16),
            dma((parts,)),
            dma((width // STRIPE,)),
            dma((slots,)),
            dma((d_slots,)),
            dma((2,)),
        ]
        + [dma((halves,))] * 4
        + [dma((1,))] * 4
        + [dma((shares,))] * 4
        + [dma((1,))] * 4
        + [dma((parts,)), dma((parts, lines))],
        compiler_params=pltpu.CompilerParams(
            collective_id=4, has_side_effects=True, vmem_limit_bytes=56 * 1024 * 1024
        ),
    )(residual, tables, *gains, *weights)


def partner(block, axis, apart):
    count = lax.axis_size(axis)
    route = []
    for low in range(count):
        high = low | 1 << apart
        if high != low and high < count:
            route += [(low, high), (high, low)]
    return lax.ppermute(block, axis, route)


def for_sending(value):
    return jax.tree.map(lambda a: a.astype(jnp.bfloat16) if a.dtype == jnp.float32 else a, value)


def from_behind(block, axis, distance):
    devices = range(lax.axis_size(axis))
    route = [(i - distance, i) for i in devices if i - distance in devices]
    return lax.ppermute(block, axis, route)


def normalize(values_in, gain_row):
    widened = values_in.astype(jnp.float32)
    mean_square = jnp.mean(widened * widened, axis=-1, keepdims=True)
    return widened * lax.rsqrt(mean_square + epsilon) * gain_row


def walsh_table(length):
    row_index = lax.broadcasted_iota(jnp.int32, (length, length), 0)
    column_index = lax.broadcasted_iota(jnp.int32, (length, length), 1)
    common = jnp.bitwise_and(row_index, column_index)
    parity = jnp.zeros((length, length), jnp.int32)
    for offset in range(max(length.bit_length() - 1, 0)):
        parity = parity + jnp.bitwise_and(jnp.right_shift(common, offset), 1)
    return (1 - 2 * jnp.bitwise_and(parity, 1)).astype(jnp.float32)


def angle_tables(positions, head_size):
    half_size = head_size // 2
    inverse = jnp.power(10000.0, -jnp.arange(half_size, dtype=jnp.float32) / half_size)
    angles = positions.astype(jnp.float32)[:, None] * inverse[None, :]
    return (jnp.cos(angles), jnp.sin(angles))


def rotary(linear, cosine_table, sine_table):
    row_count = linear.shape[0]
    half_size = cosine_table.shape[1]
    split_heads = linear.astype(jnp.float32).reshape(row_count, -1, 2 * half_size)
    front_half = split_heads[:, :, :half_size]
    back_half = split_heads[:, :, half_size:]
    cos_rows = cosine_table[:, None, :]
    sin_rows = sine_table[:, None, :]
    turned = jnp.concatenate(
        [
            front_half * cos_rows - back_half * sin_rows,
            back_half * cos_rows + front_half * sin_rows,
        ],
        axis=-1,
    )
    return turned.reshape(row_count, -1)


def join_pair(own_part, theirs, upper_bit, axis_number):
    lower_part = jnp.where(upper_bit == 1, theirs, own_part)
    upper_part = jnp.where(upper_bit == 1, own_part, theirs)
    return jnp.concatenate([lower_part, upper_part], axis=axis_number)


def attend(queries, key_rows, value_rows, allowed):
    scores = jnp.einsum("qgtd,kgd->gtqk", queries, key_rows, preferred_element_type=jnp.float32)
    scores = jnp.where(allowed[None, None], scores, -1e30)
    largest = jnp.max(scores, axis=-1, keepdims=True)
    exponent = jnp.exp(scores - largest)
    probabilities = (exponent / jnp.sum(exponent, axis=-1, keepdims=True)).astype(jnp.bfloat16)
    combined = jnp.einsum(
        "gtqk,kgd->qgtd", probabilities, value_rows, preferred_element_type=jnp.float32
    )
    return combined.astype(jnp.bfloat16)


def body(
    residual,
    positions,
    window_start,
    input_gain,
    attention_gain,
    feedforward_gain,
    output_gain,
    query_weight,
    key_weight,
    value_weight,
    output_weight,
    gate_weight,
    up_weight,
    down_weight,
):
    model_count = lax.axis_size("mp")
    model_index = lax.axis_index("mp")
    block_index = lax.axis_index("seq")
    own_rows, model_width = residual.shape
    block_length = own_rows * model_count
    joint = query_weight.shape[1] + key_weight.shape[1] + value_weight.shape[1]
    fused = (
        own_rows % 16 == 0
        and model_count == 8
        and lax.axis_size("seq") == 2
        and query_weight.shape[1] == 2 * key_weight.shape[1]
        and joint % 128 == 0
        and model_width // PART <= SLOTS * (2 * gate_weight.shape[1] // joint)
        and gate_weight.shape[1] % 384 == 0
        and model_width % (CYCLE * STRIPE) == 0
        and model_width // STRIPE <= 2 * (gate_weight.shape[1] // output_weight.shape[0])
    )
    if fused:
        cosine_table, sine_table = angle_tables(positions, HD)
        return fused_layer(
            residual,
            jnp.stack(
                [
                    jnp.concatenate([cosine_table, cosine_table], axis=1),
                    jnp.concatenate([-sine_table, sine_table], axis=1),
                    jnp.broadcast_to(
                        window_start[:, None].astype(jnp.float32), (block_length, HD)
                    ),
                ]
            ),
            (input_gain, attention_gain, feedforward_gain, output_gain),
            (
                query_weight,
                key_weight,
                value_weight,
                output_weight,
                gate_weight,
                up_weight,
                down_weight,
            ),
            WAL,
            HD,
            float(D // QH) ** (-0.5),
        )
    block_input = gather_rows(residual)
    normed = normalize(block_input, input_gain).astype(jnp.bfloat16)
    cosine_table, sine_table = angle_tables(positions, HD)
    query_scale = float(D // QH) ** (-0.5)
    paired = model_count == 2 * QH
    if paired:
        half_rows = block_length // 2
        quarter_rows = block_length // 4
        low_bit = model_index % 2
        query_first = low_bit * half_rows
        query_cosine = lax.dynamic_slice_in_dim(cosine_table, query_first, half_rows, 0)
        query_sine = lax.dynamic_slice_in_dim(sine_table, query_first, half_rows, 0)
        partner_columns = partner(query_weight, "mp", 0)
        full_query = join_pair(query_weight, partner_columns, low_bit, 1)
        query_normed = lax.dynamic_slice_in_dim(normed, query_first, half_rows, 0)
        query_linear = jnp.dot(query_normed, full_query, preferred_element_type=jnp.float32).astype(
            jnp.bfloat16
        )
        key_full = key_weight
        value_full = value_weight
        for bit_number in range(2):
            upper_bit = jnp.right_shift(model_index, bit_number) % 2
            partner_key, partner_value = (
                partner(for_sending(key_full), "mp", bit_number).astype(key_full.dtype),
                partner(for_sending(value_full), "mp", bit_number).astype(value_full.dtype),
            )
            key_full = join_pair(key_full, partner_key, upper_bit, 1)
            value_full = join_pair(value_full, partner_value, upper_bit, 1)
        quarter_first = model_index % 4 * quarter_rows
        quarter_normed = lax.dynamic_slice_in_dim(normed, quarter_first, quarter_rows, 0)
        quarter_cosine = lax.dynamic_slice_in_dim(cosine_table, quarter_first, quarter_rows, 0)
        quarter_sine = lax.dynamic_slice_in_dim(sine_table, quarter_first, quarter_rows, 0)
        key_linear = jnp.dot(quarter_normed, key_full, preferred_element_type=jnp.float32).astype(
            jnp.bfloat16
        )
        key_part = rotary(key_linear, quarter_cosine, quarter_sine).astype(jnp.bfloat16)
        value_part = jnp.dot(quarter_normed, value_full, preferred_element_type=jnp.float32).astype(
            jnp.bfloat16
        )
        for bit_number in range(2):
            upper_bit = jnp.right_shift(model_index, bit_number) % 2
            partner_key, partner_value = (
                partner(for_sending(key_part), "mp", bit_number).astype(key_part.dtype),
                partner(for_sending(value_part), "mp", bit_number).astype(value_part.dtype),
            )
            key_part = join_pair(key_part, partner_key, upper_bit, 0)
            value_part = join_pair(value_part, partner_value, upper_bit, 0)
        key_rows = key_part
        value_rows = value_part
        group_count = 1
        query_count = half_rows
        queries = (rotary(query_linear, query_cosine, query_sine) * query_scale).astype(
            jnp.bfloat16
        )
        queries = queries.reshape(query_count, 1, 1, HD)
        own_window = lax.dynamic_slice_in_dim(window_start, query_first, half_rows, 0)
    else:
        query_first = 0
        query_count = block_length
        group_count = key_weight.shape[1] // HD
        query_linear = jnp.dot(normed, query_weight, preferred_element_type=jnp.float32)
        query_linear = query_linear.astype(jnp.bfloat16)
        key_linear = jnp.dot(normed, key_weight, preferred_element_type=jnp.float32)
        key_linear = key_linear.astype(jnp.bfloat16)
        value_rows = jnp.dot(normed, value_weight, preferred_element_type=jnp.float32)
        value_rows = value_rows.astype(jnp.bfloat16)
        key_rows = rotary(key_linear, cosine_table, sine_table).astype(jnp.bfloat16)
        queries = (rotary(query_linear, cosine_table, sine_table) * query_scale).astype(
            jnp.bfloat16
        )
        queries = queries.reshape(query_count, group_count, 2, HD)
        own_window = window_start
    previous_key, previous_value = from_behind((key_rows, value_rows), "seq", 1)
    all_keys = jnp.concatenate([previous_key, key_rows], axis=0).reshape(
        2 * block_length, group_count, HD
    )
    all_values = jnp.concatenate([previous_value, value_rows], axis=0).reshape(
        2 * block_length, group_count, HD
    )
    key_index = (block_index - 1) * block_length + jnp.arange(2 * block_length, dtype=jnp.int32)
    query_index = (
        block_index * block_length + query_first + jnp.arange(query_count, dtype=jnp.int32)
    )
    allowed = (key_index[None, :] <= query_index[:, None]) & (
        key_index[None, :] >= own_window[:, None]
    )
    attended = attend(queries, all_keys, all_values, allowed)
    head_walsh = walsh_table(HD).astype(jnp.bfloat16)
    rotated = jnp.einsum(
        "qgtd,de->qgte", attended, head_walsh, preferred_element_type=jnp.float32
    ) * float(HD) ** (-0.5)
    rotated = rotated.astype(jnp.bfloat16).reshape(query_count, -1)
    if paired:
        partner_rows = partner(output_weight, "mp", 0)
        full_output = join_pair(output_weight, partner_rows, low_bit, 0)
        half_term = jnp.dot(rotated, full_output, preferred_element_type=jnp.float32)
        padded = lax.dynamic_update_slice_in_dim(
            jnp.zeros((block_length, model_width), jnp.float32), half_term, query_first, 0
        )

        def attention_term(first_row, row_count):
            return lax.dynamic_slice_in_dim(padded, first_row, row_count, 0)

    else:

        def attention_term(first_row, row_count):
            picked = lax.dynamic_slice_in_dim(rotated, first_row, row_count, 0)
            return jnp.dot(picked, output_weight, preferred_element_type=jnp.float32)

    attention_rows = scatter_rows(attention_term(jnp.int32(0), lax.axis_size("mp") * own_rows))
    first_sum = (residual.astype(jnp.float32) + normalize(attention_rows, attention_gain)).astype(
        jnp.bfloat16
    )
    feed_own = normalize(first_sum, feedforward_gain).astype(jnp.bfloat16)
    feed_input = gather_rows(feed_own)
    local_count = WAL // model_count
    block_width = FF // WAL
    if own_rows % 16 == 0 and gate_weight.shape[1] % 384 == 0:
        gathered = hidden_rows(feed_input, gate_weight, up_weight)
        gathered = gathered.reshape(model_count, own_rows, local_count, block_width)
        exchanged = gathered.transpose(1, 0, 2, 3).reshape(own_rows, WAL, block_width)
    else:
        gate_out = jnp.dot(feed_input, gate_weight, preferred_element_type=jnp.float32)
        up_out = jnp.dot(feed_input, up_weight, preferred_element_type=jnp.float32)
        activated = (jax.nn.gelu(gate_out, approximate=True) * up_out).astype(jnp.bfloat16)
        grouped = activated.reshape(block_length, local_count, block_width)
        exchanged = lax.all_to_all(grouped, "mp", split_axis=0, concat_axis=1, tiled=True)
    walsh_scale = float(WAL) ** (-0.5)
    full_table = walsh_table(WAL).astype(jnp.bfloat16)
    mixed_rows = (
        jnp.einsum(
            "rab,ac->rcb",
            exchanged,
            full_table,
            preferred_element_type=jnp.float32,
        )
        * walsh_scale
    )
    spread = lax.all_to_all(
        mixed_rows.astype(jnp.bfloat16), "mp", split_axis=1, concat_axis=0, tiled=True
    )
    spread = spread.reshape(block_length, -1)
    picked = spread
    down_rows = scatter_rows(jnp.dot(picked, down_weight, preferred_element_type=jnp.float32))
    return (first_sum.astype(jnp.float32) + normalize(down_rows, output_gain)).astype(jnp.bfloat16)


def solution(mesh):
    placed = (
        P(("groups", "seq", "mp"), None),
        P(("groups", "seq")),
        P(("groups", "seq")),
        P(),
        P(),
        P(),
        P(),
        P(None, "mp"),
        P(None, "mp"),
        P(None, "mp"),
        P("mp", None),
        P(None, "mp"),
        P(None, "mp"),
        P("mp", None),
    )
    return jax.shard_map(
        body,
        mesh=mesh,
        in_specs=placed,
        out_specs=P(("groups", "seq", "mp"), None),
        check_vma=False,
    )
```
